32 devices in a mesh: ctx: 8 (over z, y), tp: 4 (over x, core).
Axes of the slice: x: 2, y: 2, z: 4, core: 2. Of those that a mesh axis runs over, the one named last changes fastest.
Arguments:
- qkv: bfloat16 [1024, 3, 8192], P(('ctx', 'tp')), may hold values from -6 to 6
- filters: float32 [3, 7, 8192], P(None, None, 'tp'), may hold values from -1.5 to 1.5
- doc_ids: int32 [8], replicated, may hold values from 0 to 1, never falling along the last dimension, each value on 1 to 5 neighbouring positions
- upstream: bfloat16 [1024, 8192], P('ctx', 'tp'), may hold values from -6 to 6
Outputs:
- attended: bfloat16 [1024, 8192], P('ctx', 'tp')
- qkv_grad: bfloat16 [1024, 3, 8192], P(('ctx', 'tp'))
- filter_grad: float32 [3, 7, 8192], P(None, None, 'tp')
The draws below stay inside these ranges and needn't reach their ends.
Inputs may be any that keep to these rules, and one draw needn't show every extreme that they name: doc_ids never falls along the sequence; every document covers 1 to 5 whole blocks of 128 tokens.
All inputs are finite; a program needn't handle non-finite values.
Results may differ from the reference program's by a relative error of at most 0.014.
The reference program's roundings to bfloat16 on the way count: a program that leaves them out, or rounds other values in their place, can miss the bound.
Values may be sent and summed in bfloat16 or wider, within the bound.
No kernel may reach another device: no remote copies, remote signals or barrier semaphores. Data moves between devices by JAX's collectives and lax.ppermute only.
A program may use at most 128 MiB of HBM per device.

```python
import math
import jax
import jax.numpy as jnp
import numpy as np
from jax import lax

HEADS = 64
HEAD_DIM = 128
D = 8192
KW = 7
BLOCK = 128
MOST_BLOCKS = 5
TOKENS = 1024
NB = 8
DOCS = 2


def draw_qkv(key, part):
    subkeys = jax.random.split(jax.random.fold_in(key, 11), 1)
    result = jax.random.truncated_normal(subkeys[0], -6.0, 6.0, (TOKENS, 3, D), jnp.float32)
    return result.astype(jnp.bfloat16)


def draw_filters(key, part):
    subkeys = jax.random.split(jax.random.fold_in(key, 23), 2)
    leading = jax.random.uniform(subkeys[0], (3, 1, D), jnp.float32, 0.5, 1.5)
    trailing = 0.35 * jax.random.truncated_normal(subkeys[1], -4.0, 4.0, (3, KW - 1, D), jnp.float32)
    return jnp.concatenate([leading, trailing], axis=1)


def block_levels(stream_key, extent, cuts, least, high):
    factor_of, own = 1.0, jax.random.fold_in(stream_key, 6)
    for dim, parts in cuts:
        steps = jnp.exp(jax.random.uniform(jax.random.fold_in(own, dim), (parts,), jnp.float32, least / len(cuts), high / len(cuts)))
        factor_of = factor_of * jnp.repeat(steps, extent[dim] // parts).reshape([-1 if axis == dim else 1 for axis in range(len(extent))])
    return factor_of


def length_profile(number_of, total, most, slope):
    loads = [(1 << 20) // math.isqrt(grade ** slope) + 1 for grade in range(2, number_of + 1)]
    rest, holding = total - most - (number_of - 1), [1] * (number_of - 1)
    while rest > 0:
        candidates = [i for i in range(number_of - 1) if holding[i] < most]
        whole, left = sum([loads[i] for i in candidates]), rest
        for i in candidates:
            extra = min(most - holding[i], max(1, left * loads[i] // whole), rest)
            holding[i] = holding[i] + extra
            rest = rest - extra
    return np.array([most] + holding)


def uneven_parts(own_key, number_of, total, reach, skew):
    if number_of == 2:
        one = jax.random.randint(own_key, (), max(1, total - reach), min(reach, total - 1) + 1)
        return jnp.stack([one, total - one])
    tallies = jnp.asarray(length_profile(number_of, total, reach, skew), jnp.int32)
    pairs = (number_of - 1) // 2
    source_of, taker = tallies[1:1 + 2 * pairs:2], tallies[2:2 + 2 * pairs:2]
    room = jnp.minimum(source_of - 1, reach - taker)
    moved = jax.random.randint(jax.random.fold_in(own_key, 1), (pairs,), 0, 1 << 20) % (room + 1)
    tallies = tallies.at[1:1 + 2 * pairs:2].set(source_of - moved).at[2:2 + 2 * pairs:2].set(taker + moved)
    return tallies[jax.random.permutation(jax.random.fold_in(own_key, 2), number_of)]


def noise(own_key, shape, scale, reach, shards=(), kind=jnp.bfloat16):
    loudness = block_levels(own_key, shape, shards, -0.22, 0.18) if shards else 1.0
    drawn = jax.random.normal(own_key, shape, jnp.float32) * scale * loudness
    return jnp.minimum(jnp.maximum(drawn, -reach), reach).astype(kind)


def setup_inputs(seed: int = 0) -> dict:
    keys = jax.random.split(jax.random.key(seed), 5)
    qkv = draw_qkv(jax.random.fold_in(keys[4], 71), 0)
    filters = draw_filters(jax.random.fold_in(keys[4], 71), 0)
    doc_ids = jnp.searchsorted(jnp.cumsum(uneven_parts(keys[2], DOCS, NB, MOST_BLOCKS, 2)), jnp.arange(NB), side="right").astype(jnp.int32)
    upstream = noise(keys[3], (TOKENS, D), 1.0, 6.0, ((0, 8), (1, 4)))
    return {"qkv": qkv, "filters": filters, "doc_ids": doc_ids, "upstream": upstream}


def causal_mix(signal, taps):
    length = signal.shape[0]
    padded = jnp.concatenate([jnp.zeros((KW - 1,) + signal.shape[1:], signal.dtype), signal], axis=0)
    total = jnp.zeros_like(signal)
    for lag in range(KW):
        total = total + taps[:, lag, :] * padded[KW - 1 - lag:KW - 1 - lag + length]
    return total


def fold_window(window):
    total = jnp.zeros((NB + MOST_BLOCKS - 1, BLOCK, HEAD_DIM), jnp.float32)
    for lag in range(MOST_BLOCKS):
        total = total.at[lag:lag + NB].add(window[:, lag])
    return total[MOST_BLOCKS - 1:].reshape(TOKENS, HEAD_DIM)


def head_pass(qkv_head, taps, grad_head, doc_ids):
    logit_scale = HEAD_DIM ** -0.5
    inputs = qkv_head.astype(jnp.float32)
    mixed = causal_mix(inputs, taps).astype(jnp.bfloat16)
    query_rows_local = mixed[:, 0].reshape(NB, BLOCK, HEAD_DIM).astype(jnp.float32)
    padding = jnp.zeros(((MOST_BLOCKS - 1) * BLOCK, HEAD_DIM), jnp.bfloat16)
    key_blocks = jnp.concatenate([padding, mixed[:, 1]], axis=0).reshape(NB + MOST_BLOCKS - 1, BLOCK, HEAD_DIM)
    value_blocks = jnp.concatenate([padding, mixed[:, 2]], axis=0).reshape(NB + MOST_BLOCKS - 1, BLOCK, HEAD_DIM)
    key_span_rows = jnp.stack([key_blocks[lag:lag + NB] for lag in range(MOST_BLOCKS)], axis=1).astype(jnp.float32)
    value_span_rows = jnp.stack([value_blocks[lag:lag + NB] for lag in range(MOST_BLOCKS)], axis=1).astype(jnp.float32)
    block_index = jnp.arange(NB)
    key_index = block_index[:, None] - (MOST_BLOCKS - 1) + jnp.arange(MOST_BLOCKS)[None, :]
    doc_padded = jnp.concatenate([jnp.full((MOST_BLOCKS - 1,), -1, jnp.int32), doc_ids.astype(jnp.int32)])
    key_docs = jnp.stack([doc_padded[lag:lag + NB] for lag in range(MOST_BLOCKS)], axis=1)
    block_ok = (key_index >= 0) & (key_docs == doc_ids.astype(jnp.int32)[:, None])
    within = jnp.arange(BLOCK)
    causal = within[:, None] >= within[None, :]
    is_last = jnp.arange(MOST_BLOCKS) == MOST_BLOCKS - 1
    allowed = block_ok[:, None, :, None] & (jnp.logical_not(is_last)[None, None, :, None] | causal[None, :, None, :])
    attention_logits = jnp.einsum('mep,muzp->meuz', query_rows_local, key_span_rows) * logit_scale
    masked = jnp.where(allowed, attention_logits, -1e30)
    row_max = jnp.max(masked, axis=(2, 3), keepdims=True)
    expo = jnp.where(allowed, jnp.exp(masked - row_max), 0.0)
    row_sum = jnp.sum(expo, axis=(2, 3), keepdims=True)
    attention_probabilities = expo.astype(jnp.bfloat16).astype(jnp.float32)
    weighted_values = jnp.einsum('uoyv,uyvi->uoi', attention_probabilities, value_span_rows)
    attended = (weighted_values / row_sum[:, :, 0]).astype(jnp.bfloat16)
    upstream = grad_head.reshape(NB, BLOCK, HEAD_DIM).astype(jnp.float32)
    delta = jnp.sum(upstream * attended.astype(jnp.float32), axis=-1)
    prob = expo / row_sum
    probability_reduced = prob.astype(jnp.bfloat16).astype(jnp.float32)
    value_gradient_rows = jnp.einsum('wlfh,wli->wfhi', probability_reduced, upstream)
    probability_gradient = jnp.einsum('mep,muzp->meuz', upstream, value_span_rows)
    score_gradient = (prob * (probability_gradient - delta[:, :, None, None]) * logit_scale).astype(jnp.bfloat16).astype(jnp.float32)
    query_gradient_rows = jnp.einsum('uoyv,uyvi->uoi', score_gradient, key_span_rows)
    key_gradient_rows = jnp.einsum('wlfh,wli->wfhi', score_gradient, query_rows_local)
    conv_grad = jnp.stack([query_gradient_rows.reshape(TOKENS, HEAD_DIM), fold_window(key_gradient_rows), fold_window(value_gradient_rows)], axis=1)
    extended = jnp.concatenate([conv_grad, jnp.zeros((KW - 1, 3, HEAD_DIM), jnp.float32)], axis=0)
    input_grad = jnp.zeros_like(conv_grad)
    for lag in range(KW):
        input_grad = input_grad + taps[:, lag, :] * extended[lag:lag + TOKENS]
    shifted = jnp.concatenate([jnp.zeros((KW - 1, 3, HEAD_DIM), jnp.float32), inputs], axis=0)
    tap_grad = jnp.stack([jnp.sum(shifted[KW - 1 - lag:KW - 1 - lag + TOKENS] * conv_grad, axis=0) for lag in range(KW)], axis=1)
    return attended.reshape(TOKENS, HEAD_DIM), input_grad.astype(jnp.bfloat16), tap_grad


def reference(qkv, filters, doc_ids, upstream):
    head_inputs = qkv.reshape(TOKENS, 3, HEADS, HEAD_DIM).transpose(2, 0, 1, 3)
    head_taps = filters.reshape(3, KW, HEADS, HEAD_DIM).transpose(2, 0, 1, 3)
    head_grads = upstream.reshape(TOKENS, HEADS, HEAD_DIM).transpose(1, 0, 2)
    outputs, input_grads, tap_grads = lax.map(lambda packed: head_pass(packed[0], packed[1], packed[2], doc_ids), (head_inputs, head_taps, head_grads))
    attended = outputs.transpose(1, 0, 2).reshape(TOKENS, D)
    qkv_grad = input_grads.transpose(1, 2, 0, 3).reshape(TOKENS, 3, D)
    filter_grad = tap_grads.transpose(1, 2, 0, 3).reshape(3, KW, D)
    return attended, qkv_grad, filter_grad
```

```python
import jax
import jax.numpy as jnp
from jax import lax
from jax.experimental import pallas as pl
from jax.experimental.pallas import tpu as pltpu
from jax.sharding import PartitionSpec as P

HEAD_DIM = 128
KW = 7
BLOCK = 128
STEPS = 4
PAD = 8
SCALE = HEAD_DIM ** (-0.5)
AXES = ("ctx", "tp")


def dot(a, b, dims):
    return lax.dot_general(a, b, (dims, ((), ())), preferred_element_type=jnp.float32)


def estimate(flops, moved):
    return pl.CostEstimate(flops=flops, bytes_accessed=moved, transcendentals=0)


def pack_qkv(x, members):
    streams, rows, channels = x.shape
    tp = lax.axis_size("tp")
    width = channels // tp
    per = width // HEAD_DIM // members

    def kernel(x_ref, o_ref):
        for c in range(members):
            for j in range(per):
                at = (c * per + j) * HEAD_DIM
                o_ref[c, 0, j] = x_ref[:, :, at : at + HEAD_DIM]

    return pl.pallas_call(
        kernel,
        grid=(tp,),
        in_specs=[pl.BlockSpec((streams, rows, width), lambda t: (0, 0, t))],
        out_specs=pl.BlockSpec(
            (members, 1, per, streams, rows, HEAD_DIM), lambda t: (0, t, 0, 0, 0, 0)
        ),
        out_shape=jax.ShapeDtypeStruct((members, tp, per, streams, rows, HEAD_DIM), x.dtype),
        cost_estimate=estimate(0, 4 * x.size),
        name="pack_qkv",
    )(x)


def unpack_qkv(x, members):
    _, tp, per, streams, rows, _ = x.shape
    width = members * per * HEAD_DIM

    def kernel(x_ref, o_ref):
        for c in range(members):
            for j in range(per):
                at = (c * per + j) * HEAD_DIM
                o_ref[:, :, at : at + HEAD_DIM] = x_ref[c, 0, j]

    return pl.pallas_call(
        kernel,
        grid=(tp,),
        in_specs=[
            pl.BlockSpec((members, 1, per, streams, rows, HEAD_DIM), lambda t: (0, t, 0, 0, 0, 0))
        ],
        out_specs=pl.BlockSpec((streams, rows, width), lambda t: (0, 0, t)),
        out_shape=jax.ShapeDtypeStruct((streams, rows, tp * width), x.dtype),
        cost_estimate=estimate(0, 4 * x.size),
        name="unpack_qkv",
    )(x)


def pack_rows(x, members):
    tokens, width = x.shape
    per = width // HEAD_DIM // members

    def kernel(x_ref, o_ref):
        for c in range(members):
            for j in range(per):
                at = (c * per + j) * HEAD_DIM
                o_ref[c, j] = x_ref[:, at : at + HEAD_DIM]

    return pl.pallas_call(
        kernel,
        out_shape=jax.ShapeDtypeStruct((members, per, tokens, HEAD_DIM), x.dtype),
        cost_estimate=estimate(0, 4 * x.size),
        name="pack_rows",
    )(x)


def unpack_rows(x):
    members, per, tokens, _ = x.shape

    def kernel(x_ref, o_ref):
        for c in range(members):
            for j in range(per):
                at = (c * per + j) * HEAD_DIM
                o_ref[:, at : at + HEAD_DIM] = x_ref[c, j]

    return pl.pallas_call(
        kernel,
        out_shape=jax.ShapeDtypeStruct((tokens, members * per * HEAD_DIM), x.dtype),
        cost_estimate=estimate(0, 4 * x.size),
        name="unpack_rows",
    )(x)


def masked_scores(docs, query, keys, block, first):
    raw = dot(query, keys, ((1,), (1,))) * SCALE
    rows = lax.broadcasted_iota(jnp.int32, (BLOCK, BLOCK), 0)
    cols = lax.broadcasted_iota(jnp.int32, (BLOCK, BLOCK), 1)
    tiles = []
    for other in range(first, block + 1):
        tile = raw[:, (other - first) * BLOCK : (other - first + 1) * BLOCK]
        if other == block:
            tile = jnp.where(cols <= rows, tile, -1e30)
        else:
            tile = jnp.where(docs[other] == docs[block], tile, -1e30)
        tiles.append(tile)
    masked = jnp.concatenate(tiles, axis=1) if len(tiles) > 1 else tiles[0]
    row_max = jnp.max(masked, axis=1, keepdims=True)
    expo = jnp.exp(masked - row_max)
    return expo, jnp.sum(expo, axis=1, keepdims=True)


def forward_kernel(docs, x_ref, taps_ref, mixed_ref, out_ref, padded):
    sources, _, streams, rows, _ = x_ref.shape
    tokens = sources * rows
    padded[:, 0:PAD, :] = jnp.zeros((streams, PAD, HEAD_DIM), jnp.float32)
    for m in range(streams):
        padded[m, PAD:, :] = x_ref[:, 0, m].reshape(tokens, HEAD_DIM).astype(jnp.float32)
    for m in range(streams):
        for start in range(0, tokens, BLOCK):
            total = jnp.zeros((BLOCK, HEAD_DIM), jnp.float32)
            for lag in range(KW):
                at = PAD + start - lag
                total = total + taps_ref[m, lag : lag + 1, :] * padded[m, at : at + BLOCK, :]
            mixed_ref[0, m, start : start + BLOCK, :] = total.astype(jnp.bfloat16)
    for block in range(tokens // BLOCK):
        first = max(0, block - STEPS)
        own = slice(block * BLOCK, (block + 1) * BLOCK)
        span = slice(first * BLOCK, (block + 1) * BLOCK)
        expo, row_sum = masked_scores(
            docs, mixed_ref[0, 0, own, :], mixed_ref[0, 1, span, :], block, first
        )
        total = dot(expo.astype(jnp.bfloat16), mixed_ref[0, 2, span, :], ((1,), (0,)))
        per = out_ref.shape[2]
        at = block * BLOCK
        out_ref[at // per, 0, at % per : at % per + BLOCK, :] = (total / row_sum).astype(
            jnp.bfloat16
        )


def forward(docs, x, taps, members):
    sources, per, streams, rows, _ = x.shape
    tokens = sources * rows
    return pl.pallas_call(
        forward_kernel,
        grid_spec=pltpu.PrefetchScalarGridSpec(
            num_scalar_prefetch=1,
            grid=(per,),
            in_specs=[
                pl.BlockSpec((sources, 1, streams, rows, HEAD_DIM), lambda h, d: (0, h, 0, 0, 0)),
                pl.BlockSpec((streams, KW, HEAD_DIM), lambda h, d: (0, 0, h)),
            ],
            out_specs=[
                pl.BlockSpec((1, streams, tokens, HEAD_DIM), lambda h, d: (h, 0, 0, 0)),
                pl.BlockSpec((members, 1, tokens // members, HEAD_DIM), lambda h, d: (0, h, 0, 0)),
            ],
            scratch_shapes=[pltpu.VMEM((streams, tokens + PAD, HEAD_DIM), jnp.float32)],
        ),
        out_shape=[
            jax.ShapeDtypeStruct((per, streams, tokens, HEAD_DIM), jnp.bfloat16),
            jax.ShapeDtypeStruct((members, per, tokens // members, HEAD_DIM), jnp.bfloat16),
        ],
        cost_estimate=estimate(10_000_000_000, 8 * x.size),
        name="forward",
    )(docs, x, taps)


def backward_kernel(
    docs, x_ref, taps_ref, mixed_ref, att_ref, up_ref, grad_ref, tapg_ref, padded, cgrad
):
    sources, _, streams, rows, _ = x_ref.shape
    tokens = sources * rows
    per = att_ref.shape[2]
    cgrad[...] = jnp.zeros_like(cgrad)
    for block in range(tokens // BLOCK):
        first = max(0, block - STEPS)
        own = slice(block * BLOCK, (block + 1) * BLOCK)
        span = slice(first * BLOCK, (block + 1) * BLOCK)
        query, keys, values = (
            mixed_ref[0, 0, own, :],
            mixed_ref[0, 1, span, :],
            mixed_ref[0, 2, span, :],
        )
        at = block * BLOCK
        up = up_ref[at // per, 0, at % per : at % per + BLOCK, :]
        att = att_ref[at // per, 0, at % per : at % per + BLOCK, :]
        delta = jnp.sum(up.astype(jnp.float32) * att.astype(jnp.float32), axis=1, keepdims=True)
        expo, row_sum = masked_scores(docs, query, keys, block, first)
        prob = expo / row_sum
        dprob = dot(up, values, ((1,), (1,)))
        dscore = (prob * (dprob - delta) * SCALE).astype(jnp.bfloat16)
        cgrad[0, own, :] = dot(dscore, keys, ((1,), (0,)))
        cgrad[1, span, :] += dot(dscore, query, ((0,), (0,)))
        cgrad[2, span, :] += dot(prob.astype(jnp.bfloat16), up, ((0,), (0,)))
    padded[:, 0:PAD, :] = jnp.zeros((streams, PAD, HEAD_DIM), jnp.float32)
    for m in range(streams):
        padded[m, PAD:, :] = x_ref[:, 0, m].reshape(tokens, HEAD_DIM).astype(jnp.float32)
    for m in range(streams):
        sums = [jnp.zeros((8, HEAD_DIM), jnp.float32) for _ in range(KW)]
        for start in range(0, tokens, BLOCK):
            total = jnp.zeros((BLOCK, HEAD_DIM), jnp.float32)
            here = cgrad[m, start : start + BLOCK, :]
            for lag in range(KW):
                total = (
                    total
                    + taps_ref[m, lag : lag + 1, :]
                    * cgrad[m, start + lag : start + lag + BLOCK, :]
                )
                at = PAD + start - lag
                product = padded[m, at : at + BLOCK, :] * here
                sums[lag] = sums[lag] + jnp.sum(product.reshape(BLOCK // 8, 8, HEAD_DIM), axis=0)
            grad_ref[start // rows : (start + BLOCK) // rows, 0, m] = total.astype(
                jnp.bfloat16
            ).reshape(BLOCK // rows, rows, HEAD_DIM)
        for lag in range(KW):
            tapg_ref[m, lag : lag + 1, :] = jnp.sum(sums[lag], axis=0, keepdims=True)


def backward(docs, x, taps, mixed, att, up):
    sources, per, streams, rows, _ = x.shape
    tokens = sources * rows
    members = att.shape[0]
    slab = pl.BlockSpec((sources, 1, streams, rows, HEAD_DIM), lambda h, d: (0, h, 0, 0, 0))
    tap = pl.BlockSpec((streams, KW, HEAD_DIM), lambda h, d: (0, 0, h))
    rowspec = pl.BlockSpec((members, 1, tokens // members, HEAD_DIM), lambda h, d: (0, h, 0, 0))
    return pl.pallas_call(
        backward_kernel,
        grid_spec=pltpu.PrefetchScalarGridSpec(
            num_scalar_prefetch=1,
            grid=(per,),
            in_specs=[
                slab,
                tap,
                pl.BlockSpec((1, streams, tokens, HEAD_DIM), lambda h, d: (h, 0, 0, 0)),
                rowspec,
                rowspec,
            ],
            out_specs=[slab, tap],
            scratch_shapes=[
                pltpu.VMEM((streams, tokens + PAD, HEAD_DIM), jnp.float32),
                pltpu.VMEM((streams, tokens + PAD, HEAD_DIM), jnp.float32),
            ],
        ),
        out_shape=[
            jax.ShapeDtypeStruct(x.shape, jnp.bfloat16),
            jax.ShapeDtypeStruct(taps.shape, jnp.float32),
        ],
        cost_estimate=estimate(20_000_000_000, 12 * x.size),
        name="backward",
    )(docs, x, taps, mixed, att, up)


def swap(value, axes):
    shape = value.shape
    return lax.all_to_all(
        value.reshape(shape[0], -1, HEAD_DIM), axes, split_axis=0, concat_axis=0, tiled=True
    ).reshape(shape)


def by_heads(qkv, filters, doc_ids, upstream):
    members, tp = lax.axis_size("ctx"), lax.axis_size("tp")
    rows, streams, _ = qkv.shape
    per = upstream.shape[1] // HEAD_DIM // members
    position = lax.axis_index("ctx")
    packed = pack_qkv(jnp.transpose(qkv, (1, 0, 2)), members)
    x = swap(packed.reshape((members * tp,) + packed.shape[2:]), AXES)
    up = swap(pack_rows(upstream, members), "ctx")
    taps = lax.dynamic_slice_in_dim(filters, position * per * HEAD_DIM, per * HEAD_DIM, 2)
    mixed, att = forward(doc_ids, x, taps, members)
    attended = unpack_rows(swap(att, "ctx"))
    grad, tap_grad = backward(doc_ids, x, taps, mixed, att, up)
    grad = swap(grad, AXES)
    qkv_grad = unpack_qkv(grad.reshape((members, tp) + grad.shape[1:]), members)
    pieces = lax.all_gather(tap_grad, "ctx", axis=0)
    filter_grad = jnp.transpose(pieces, (1, 2, 0, 3)).reshape(filters.shape)
    return attended, jnp.transpose(qkv_grad, (1, 0, 2)), filter_grad


def from_behind(value, axis, steps):
    count = lax.axis_size(axis)
    first, last = (max(0, -steps), min(count, count - steps))
    return lax.ppermute(value, axis, [(source, source + steps) for source in range(first, last)])


def block_docs(doc_ids, first_block, count):
    start = jnp.maximum(first_block, 0)
    picked = lax.dynamic_slice_in_dim(doc_ids, start, count)
    return jnp.repeat(picked, BLOCK)


def by_ring(qkv, filters, doc_ids, upstream):
    local = lax.all_to_all(qkv, "tp", split_axis=2, concat_axis=0, tiled=True)
    tokens = local.shape[0]
    width = local.shape[2]
    heads = width // HEAD_DIM
    blocks_here = tokens // BLOCK
    logit_scale = HEAD_DIM ** (-0.5)
    position = lax.axis_index("ctx")
    reach = STEPS + 1
    rim = from_behind(local[tokens - (KW - 1) :], "ctx", 1)
    inputs = jnp.concatenate([rim, local], axis=0).astype(jnp.float32)
    mixed = sum(
        (filters[:, lag, :] * inputs[KW - 1 - lag : KW - 1 - lag + tokens] for lag in range(KW))
    )
    mixed = mixed.astype(jnp.bfloat16)
    queries = mixed[:, 0].reshape(tokens, heads, HEAD_DIM)
    key_value = mixed[:, 1:3]
    tiles = [key_value]
    current = key_value
    for distance in range(1, STEPS + 1):
        current = from_behind(current, "ctx", 1)
        tiles.append(current)
    joined = jnp.concatenate(tiles, axis=0)
    keys = joined[:, 0].reshape(reach * tokens, heads, HEAD_DIM)
    values = joined[:, 1].reshape(reach * tokens, heads, HEAD_DIM)
    rows = jnp.arange(tokens)
    query_token = position * tokens + rows
    query_doc = block_docs(doc_ids, position * blocks_here, blocks_here)
    key_tokens = jnp.concatenate(
        [(position - distance) * tokens + rows for distance in range(reach)]
    )
    key_docs = jnp.concatenate(
        [
            block_docs(doc_ids, (position - distance) * blocks_here, blocks_here)
            for distance in range(reach)
        ]
    )
    allowed = (
        (key_tokens[None, :] >= 0)
        & (key_tokens[None, :] <= query_token[:, None])
        & (key_docs[None, :] == query_doc[:, None])
    )
    raw = (
        jnp.einsum("qhd,khd->hqk", queries, keys, preferred_element_type=jnp.float32) * logit_scale
    )
    masked = jnp.where(allowed[None], raw, -1e30)
    row_max = masked.max(axis=2)
    expo = jnp.where(allowed[None], jnp.exp(masked - row_max[:, :, None]), 0.0)
    row_sum = expo.sum(axis=2)
    weighted_values = jnp.einsum(
        "hqk,khd->qhd", expo.astype(jnp.bfloat16), values, preferred_element_type=jnp.float32
    )
    attended = (weighted_values / row_sum.T[:, :, None]).astype(jnp.bfloat16)
    grad_out = upstream.reshape(tokens, heads, HEAD_DIM)
    delta = jnp.sum(grad_out.astype(jnp.float32) * attended.astype(jnp.float32), axis=-1).T
    prob = expo / row_sum[:, :, None]
    value_part = jnp.einsum(
        "hqk,qhd->khd", prob.astype(jnp.bfloat16), grad_out, preferred_element_type=jnp.float32
    )
    probability_gradient = jnp.einsum(
        "qhd,khd->hqk", grad_out, values, preferred_element_type=jnp.float32
    )
    score_gradient = (prob * (probability_gradient - delta[:, :, None]) * logit_scale).astype(
        jnp.bfloat16
    )
    query_gradient_rows = jnp.einsum(
        "hqk,khd->qhd", score_gradient, keys, preferred_element_type=jnp.float32
    )
    key_part = jnp.einsum(
        "hqk,qhd->khd", score_gradient, queries, preferred_element_type=jnp.float32
    )
    stacked = jnp.stack(
        [key_part.reshape(reach, tokens, width), value_part.reshape(reach, tokens, width)], axis=2
    )
    partials = [stacked[distance] for distance in range(reach)]
    carried = partials[STEPS]
    for distance in range(STEPS - 1, -1, -1):
        carried = from_behind(carried, "ctx", -1)
        carried = carried + partials[distance]
    conv_grad = jnp.concatenate([query_gradient_rows.reshape(tokens, 1, width), carried], axis=1)
    grad_edge = from_behind(conv_grad[: KW - 1], "ctx", -1)
    extended = jnp.concatenate([conv_grad, grad_edge], axis=0)
    input_grad = sum((filters[:, lag, :] * extended[lag : lag + tokens] for lag in range(KW)))
    tap_terms = jnp.stack(
        [
            jnp.sum(inputs[KW - 1 - lag : KW - 1 - lag + tokens] * conv_grad, axis=0)
            for lag in range(KW)
        ],
        axis=1,
    )
    filter_grad = lax.psum(tap_terms, "ctx")
    qkv_grad = lax.all_to_all(
        input_grad.astype(jnp.bfloat16), "tp", split_axis=0, concat_axis=2, tiled=True
    )
    return (attended.reshape(tokens, width), qkv_grad, filter_grad)


def solution(mesh):
    def shards(qkv, filters, doc_ids, upstream):
        heads = upstream.shape[1] // HEAD_DIM
        tokens = upstream.shape[0]
        whole = heads % mesh.shape["ctx"] == 0 and tokens % BLOCK == 0
        form = by_heads if whole else by_ring
        return form(qkv, filters, doc_ids, upstream)

    return jax.shard_map(
        shards,
        mesh=mesh,
        in_specs=(P(("ctx", "tp"), None, None), P(None, None, "tp"), P(), P("ctx", "tp")),
        out_specs=(P("ctx", "tp"), P(("ctx", "tp"), None, None), P(None, None, "tp")),
        check_vma=False,
    )
```

```python
import jax
import jax.numpy as jnp
from jax import lax
from jax.experimental import pallas as pl
from jax.experimental.pallas import tpu as pltpu
from jax.sharding import PartitionSpec as P

HEAD_DIM = 128
KW = 7
BLOCK = 128
STEPS = 4
PAD = 8
SCALE = HEAD_DIM ** (-0.5)
AXES = ("ctx", "tp")


def dot(a, b, dims):
    return lax.dot_general(a, b, (dims, ((), ())), preferred_element_type=jnp.float32)


def estimate(flops, moved):
    return pl.CostEstimate(flops=flops, bytes_accessed=moved, transcendentals=0)


def split_columns(x, members, place):
    *outer, channels = x.shape
    width = channels // members

    def kernel(x_ref, o_ref, sems):
        copies = []
        for d in range(members):
            at = [slice(None)] * len(outer) + [pl.ds(place(d) * width, width)]
            copies.append(pltpu.make_async_copy(x_ref.at[tuple(at)], o_ref.at[d], sems.at[d]))
        for copy in copies:
            copy.start()
        for copy in copies:
            copy.wait()

    return pl.pallas_call(
        kernel,
        in_specs=[pl.BlockSpec(memory_space=pl.ANY)],
        out_specs=pl.BlockSpec(memory_space=pl.ANY),
        out_shape=jax.ShapeDtypeStruct((members, *outer, width), x.dtype),
        scratch_shapes=[pltpu.SemaphoreType.DMA((members,))],
        cost_estimate=estimate(0, 4 * x.size),
        name="split_columns",
    )(x)


def join_columns(x, place):
    members, *outer, width = x.shape

    def kernel(x_ref, o_ref, sems):
        copies = []
        for d in range(members):
            at = [slice(None)] * len(outer) + [pl.ds(place(d) * width, width)]
            copies.append(pltpu.make_async_copy(x_ref.at[d], o_ref.at[tuple(at)], sems.at[d]))
        for copy in copies:
            copy.start()
        for copy in copies:
            copy.wait()

    return pl.pallas_call(
        kernel,
        in_specs=[pl.BlockSpec(memory_space=pl.ANY)],
        out_specs=pl.BlockSpec(memory_space=pl.ANY),
        out_shape=jax.ShapeDtypeStruct((*outer, members * width), x.dtype),
        scratch_shapes=[pltpu.SemaphoreType.DMA((members,))],
        cost_estimate=estimate(0, 4 * x.size),
        name="join_columns",
    )(x)


def masked_scores(docs, query, keys, block, first):
    raw = dot(query, keys, ((1,), (1,))) * SCALE
    rows = lax.broadcasted_iota(jnp.int32, (BLOCK, BLOCK), 0)
    cols = lax.broadcasted_iota(jnp.int32, (BLOCK, BLOCK), 1)
    tiles = []
    for other in range(first, block + 1):
        tile = raw[:, (other - first) * BLOCK : (other - first + 1) * BLOCK]
        if other == block:
            tile = jnp.where(cols <= rows, tile, -1e30)
        else:
            tile = jnp.where(docs[other] == docs[block], tile, -1e30)
        tiles.append(tile)
    masked = jnp.concatenate(tiles, axis=1) if len(tiles) > 1 else tiles[0]
    row_max = jnp.max(masked, axis=1, keepdims=True)
    expo = jnp.exp(masked - row_max)
    return expo, jnp.sum(expo, axis=1, keepdims=True)


def forward_kernel(docs, x_ref, taps_ref, mixed_ref, out_ref, padded):
    sources, streams, rows, _ = x_ref.shape
    tokens = sources * rows
    padded[:, 0:PAD, :] = jnp.zeros((streams, PAD, HEAD_DIM), jnp.float32)
    for m in range(streams):
        padded[m, PAD:, :] = x_ref[:, m].reshape(tokens, HEAD_DIM).astype(jnp.float32)
    for m in range(streams):
        for start in range(0, tokens, BLOCK):
            total = jnp.zeros((BLOCK, HEAD_DIM), jnp.float32)
            for lag in range(KW):
                at = PAD + start - lag
                total = total + taps_ref[m, lag : lag + 1, :] * padded[m, at : at + BLOCK, :]
            mixed_ref[0, m, start : start + BLOCK, :] = total.astype(jnp.bfloat16)
    for block in range(tokens // BLOCK):
        first = max(0, block - STEPS)
        own = slice(block * BLOCK, (block + 1) * BLOCK)
        span = slice(first * BLOCK, (block + 1) * BLOCK)
        expo, row_sum = masked_scores(
            docs, mixed_ref[0, 0, own, :], mixed_ref[0, 1, span, :], block, first
        )
        total = dot(expo.astype(jnp.bfloat16), mixed_ref[0, 2, span, :], ((1,), (0,)))
        per = out_ref.shape[1]
        at = block * BLOCK
        out_ref[at // per, at % per : at % per + BLOCK, :] = (total / row_sum).astype(
            jnp.bfloat16
        )


def forward(docs, x, taps, members):
    sources, streams, rows, width = x.shape
    per = width // HEAD_DIM
    tokens = sources * rows
    return pl.pallas_call(
        forward_kernel,
        grid_spec=pltpu.PrefetchScalarGridSpec(
            num_scalar_prefetch=1,
            grid=(per,),
            in_specs=[
                pl.BlockSpec((sources, streams, rows, HEAD_DIM), lambda h, d: (0, 0, 0, h)),
                pl.BlockSpec((streams, KW, HEAD_DIM), lambda h, d: (0, 0, h)),
            ],
            out_specs=[
                pl.BlockSpec((1, streams, tokens, HEAD_DIM), lambda h, d: (h, 0, 0, 0)),
                pl.BlockSpec((members, tokens // members, HEAD_DIM), lambda h, d: (0, 0, h)),
            ],
            scratch_shapes=[pltpu.VMEM((streams, tokens + PAD, HEAD_DIM), jnp.float32)],
        ),
        out_shape=[
            jax.ShapeDtypeStruct((per, streams, tokens, HEAD_DIM), jnp.bfloat16),
            jax.ShapeDtypeStruct((members, tokens // members, width), jnp.bfloat16),
        ],
        cost_estimate=estimate(10_000_000_000, 8 * x.size),
        name="forward",
    )(docs, x, taps)


def backward_kernel(
    docs, x_ref, taps_ref, mixed_ref, att_ref, up_ref, grad_ref, tapg_ref, padded, cgrad
):
    sources, streams, rows, _ = x_ref.shape
    tokens = sources * rows
    per = att_ref.shape[1]
    cgrad[...] = jnp.zeros_like(cgrad)
    for block in range(tokens // BLOCK):
        first = max(0, block - STEPS)
        own = slice(block * BLOCK, (block + 1) * BLOCK)
        span = slice(first * BLOCK, (block + 1) * BLOCK)
        query, keys, values = (
            mixed_ref[0, 0, own, :],
            mixed_ref[0, 1, span, :],
            mixed_ref[0, 2, span, :],
        )
        at = block * BLOCK
        up = up_ref[at // per, at % per : at % per + BLOCK, :]
        att = att_ref[at // per, at % per : at % per + BLOCK, :]
        delta = jnp.sum(up.astype(jnp.float32) * att.astype(jnp.float32), axis=1, keepdims=True)
        expo, row_sum = masked_scores(docs, query, keys, block, first)
        prob = expo / row_sum
        dprob = dot(up, values, ((1,), (1,)))
        dscore = (prob * (dprob - delta) * SCALE).astype(jnp.bfloat16)
        cgrad[0, own, :] = dot(dscore, keys, ((1,), (0,)))
        cgrad[1, span, :] += dot(dscore, query, ((0,), (0,)))
        cgrad[2, span, :] += dot(prob.astype(jnp.bfloat16), up, ((0,), (0,)))
    padded[:, 0:PAD, :] = jnp.zeros((streams, PAD, HEAD_DIM), jnp.float32)
    for m in range(streams):
        padded[m, PAD:, :] = x_ref[:, m].reshape(tokens, HEAD_DIM).astype(jnp.float32)
    for m in range(streams):
        sums = [jnp.zeros((8, HEAD_DIM), jnp.float32) for _ in range(KW)]
        for start in range(0, tokens, BLOCK):
            total = jnp.zeros((BLOCK, HEAD_DIM), jnp.float32)
            here = cgrad[m, start : start + BLOCK, :]
            for lag in range(KW):
                total = (
                    total
                    + taps_ref[m, lag : lag + 1, :]
                    * cgrad[m, start + lag : start + lag + BLOCK, :]
                )
                at = PAD + start - lag
                product = padded[m, at : at + BLOCK, :] * here
                sums[lag] = sums[lag] + jnp.sum(product.reshape(BLOCK // 8, 8, HEAD_DIM), axis=0)
            grad_ref[start // rows : (start + BLOCK) // rows, m] = total.astype(
                jnp.bfloat16
            ).reshape(BLOCK // rows, rows, HEAD_DIM)
        for lag in range(KW):
            tapg_ref[m, lag : lag + 1, :] = jnp.sum(sums[lag], axis=0, keepdims=True)


def backward(docs, x, taps, mixed, att, up):
    sources, streams, rows, width = x.shape
    per = width // HEAD_DIM
    tokens = sources * rows
    members = att.shape[0]
    slab = pl.BlockSpec((sources, streams, rows, HEAD_DIM), lambda h, d: (0, 0, 0, h))
    tap = pl.BlockSpec((streams, KW, HEAD_DIM), lambda h, d: (0, 0, h))
    rowspec = pl.BlockSpec((members, tokens // members, HEAD_DIM), lambda h, d: (0, 0, h))
    return pl.pallas_call(
        backward_kernel,
        grid_spec=pltpu.PrefetchScalarGridSpec(
            num_scalar_prefetch=1,
            grid=(per,),
            in_specs=[
                slab,
                tap,
                pl.BlockSpec((1, streams, tokens, HEAD_DIM), lambda h, d: (h, 0, 0, 0)),
                rowspec,
                rowspec,
            ],
            out_specs=[slab, tap],
            scratch_shapes=[
                pltpu.VMEM((streams, tokens + PAD, HEAD_DIM), jnp.float32),
                pltpu.VMEM((streams, tokens + PAD, HEAD_DIM), jnp.float32),
            ],
        ),
        out_shape=[
            jax.ShapeDtypeStruct(x.shape, jnp.bfloat16),
            jax.ShapeDtypeStruct(taps.shape, jnp.float32),
        ],
        cost_estimate=estimate(20_000_000_000, 12 * x.size),
        name="backward",
    )(docs, x, taps, mixed, att, up)


def swap(value, axes):
    shape = value.shape
    return lax.all_to_all(
        value.reshape(shape[0], -1, shape[-1]), axes, split_axis=0, concat_axis=0, tiled=True
    ).reshape(shape)


def gather_columns(piece):
    count = lax.axis_size("ctx")
    position = lax.axis_index("ctx")
    held, step = piece, 1
    while step < count:
        other = lax.ppermute(held, "ctx", [(i, i ^ step) for i in range(count)])
        low = (position & step) == 0
        held = jnp.concatenate(
            [jnp.where(low, held, other), jnp.where(low, other, held)], axis=-1
        )
        step *= 2
    return held


def by_heads(qkv, filters, doc_ids, upstream):
    members, tp = lax.axis_size("ctx"), lax.axis_size("tp")
    width = upstream.shape[1] // members
    position = lax.axis_index("ctx")

    def column_of(d):
        return d % tp * members + d // tp

    def same(d):
        return d

    x = swap(split_columns(jnp.transpose(qkv, (1, 0, 2)), members * tp, column_of), AXES)
    up = swap(split_columns(upstream, members, same), "ctx")
    taps = lax.dynamic_slice_in_dim(filters, position * width, width, 2)
    mixed, att = forward(doc_ids, x, taps, members)
    attended = join_columns(swap(att, "ctx"), same)
    grad, tap_grad = backward(doc_ids, x, taps, mixed, att, up)
    qkv_grad = join_columns(swap(grad, AXES), column_of)
    return attended, jnp.transpose(qkv_grad, (1, 0, 2)), gather_columns(tap_grad)


def from_behind(value, axis, steps):
    count = lax.axis_size(axis)
    first, last = (max(0, -steps), min(count, count - steps))
    return lax.ppermute(value, axis, [(source, source + steps) for source in range(first, last)])


def block_docs(doc_ids, first_block, count):
    start = jnp.maximum(first_block, 0)
    picked = lax.dynamic_slice_in_dim(doc_ids, start, count)
    return jnp.repeat(picked, BLOCK)


def by_ring(qkv, filters, doc_ids, upstream):
    local = lax.all_to_all(qkv, "tp", split_axis=2, concat_axis=0, tiled=True)
    tokens = local.shape[0]
    width = local.shape[2]
    heads = width // HEAD_DIM
    blocks_here = tokens // BLOCK
    logit_scale = HEAD_DIM ** (-0.5)
    position = lax.axis_index("ctx")
    reach = STEPS + 1
    rim = from_behind(local[tokens - (KW - 1) :], "ctx", 1)
    inputs = jnp.concatenate([rim, local], axis=0).astype(jnp.float32)
    mixed = sum(
        (filters[:, lag, :] * inputs[KW - 1 - lag : KW - 1 - lag + tokens] for lag in range(KW))
    )
    mixed = mixed.astype(jnp.bfloat16)
    queries = mixed[:, 0].reshape(tokens, heads, HEAD_DIM)
    key_value = mixed[:, 1:3]
    tiles = [key_value]
    current = key_value
    for distance in range(1, STEPS + 1):
        current = from_behind(current, "ctx", 1)
        tiles.append(current)
    joined = jnp.concatenate(tiles, axis=0)
    keys = joined[:, 0].reshape(reach * tokens, heads, HEAD_DIM)
    values = joined[:, 1].reshape(reach * tokens, heads, HEAD_DIM)
    rows = jnp.arange(tokens)
    query_token = position * tokens + rows
    query_doc = block_docs(doc_ids, position * blocks_here, blocks_here)
    key_tokens = jnp.concatenate(
        [(position - distance) * tokens + rows for distance in range(reach)]
    )
    key_docs = jnp.concatenate(
        [
            block_docs(doc_ids, (position - distance) * blocks_here, blocks_here)
            for distance in range(reach)
        ]
    )
    allowed = (
        (key_tokens[None, :] >= 0)
        & (key_tokens[None, :] <= query_token[:, None])
        & (key_docs[None, :] == query_doc[:, None])
    )
    raw = (
        jnp.einsum("qhd,khd->hqk", queries, keys, preferred_element_type=jnp.float32) * logit_scale
    )
    masked = jnp.where(allowed[None], raw, -1e30)
    row_max = masked.max(axis=2)
    expo = jnp.where(allowed[None], jnp.exp(masked - row_max[:, :, None]), 0.0)
    row_sum = expo.sum(axis=2)
    weighted_values = jnp.einsum(
        "hqk,khd->qhd", expo.astype(jnp.bfloat16), values, preferred_element_type=jnp.float32
    )
    attended = (weighted_values / row_sum.T[:, :, None]).astype(jnp.bfloat16)
    grad_out = upstream.reshape(tokens, heads, HEAD_DIM)
    delta = jnp.sum(grad_out.astype(jnp.float32) * attended.astype(jnp.float32), axis=-1).T
    prob = expo / row_sum[:, :, None]
    value_part = jnp.einsum(
        "hqk,qhd->khd", prob.astype(jnp.bfloat16), grad_out, preferred_element_type=jnp.float32
    )
    probability_gradient = jnp.einsum(
        "qhd,khd->hqk", grad_out, values, preferred_element_type=jnp.float32
    )
    score_gradient = (prob * (probability_gradient - delta[:, :, None]) * logit_scale).astype(
        jnp.bfloat16
    )
    query_gradient_rows = jnp.einsum(
        "hqk,khd->qhd", score_gradient, keys, preferred_element_type=jnp.float32
    )
    key_part = jnp.einsum(
        "hqk,qhd->khd", score_gradient, queries, preferred_element_type=jnp.float32
    )
    stacked = jnp.stack(
        [key_part.reshape(reach, tokens, width), value_part.reshape(reach, tokens, width)], axis=2
    )
    partials = [stacked[distance] for distance in range(reach)]
    carried = partials[STEPS]
    for distance in range(STEPS - 1, -1, -1):
        carried = from_behind(carried, "ctx", -1)
        carried = carried + partials[distance]
    conv_grad = jnp.concatenate([query_gradient_rows.reshape(tokens, 1, width), carried], axis=1)
    grad_edge = from_behind(conv_grad[: KW - 1], "ctx", -1)
    extended = jnp.concatenate([conv_grad, grad_edge], axis=0)
    input_grad = sum((filters[:, lag, :] * extended[lag : lag + tokens] for lag in range(KW)))
    tap_terms = jnp.stack(
        [
            jnp.sum(inputs[KW - 1 - lag : KW - 1 - lag + tokens] * conv_grad, axis=0)
            for lag in range(KW)
        ],
        axis=1,
    )
    filter_grad = lax.psum(tap_terms, "ctx")
    qkv_grad = lax.all_to_all(
        input_grad.astype(jnp.bfloat16), "tp", split_axis=0, concat_axis=2, tiled=True
    )
    return (attended.reshape(tokens, width), qkv_grad, filter_grad)


def solution(mesh):
    def shards(qkv, filters, doc_ids, upstream):
        heads = upstream.shape[1] // HEAD_DIM
        tokens = upstream.shape[0]
        whole = heads % mesh.shape["ctx"] == 0 and tokens % BLOCK == 0
        form = by_heads if whole else by_ring
        return form(qkv, filters, doc_ids, upstream)

    return jax.shard_map(
        shards,
        mesh=mesh,
        in_specs=(P(("ctx", "tp"), None, None), P(None, None, "tp"), P(), P("ctx", "tp")),
        out_specs=(P("ctx", "tp"), P(("ctx", "tp"), None, None), P(None, None, "tp")),
        check_vma=False,
    )
```

```python
import jax
import jax.numpy as jnp
from jax import lax
from jax.experimental import pallas as pl
from jax.experimental.pallas import tpu as pltpu
from jax.sharding import PartitionSpec as P

HEAD_DIM = 128
KW = 7
BLOCK = 128
STEPS = 4
PAD = 8
SCALE = HEAD_DIM ** (-0.5)
AXES = ("ctx", "tp")


def dot(a, b, dims):
    return lax.dot_general(a, b, (dims, ((), ())), preferred_element_type=jnp.float32)


def estimate(flops, moved):
    return pl.CostEstimate(flops=flops, bytes_accessed=moved, transcendentals=0)


def split_columns(x, members, tp):
    streams, rows, channels = x.shape
    width = channels // tp // members
    steps = 2 if tp % 2 == 0 else 1
    part = tp // steps

    def kernel(x_ref, o_ref):
        for t in range(part):
            for c in range(members):
                at = (t * members + c) * width
                o_ref[c, t] = x_ref[:, :, at : at + width]

    return pl.pallas_call(
        kernel,
        grid=(steps,),
        in_specs=[pl.BlockSpec((streams, rows, part * members * width), lambda i: (0, 0, i))],
        out_specs=pl.BlockSpec((members, part, streams, rows, width), lambda i: (0, i, 0, 0, 0)),
        out_shape=jax.ShapeDtypeStruct((members, tp, streams, rows, width), x.dtype),
        cost_estimate=estimate(0, 4 * x.size),
        name="split_columns",
    )(x)


def join_columns(x):
    members, tp, streams, rows, width = x.shape
    steps = 2 if tp % 2 == 0 else 1
    part = tp // steps

    def kernel(x_ref, o_ref):
        for t in range(part):
            for c in range(members):
                at = (t * members + c) * width
                o_ref[:, :, at : at + width] = x_ref[c, t]

    return pl.pallas_call(
        kernel,
        grid=(steps,),
        in_specs=[pl.BlockSpec((members, part, streams, rows, width), lambda i: (0, i, 0, 0, 0))],
        out_specs=pl.BlockSpec((streams, rows, part * members * width), lambda i: (0, 0, i)),
        out_shape=jax.ShapeDtypeStruct((streams, rows, tp * members * width), x.dtype),
        cost_estimate=estimate(0, 4 * x.size),
        name="join_columns",
    )(x)


def masked_scores(docs, query, keys, block, first):
    raw = dot(query, keys, ((1,), (1,))) * SCALE
    rows = lax.broadcasted_iota(jnp.int32, (BLOCK, BLOCK), 0)
    cols = lax.broadcasted_iota(jnp.int32, (BLOCK, BLOCK), 1)
    tiles = []
    for other in range(first, block + 1):
        tile = raw[:, (other - first) * BLOCK : (other - first + 1) * BLOCK]
        if other == block:
            tile = jnp.where(cols <= rows, tile, -1e30)
        else:
            tile = jnp.where(docs[other] == docs[block], tile, -1e30)
        tiles.append(tile)
    masked = jnp.concatenate(tiles, axis=1) if len(tiles) > 1 else tiles[0]
    row_max = jnp.max(masked, axis=1, keepdims=True)
    expo = jnp.exp(masked - row_max)
    return expo, jnp.sum(expo, axis=1, keepdims=True)


def forward_kernel(docs, x_ref, taps_ref, mixed_ref, out_ref, padded):
    sources, streams, rows, _ = x_ref.shape
    tokens = sources * rows
    padded[:, 0:PAD, :] = jnp.zeros((streams, PAD, HEAD_DIM), jnp.float32)
    for m in range(streams):
        padded[m, PAD:, :] = x_ref[:, m].reshape(tokens, HEAD_DIM).astype(jnp.float32)
    for m in range(streams):
        for start in range(0, tokens, BLOCK):
            total = jnp.zeros((BLOCK, HEAD_DIM), jnp.float32)
            for lag in range(KW):
                at = PAD + start - lag
                total = total + taps_ref[m, lag : lag + 1, :] * padded[m, at : at + BLOCK, :]
            mixed_ref[0, m, start : start + BLOCK, :] = total.astype(jnp.bfloat16)
    for block in range(tokens // BLOCK):
        first = max(0, block - STEPS)
        own = slice(block * BLOCK, (block + 1) * BLOCK)
        span = slice(first * BLOCK, (block + 1) * BLOCK)
        expo, row_sum = masked_scores(
            docs, mixed_ref[0, 0, own, :], mixed_ref[0, 1, span, :], block, first
        )
        total = dot(expo.astype(jnp.bfloat16), mixed_ref[0, 2, span, :], ((1,), (0,)))
        per = out_ref.shape[1]
        at = block * BLOCK
        out_ref[at // per, at % per : at % per + BLOCK, :] = (total / row_sum).astype(
            jnp.bfloat16
        )


def forward(docs, x, taps, members):
    sources, streams, rows, width = x.shape
    per = width // HEAD_DIM
    tokens = sources * rows
    return pl.pallas_call(
        forward_kernel,
        grid_spec=pltpu.PrefetchScalarGridSpec(
            num_scalar_prefetch=1,
            grid=(per,),
            in_specs=[
                pl.BlockSpec((sources, streams, rows, HEAD_DIM), lambda h, d: (0, 0, 0, h)),
                pl.BlockSpec((streams, KW, HEAD_DIM), lambda h, d: (0, 0, h)),
            ],
            out_specs=[
                pl.BlockSpec((1, streams, tokens, HEAD_DIM), lambda h, d: (h, 0, 0, 0)),
                pl.BlockSpec((members, tokens // members, HEAD_DIM), lambda h, d: (0, 0, h)),
            ],
            scratch_shapes=[pltpu.VMEM((streams, tokens + PAD, HEAD_DIM), jnp.float32)],
        ),
        out_shape=[
            jax.ShapeDtypeStruct((per, streams, tokens, HEAD_DIM), jnp.bfloat16),
            jax.ShapeDtypeStruct((members, tokens // members, width), jnp.bfloat16),
        ],
        cost_estimate=estimate(10_000_000_000, 8 * x.size),
        name="forward",
    )(docs, x, taps)


def backward_kernel(
    docs, x_ref, taps_ref, mixed_ref, att_ref, up_ref, grad_ref, tapg_ref, padded, cgrad
):
    sources, streams, rows, _ = x_ref.shape
    tokens = sources * rows
    per = att_ref.shape[1]
    cgrad[...] = jnp.zeros_like(cgrad)
    for block in range(tokens // BLOCK):
        first = max(0, block - STEPS)
        own = slice(block * BLOCK, (block + 1) * BLOCK)
        span = slice(first * BLOCK, (block + 1) * BLOCK)
        query, keys, values = (
            mixed_ref[0, 0, own, :],
            mixed_ref[0, 1, span, :],
            mixed_ref[0, 2, span, :],
        )
        at = block * BLOCK
        up = up_ref[at // per, at % per : at % per + BLOCK, :]
        att = att_ref[at // per, at % per : at % per + BLOCK, :]
        delta = jnp.sum(up.astype(jnp.float32) * att.astype(jnp.float32), axis=1, keepdims=True)
        expo, row_sum = masked_scores(docs, query, keys, block, first)
        prob = expo / row_sum
        dprob = dot(up, values, ((1,), (1,)))
        dscore = (prob * (dprob - delta) * SCALE).astype(jnp.bfloat16)
        cgrad[0, own, :] = dot(dscore, keys, ((1,), (0,)))
        cgrad[1, span, :] += dot(dscore, query, ((0,), (0,)))
        cgrad[2, span, :] += dot(prob.astype(jnp.bfloat16), up, ((0,), (0,)))
    padded[:, 0:PAD, :] = jnp.zeros((streams, PAD, HEAD_DIM), jnp.float32)
    for m in range(streams):
        padded[m, PAD:, :] = x_ref[:, m].reshape(tokens, HEAD_DIM).astype(jnp.float32)
    for m in range(streams):
        sums = [jnp.zeros((8, HEAD_DIM), jnp.float32) for _ in range(KW)]
        for start in range(0, tokens, BLOCK):
            total = jnp.zeros((BLOCK, HEAD_DIM), jnp.float32)
            here = cgrad[m, start : start + BLOCK, :]
            for lag in range(KW):
                total = (
                    total
                    + taps_ref[m, lag : lag + 1, :]
                    * cgrad[m, start + lag : start + lag + BLOCK, :]
                )
                at = PAD + start - lag
                product = padded[m, at : at + BLOCK, :] * here
                sums[lag] = sums[lag] + jnp.sum(product.reshape(BLOCK // 8, 8, HEAD_DIM), axis=0)
            grad_ref[start // rows : (start + BLOCK) // rows, m] = total.astype(
                jnp.bfloat16
            ).reshape(BLOCK // rows, rows, HEAD_DIM)
        for lag in range(KW):
            tapg_ref[m, lag : lag + 1, :] = jnp.sum(sums[lag], axis=0, keepdims=True)


def backward(docs, x, taps, mixed, att, up):
    sources, streams, rows, width = x.shape
    per = width // HEAD_DIM
    tokens = sources * rows
    members = att.shape[0]
    slab = pl.BlockSpec((sources, streams, rows, HEAD_DIM), lambda h, d: (0, 0, 0, h))
    tap = pl.BlockSpec((streams, KW, HEAD_DIM), lambda h, d: (0, 0, h))
    rowspec = pl.BlockSpec((members, tokens // members, HEAD_DIM), lambda h, d: (0, 0, h))
    return pl.pallas_call(
        backward_kernel,
        grid_spec=pltpu.PrefetchScalarGridSpec(
            num_scalar_prefetch=1,
            grid=(per,),
            in_specs=[
                slab,
                tap,
                pl.BlockSpec((1, streams, tokens, HEAD_DIM), lambda h, d: (h, 0, 0, 0)),
                rowspec,
                rowspec,
            ],
            out_specs=[slab, tap],
            scratch_shapes=[
                pltpu.VMEM((streams, tokens + PAD, HEAD_DIM), jnp.float32),
                pltpu.VMEM((streams, tokens + PAD, HEAD_DIM), jnp.float32),
            ],
        ),
        out_shape=[
            jax.ShapeDtypeStruct(x.shape, jnp.bfloat16),
            jax.ShapeDtypeStruct(taps.shape, jnp.float32),
        ],
        cost_estimate=estimate(20_000_000_000, 12 * x.size),
        name="backward",
    )(docs, x, taps, mixed, att, up)


def swap(value, axes):
    shape = value.shape
    return lax.all_to_all(
        value.reshape(shape[0], -1, shape[-1]), axes, split_axis=0, concat_axis=0, tiled=True
    ).reshape(shape)


def gather_columns(piece, members):
    count = lax.axis_size("ctx")
    streams, taps, width = piece.shape
    pieces = [piece]
    for step in range(1, count):
        pieces.append(lax.ppermute(piece, "ctx", [(i, i ^ step) for i in range(count)]))
    position = lax.axis_index("ctx").astype(jnp.int32).reshape(1)

    def kernel(position_ref, *refs):
        o_ref = refs[-1]
        for step in range(members):
            column = lax.rem(position_ref[0] ^ step, members)
            at = pl.multiple_of(column * width, width)
            total = refs[step][...]
            for other in range(step + members, count, members):
                total = total + refs[other][...]
            o_ref[:, :, pl.ds(at, width)] = total

    whole = pl.BlockSpec((streams, taps, width), lambda i, p: (0, 0, 0))
    return pl.pallas_call(
        kernel,
        grid_spec=pltpu.PrefetchScalarGridSpec(
            num_scalar_prefetch=1,
            grid=(1,),
            in_specs=[whole] * count,
            out_specs=pl.BlockSpec((streams, taps, members * width), lambda i, p: (0, 0, 0)),
        ),
        out_shape=jax.ShapeDtypeStruct((streams, taps, members * width), piece.dtype),
        name="place_columns",
    )(position, *pieces)


def by_heads(qkv, filters, doc_ids, upstream):
    members, tp = lax.axis_size("ctx"), lax.axis_size("tp")
    width = upstream.shape[1] // members
    position = lax.axis_index("ctx")
    slabs = split_columns(jnp.transpose(qkv, (1, 0, 2)), members, tp)
    x = swap(slabs.reshape((members * tp,) + slabs.shape[2:]), AXES)
    up = swap(split_columns(upstream[None], members, 1)[:, 0, 0], "ctx")
    taps = lax.dynamic_slice_in_dim(filters, position * width, width, 2)
    mixed, att = forward(doc_ids, x, taps, members)
    attended = join_columns(swap(att, "ctx")[:, None, None])[0]
    grad, tap_grad = backward(doc_ids, x, taps, mixed, att, up)
    qkv_grad = join_columns(swap(grad, AXES).reshape(slabs.shape))
    return attended, jnp.transpose(qkv_grad, (1, 0, 2)), gather_columns(tap_grad, members)


def from_behind(value, axis, steps):
    count = lax.axis_size(axis)
    first, last = (max(0, -steps), min(count, count - steps))
    return lax.ppermute(value, axis, [(source, source + steps) for source in range(first, last)])


def block_docs(doc_ids, first_block, count):
    start = jnp.maximum(first_block, 0)
    picked = lax.dynamic_slice_in_dim(doc_ids, start, count)
    return jnp.repeat(picked, BLOCK)


def by_ring(qkv, filters, doc_ids, upstream):
    local = lax.all_to_all(qkv, "tp", split_axis=2, concat_axis=0, tiled=True)
    tokens = local.shape[0]
    width = local.shape[2]
    heads = width // HEAD_DIM
    blocks_here = tokens // BLOCK
    logit_scale = HEAD_DIM ** (-0.5)
    position = lax.axis_index("ctx")
    reach = STEPS + 1
    rim = from_behind(local[tokens - (KW - 1) :], "ctx", 1)
    inputs = jnp.concatenate([rim, local], axis=0).astype(jnp.float32)
    mixed = sum(
        (filters[:, lag, :] * inputs[KW - 1 - lag : KW - 1 - lag + tokens] for lag in range(KW))
    )
    mixed = mixed.astype(jnp.bfloat16)
    queries = mixed[:, 0].reshape(tokens, heads, HEAD_DIM)
    key_value = mixed[:, 1:3]
    tiles = [key_value]
    current = key_value
    for distance in range(1, STEPS + 1):
        current = from_behind(current, "ctx", 1)
        tiles.append(current)
    joined = jnp.concatenate(tiles, axis=0)
    keys = joined[:, 0].reshape(reach * tokens, heads, HEAD_DIM)
    values = joined[:, 1].reshape(reach * tokens, heads, HEAD_DIM)
    rows = jnp.arange(tokens)
    query_token = position * tokens + rows
    query_doc = block_docs(doc_ids, position * blocks_here, blocks_here)
    key_tokens = jnp.concatenate(
        [(position - distance) * tokens + rows for distance in range(reach)]
    )
    key_docs = jnp.concatenate(
        [
            block_docs(doc_ids, (position - distance) * blocks_here, blocks_here)
            for distance in range(reach)
        ]
    )
    allowed = (
        (key_tokens[None, :] >= 0)
        & (key_tokens[None, :] <= query_token[:, None])
        & (key_docs[None, :] == query_doc[:, None])
    )
    raw = (
        jnp.einsum("qhd,khd->hqk", queries, keys, preferred_element_type=jnp.float32) * logit_scale
    )
    masked = jnp.where(allowed[None], raw, -1e30)
    row_max = masked.max(axis=2)
    expo = jnp.where(allowed[None], jnp.exp(masked - row_max[:, :, None]), 0.0)
    row_sum = expo.sum(axis=2)
    weighted_values = jnp.einsum(
        "hqk,khd->qhd", expo.astype(jnp.bfloat16), values, preferred_element_type=jnp.float32
    )
    attended = (weighted_values / row_sum.T[:, :, None]).astype(jnp.bfloat16)
    grad_out = upstream.reshape(tokens, heads, HEAD_DIM)
    delta = jnp.sum(grad_out.astype(jnp.float32) * attended.astype(jnp.float32), axis=-1).T
    prob = expo / row_sum[:, :, None]
    value_part = jnp.einsum(
        "hqk,qhd->khd", prob.astype(jnp.bfloat16), grad_out, preferred_element_type=jnp.float32
    )
    probability_gradient = jnp.einsum(
        "qhd,khd->hqk", grad_out, values, preferred_element_type=jnp.float32
    )
    score_gradient = (prob * (probability_gradient - delta[:, :, None]) * logit_scale).astype(
        jnp.bfloat16
    )
    query_gradient_rows = jnp.einsum(
        "hqk,khd->qhd", score_gradient, keys, preferred_element_type=jnp.float32
    )
    key_part = jnp.einsum(
        "hqk,qhd->khd", score_gradient, queries, preferred_element_type=jnp.float32
    )
    stacked = jnp.stack(
        [key_part.reshape(reach, tokens, width), value_part.reshape(reach, tokens, width)], axis=2
    )
    partials = [stacked[distance] for distance in range(reach)]
    carried = partials[STEPS]
    for distance in range(STEPS - 1, -1, -1):
        carried = from_behind(carried, "ctx", -1)
        carried = carried + partials[distance]
    conv_grad = jnp.concatenate([query_gradient_rows.reshape(tokens, 1, width), carried], axis=1)
    grad_edge = from_behind(conv_grad[: KW - 1], "ctx", -1)
    extended = jnp.concatenate([conv_grad, grad_edge], axis=0)
    input_grad = sum((filters[:, lag, :] * extended[lag : lag + tokens] for lag in range(KW)))
    tap_terms = jnp.stack(
        [
            jnp.sum(inputs[KW - 1 - lag : KW - 1 - lag + tokens] * conv_grad, axis=0)
            for lag in range(KW)
        ],
        axis=1,
    )
    filter_grad = lax.psum(tap_terms, "ctx")
    qkv_grad = lax.all_to_all(
        input_grad.astype(jnp.bfloat16), "tp", split_axis=0, concat_axis=2, tiled=True
    )
    return (attended.reshape(tokens, width), qkv_grad, filter_grad)


def solution(mesh):
    def shards(qkv, filters, doc_ids, upstream):
        heads = upstream.shape[1] // HEAD_DIM
        tokens = upstream.shape[0]
        count = mesh.shape["ctx"]
        whole = heads % count == 0 and tokens % BLOCK == 0 and count & (count - 1) == 0
        form = by_heads if whole else by_ring
        return form(qkv, filters, doc_ids, upstream)

    return jax.shard_map(
        shards,
        mesh=mesh,
        in_specs=(P(("ctx", "tp"), None, None), P(None, None, "tp"), P(), P("ctx", "tp")),
        out_specs=(P("ctx", "tp"), P(("ctx", "tp"), None, None), P(None, None, "tp")),
        check_vma=False,
    )
```

```python
import jax
import jax.numpy as jnp
from jax import lax
from jax.experimental import pallas as pl
from jax.experimental.pallas import tpu as pltpu
from jax.sharding import PartitionSpec as P

HEAD_DIM = 128
KW = 7
BLOCK = 128
STEPS = 4
PAD = 8
SCALE = HEAD_DIM ** (-0.5)
AXES = ("ctx", "tp")


def dot(a, b, dims):
    return lax.dot_general(a, b, (dims, ((), ())), preferred_element_type=jnp.float32)


def room(mebibytes):
    return pltpu.CompilerParams(vmem_limit_bytes=mebibytes << 20)


def estimate(flops, moved):
    return pl.CostEstimate(flops=flops, bytes_accessed=moved, transcendentals=0)


def split_columns(x, members, tp, mebibytes):
    streams, rows, channels = x.shape
    width = channels // tp // members
    steps = 2 if tp % 2 == 0 else 1
    part = tp // steps

    def kernel(x_ref, o_ref):
        for t in range(part):
            for c in range(members):
                at = (t * members + c) * width
                o_ref[c, t] = x_ref[:, :, at : at + width]

    return pl.pallas_call(
        kernel,
        grid=(steps,),
        in_specs=[pl.BlockSpec((streams, rows, part * members * width), lambda i: (0, 0, i))],
        out_specs=pl.BlockSpec((members, part, streams, rows, width), lambda i: (0, i, 0, 0, 0)),
        out_shape=jax.ShapeDtypeStruct((members, tp, streams, rows, width), x.dtype),
        cost_estimate=estimate(0, 4 * x.size),
        compiler_params=room(mebibytes),
        name="split_columns",
    )(x)


def join_columns(x):
    members, tp, streams, rows, width = x.shape
    steps = 2 if tp % 2 == 0 else 1
    part = tp // steps

    def kernel(x_ref, o_ref):
        for t in range(part):
            for c in range(members):
                at = (t * members + c) * width
                o_ref[:, :, at : at + width] = x_ref[c, pl.program_id(0) * part + t]

    return pl.pallas_call(
        kernel,
        grid=(steps,),
        in_specs=[pl.BlockSpec(memory_space=pltpu.VMEM)],
        out_specs=pl.BlockSpec((streams, rows, part * members * width), lambda i: (0, 0, i)),
        out_shape=jax.ShapeDtypeStruct((streams, rows, tp * members * width), x.dtype),
        cost_estimate=estimate(0, 4 * x.size),
        compiler_params=room(10),
        name="join_columns",
    )(x)


def masked_scores(docs, query, keys, block, first):
    raw = dot(query, keys, ((1,), (1,))) * SCALE
    rows = lax.broadcasted_iota(jnp.int32, (BLOCK, BLOCK), 0)
    cols = lax.broadcasted_iota(jnp.int32, (BLOCK, BLOCK), 1)
    tiles = []
    for other in range(first, block + 1):
        tile = raw[:, (other - first) * BLOCK : (other - first + 1) * BLOCK]
        if other == block:
            tile = jnp.where(cols <= rows, tile, -1e30)
        else:
            tile = jnp.where(docs[other] == docs[block], tile, -1e30)
        tiles.append(tile)
    masked = jnp.concatenate(tiles, axis=1) if len(tiles) > 1 else tiles[0]
    row_max = jnp.max(masked, axis=1, keepdims=True)
    expo = jnp.exp(masked - row_max)
    return expo, jnp.sum(expo, axis=1, keepdims=True)


def forward_kernel(docs, x_ref, taps_ref, mixed_ref, out_ref, padded):
    sources, streams, rows, _ = x_ref.shape
    tokens = sources * rows
    padded[:, 0:PAD, :] = jnp.zeros((streams, PAD, HEAD_DIM), jnp.float32)
    for m in range(streams):
        padded[m, PAD:, :] = x_ref[:, m].reshape(tokens, HEAD_DIM).astype(jnp.float32)
    for m in range(streams):
        for start in range(0, tokens, BLOCK):
            total = jnp.zeros((BLOCK, HEAD_DIM), jnp.float32)
            for lag in range(KW):
                at = PAD + start - lag
                total = total + taps_ref[m, lag : lag + 1, :] * padded[m, at : at + BLOCK, :]
            mixed_ref[0, m, start : start + BLOCK, :] = total.astype(jnp.bfloat16)
    for block in range(tokens // BLOCK):
        first = max(0, block - STEPS)
        own = slice(block * BLOCK, (block + 1) * BLOCK)
        span = slice(first * BLOCK, (block + 1) * BLOCK)
        expo, row_sum = masked_scores(
            docs, mixed_ref[0, 0, own, :], mixed_ref[0, 1, span, :], block, first
        )
        total = dot(expo.astype(jnp.bfloat16), mixed_ref[0, 2, span, :], ((1,), (0,)))
        per = out_ref.shape[1]
        at = block * BLOCK
        out_ref[at // per, at % per : at % per + BLOCK, :] = (total / row_sum).astype(
            jnp.bfloat16
        )


def forward(docs, x, taps, members):
    sources, streams, rows, width = x.shape
    per = width // HEAD_DIM
    tokens = sources * rows
    return pl.pallas_call(
        forward_kernel,
        grid_spec=pltpu.PrefetchScalarGridSpec(
            num_scalar_prefetch=1,
            grid=(per,),
            in_specs=[
                pl.BlockSpec((sources, streams, rows, HEAD_DIM), lambda h, d: (0, 0, 0, h)),
                pl.BlockSpec((streams, KW, HEAD_DIM), lambda h, d: (0, 0, h)),
            ],
            out_specs=[
                pl.BlockSpec((1, streams, tokens, HEAD_DIM), lambda h, d: (h, 0, 0, 0)),
                pl.BlockSpec((members, tokens // members, HEAD_DIM), lambda h, d: (0, 0, h)),
            ],
            scratch_shapes=[pltpu.VMEM((streams, tokens + PAD, HEAD_DIM), jnp.float32)],
        ),
        out_shape=[
            jax.ShapeDtypeStruct((per, streams, tokens, HEAD_DIM), jnp.bfloat16),
            jax.ShapeDtypeStruct((members, tokens // members, width), jnp.bfloat16),
        ],
        cost_estimate=estimate(10_000_000_000, 8 * x.size),
        compiler_params=room(16),
        name="forward",
    )(docs, x, taps)


def backward_kernel(
    docs, x_ref, taps_ref, mixed_ref, att_ref, up_ref, grad_ref, tapg_ref, padded, cgrad
):
    sources, streams, rows, _ = x_ref.shape
    tokens = sources * rows
    per = att_ref.shape[1]
    cgrad[...] = jnp.zeros_like(cgrad)
    for block in range(tokens // BLOCK):
        first = max(0, block - STEPS)
        own = slice(block * BLOCK, (block + 1) * BLOCK)
        span = slice(first * BLOCK, (block + 1) * BLOCK)
        query, keys, values = (
            mixed_ref[0, 0, own, :],
            mixed_ref[0, 1, span, :],
            mixed_ref[0, 2, span, :],
        )
        at = block * BLOCK
        up = up_ref[at // per, at % per : at % per + BLOCK, :]
        att = att_ref[at // per, at % per : at % per + BLOCK, :]
        delta = jnp.sum(up.astype(jnp.float32) * att.astype(jnp.float32), axis=1, keepdims=True)
        expo, row_sum = masked_scores(docs, query, keys, block, first)
        prob = expo / row_sum
        dprob = dot(up, values, ((1,), (1,)))
        dscore = (prob * (dprob - delta) * SCALE).astype(jnp.bfloat16)
        cgrad[0, own, :] = dot(dscore, keys, ((1,), (0,)))
        cgrad[1, span, :] += dot(dscore, query, ((0,), (0,)))
        cgrad[2, span, :] += dot(prob.astype(jnp.bfloat16), up, ((0,), (0,)))
    padded[:, 0:PAD, :] = jnp.zeros((streams, PAD, HEAD_DIM), jnp.float32)
    for m in range(streams):
        padded[m, PAD:, :] = x_ref[:, m].reshape(tokens, HEAD_DIM).astype(jnp.float32)
    for m in range(streams):
        sums = [jnp.zeros((8, HEAD_DIM), jnp.float32) for _ in range(KW)]
        for start in range(0, tokens, BLOCK):
            total = jnp.zeros((BLOCK, HEAD_DIM), jnp.float32)
            here = cgrad[m, start : start + BLOCK, :]
            for lag in range(KW):
                total = (
                    total
                    + taps_ref[m, lag : lag + 1, :]
                    * cgrad[m, start + lag : start + lag + BLOCK, :]
                )
                at = PAD + start - lag
                product = padded[m, at : at + BLOCK, :] * here
                sums[lag] = sums[lag] + jnp.sum(product.reshape(BLOCK // 8, 8, HEAD_DIM), axis=0)
            grad_ref[start // rows : (start + BLOCK) // rows, m] = total.astype(
                jnp.bfloat16
            ).reshape(BLOCK // rows, rows, HEAD_DIM)
        for lag in range(KW):
            tapg_ref[m, lag : lag + 1, :] = jnp.sum(sums[lag], axis=0, keepdims=True)


def backward(docs, x, taps, mixed, att, up):
    sources, streams, rows, width = x.shape
    per = width // HEAD_DIM
    tokens = sources * rows
    members = att.shape[0]
    slab = pl.BlockSpec((sources, streams, rows, HEAD_DIM), lambda h, d: (0, 0, 0, h))
    tap = pl.BlockSpec((streams, KW, HEAD_DIM), lambda h, d: (0, 0, h))
    rowspec = pl.BlockSpec((members, tokens // members, HEAD_DIM), lambda h, d: (0, 0, h))
    return pl.pallas_call(
        backward_kernel,
        grid_spec=pltpu.PrefetchScalarGridSpec(
            num_scalar_prefetch=1,
            grid=(per,),
            in_specs=[
                slab,
                tap,
                pl.BlockSpec((1, streams, tokens, HEAD_DIM), lambda h, d: (h, 0, 0, 0)),
                rowspec,
                rowspec,
            ],
            out_specs=[slab, tap],
            scratch_shapes=[
                pltpu.VMEM((streams, tokens + PAD, HEAD_DIM), jnp.float32),
                pltpu.VMEM((streams, tokens + PAD, HEAD_DIM), jnp.float32),
            ],
        ),
        out_shape=[
            jax.ShapeDtypeStruct(x.shape, jnp.bfloat16),
            jax.ShapeDtypeStruct(taps.shape, jnp.float32),
        ],
        cost_estimate=estimate(20_000_000_000, 12 * x.size),
        compiler_params=room(24),
        name="backward",
    )(docs, x, taps, mixed, att, up)


def swap(value, axes):
    shape = value.shape
    return lax.all_to_all(
        value.reshape(shape[0], -1, shape[-1]), axes, split_axis=0, concat_axis=0, tiled=True
    ).reshape(shape)


def gather_columns(piece, members, after):
    count = lax.axis_size("ctx")
    position = lax.axis_index("ctx").astype(jnp.int32)
    streams, taps, width = piece.shape
    other = lax.ppermute(piece, "ctx", [(i, i ^ 1) for i in range(count)])
    even = position % 2 == 0
    pair = jnp.concatenate(
        [jnp.where(even, piece, other), jnp.where(even, other, piece)], axis=-1
    )
    pair, after = lax.optimization_barrier((pair, after))
    pairs = [pair]
    for step in range(2, count, 2):
        pairs.append(lax.ppermute(pair, "ctx", [(i, i ^ step) for i in range(count)]))

    def kernel(position_ref, *refs):
        o_ref = refs[-1]
        for step in range(0, members, 2):
            column = lax.rem(position_ref[0] ^ step, members) // 2
            at = pl.multiple_of(column * 2 * width, 2 * width)
            total = refs[step // 2][...]
            for further in range(step + members, count, members):
                total = total + refs[further // 2][...]
            o_ref[:, :, pl.ds(at, 2 * width)] = total

    whole = pl.BlockSpec((streams, taps, 2 * width), lambda i, p: (0, 0, 0))
    gathered = pl.pallas_call(
        kernel,
        grid_spec=pltpu.PrefetchScalarGridSpec(
            num_scalar_prefetch=1,
            grid=(1,),
            in_specs=[whole] * (count // 2),
            out_specs=pl.BlockSpec((streams, taps, members * width), lambda i, p: (0, 0, 0)),
        ),
        out_shape=jax.ShapeDtypeStruct((streams, taps, members * width), piece.dtype),
        compiler_params=room(4),
        name="place_columns",
    )(position.reshape(1), *pairs)
    return gathered, after


def by_heads(qkv, filters, doc_ids, upstream):
    members, tp = lax.axis_size("ctx"), lax.axis_size("tp")
    width = upstream.shape[1] // members
    position = lax.axis_index("ctx")
    slabs = split_columns(jnp.transpose(qkv, (1, 0, 2)), members, tp, 60)
    x = swap(slabs.reshape((members * tp,) + slabs.shape[2:]), AXES)
    up = swap(split_columns(upstream[None], members, 1, 10)[:, 0, 0], "ctx")
    taps = lax.dynamic_slice_in_dim(filters, position * width, width, 2)
    mixed, att = forward(doc_ids, x, taps, members)
    attended = join_columns(swap(att, "ctx")[:, None, None])[0]
    grad, tap_grad = backward(doc_ids, x, taps, mixed, att, up)
    qkv_grad = join_columns(swap(grad, AXES).reshape(slabs.shape))
    filter_grad, attended = gather_columns(tap_grad, members, attended)
    return attended, jnp.transpose(qkv_grad, (1, 0, 2)), filter_grad


def from_behind(value, axis, steps):
    count = lax.axis_size(axis)
    first, last = (max(0, -steps), min(count, count - steps))
    return lax.ppermute(value, axis, [(source, source + steps) for source in range(first, last)])


def block_docs(doc_ids, first_block, count):
    start = jnp.maximum(first_block, 0)
    picked = lax.dynamic_slice_in_dim(doc_ids, start, count)
    return jnp.repeat(picked, BLOCK)


def by_ring(qkv, filters, doc_ids, upstream):
    local = lax.all_to_all(qkv, "tp", split_axis=2, concat_axis=0, tiled=True)
    tokens = local.shape[0]
    width = local.shape[2]
    heads = width // HEAD_DIM
    blocks_here = tokens // BLOCK
    logit_scale = HEAD_DIM ** (-0.5)
    position = lax.axis_index("ctx")
    reach = STEPS + 1
    rim = from_behind(local[tokens - (KW - 1) :], "ctx", 1)
    inputs = jnp.concatenate([rim, local], axis=0).astype(jnp.float32)
    mixed = sum(
        (filters[:, lag, :] * inputs[KW - 1 - lag : KW - 1 - lag + tokens] for lag in range(KW))
    )
    mixed = mixed.astype(jnp.bfloat16)
    queries = mixed[:, 0].reshape(tokens, heads, HEAD_DIM)
    key_value = mixed[:, 1:3]
    tiles = [key_value]
    current = key_value
    for distance in range(1, STEPS + 1):
        current = from_behind(current, "ctx", 1)
        tiles.append(current)
    joined = jnp.concatenate(tiles, axis=0)
    keys = joined[:, 0].reshape(reach * tokens, heads, HEAD_DIM)
    values = joined[:, 1].reshape(reach * tokens, heads, HEAD_DIM)
    rows = jnp.arange(tokens)
    query_token = position * tokens + rows
    query_doc = block_docs(doc_ids, position * blocks_here, blocks_here)
    key_tokens = jnp.concatenate(
        [(position - distance) * tokens + rows for distance in range(reach)]
    )
    key_docs = jnp.concatenate(
        [
            block_docs(doc_ids, (position - distance) * blocks_here, blocks_here)
            for distance in range(reach)
        ]
    )
    allowed = (
        (key_tokens[None, :] >= 0)
        & (key_tokens[None, :] <= query_token[:, None])
        & (key_docs[None, :] == query_doc[:, None])
    )
    raw = (
        jnp.einsum("qhd,khd->hqk", queries, keys, preferred_element_type=jnp.float32) * logit_scale
    )
    masked = jnp.where(allowed[None], raw, -1e30)
    row_max = masked.max(axis=2)
    expo = jnp.where(allowed[None], jnp.exp(masked - row_max[:, :, None]), 0.0)
    row_sum = expo.sum(axis=2)
    weighted_values = jnp.einsum(
        "hqk,khd->qhd", expo.astype(jnp.bfloat16), values, preferred_element_type=jnp.float32
    )
    attended = (weighted_values / row_sum.T[:, :, None]).astype(jnp.bfloat16)
    grad_out = upstream.reshape(tokens, heads, HEAD_DIM)
    delta = jnp.sum(grad_out.astype(jnp.float32) * attended.astype(jnp.float32), axis=-1).T
    prob = expo / row_sum[:, :, None]
    value_part = jnp.einsum(
        "hqk,qhd->khd", prob.astype(jnp.bfloat16), grad_out, preferred_element_type=jnp.float32
    )
    probability_gradient = jnp.einsum(
        "qhd,khd->hqk", grad_out, values, preferred_element_type=jnp.float32
    )
    score_gradient = (prob * (probability_gradient - delta[:, :, None]) * logit_scale).astype(
        jnp.bfloat16
    )
    query_gradient_rows = jnp.einsum(
        "hqk,khd->qhd", score_gradient, keys, preferred_element_type=jnp.float32
    )
    key_part = jnp.einsum(
        "hqk,qhd->khd", score_gradient, queries, preferred_element_type=jnp.float32
    )
    stacked = jnp.stack(
        [key_part.reshape(reach, tokens, width), value_part.reshape(reach, tokens, width)], axis=2
    )
    partials = [stacked[distance] for distance in range(reach)]
    carried = partials[STEPS]
    for distance in range(STEPS - 1, -1, -1):
        carried = from_behind(carried, "ctx", -1)
        carried = carried + partials[distance]
    conv_grad = jnp.concatenate([query_gradient_rows.reshape(tokens, 1, width), carried], axis=1)
    grad_edge = from_behind(conv_grad[: KW - 1], "ctx", -1)
    extended = jnp.concatenate([conv_grad, grad_edge], axis=0)
    input_grad = sum((filters[:, lag, :] * extended[lag : lag + tokens] for lag in range(KW)))
    tap_terms = jnp.stack(
        [
            jnp.sum(inputs[KW - 1 - lag : KW - 1 - lag + tokens] * conv_grad, axis=0)
            for lag in range(KW)
        ],
        axis=1,
    )
    filter_grad = lax.psum(tap_terms, "ctx")
    qkv_grad = lax.all_to_all(
        input_grad.astype(jnp.bfloat16), "tp", split_axis=0, concat_axis=2, tiled=True
    )
    return (attended.reshape(tokens, width), qkv_grad, filter_grad)


def solution(mesh):
    def shards(qkv, filters, doc_ids, upstream):
        heads = upstream.shape[1] // HEAD_DIM
        tokens = upstream.shape[0]
        count = mesh.shape["ctx"]
        whole = heads % count == 0 and tokens % BLOCK == 0 and count & (count - 1) == 0
        form = by_heads if whole else by_ring
        return form(qkv, filters, doc_ids, upstream)

    return jax.shard_map(
        shards,
        mesh=mesh,
        in_specs=(P(("ctx", "tp"), None, None), P(None, None, "tp"), P(), P("ctx", "tp")),
        out_specs=(P("ctx", "tp"), P(("ctx", "tp"), None, None), P(None, None, "tp")),
        check_vma=False,
    )
```

```python
import functools

import jax
import jax.numpy as jnp
from jax import lax
from jax.experimental import pallas as pl
from jax.experimental.pallas import tpu as pltpu
from jax.sharding import PartitionSpec as P

HEAD_DIM = 128
KW = 7
BLOCK = 128
STEPS = 4
PAD = 8
SCALE = HEAD_DIM ** (-0.5)
AXES = ("ctx", "tp")


def dot(a, b, dims):
    return lax.dot_general(a, b, (dims, ((), ())), preferred_element_type=jnp.float32)


def room(mebibytes):
    return pltpu.CompilerParams(vmem_limit_bytes=mebibytes << 20)


def estimate(flops, moved):
    return pl.CostEstimate(flops=flops, bytes_accessed=moved, transcendentals=0)


def split_columns(x, members, tp, mebibytes):
    streams, rows, channels = x.shape
    width = channels // tp // members
    steps = 2 if tp % 2 == 0 else 1
    part = tp // steps

    def kernel(x_ref, o_ref):
        for t in range(part):
            for c in range(members):
                at = (t * members + c) * width
                o_ref[c, t] = x_ref[:, :, at : at + width]

    return pl.pallas_call(
        kernel,
        grid=(steps,),
        in_specs=[pl.BlockSpec((streams, rows, part * members * width), lambda i: (0, 0, i))],
        out_specs=pl.BlockSpec((members, part, streams, rows, width), lambda i: (0, i, 0, 0, 0)),
        out_shape=jax.ShapeDtypeStruct((members, tp, streams, rows, width), x.dtype),
        cost_estimate=estimate(0, 4 * x.size),
        compiler_params=room(mebibytes),
        name="split_columns",
    )(x)


def join_columns(x):
    members, tp, streams, rows, width = x.shape
    steps = 2 if tp % 2 == 0 else 1
    part = tp // steps

    def kernel(x_ref, o_ref):
        for t in range(part):
            for c in range(members):
                at = (t * members + c) * width
                o_ref[:, :, at : at + width] = x_ref[c, pl.program_id(0) * part + t]

    return pl.pallas_call(
        kernel,
        grid=(steps,),
        in_specs=[pl.BlockSpec(memory_space=pltpu.VMEM)],
        out_specs=pl.BlockSpec((streams, rows, part * members * width), lambda i: (0, 0, i)),
        out_shape=jax.ShapeDtypeStruct((streams, rows, tp * members * width), x.dtype),
        cost_estimate=estimate(0, 4 * x.size),
        compiler_params=room(10),
        name="join_columns",
    )(x)


def masked_scores(docs, query, keys, block, first):
    raw = dot(query, keys, ((1,), (1,))) * SCALE
    rows = lax.broadcasted_iota(jnp.int32, (BLOCK, BLOCK), 0)
    cols = lax.broadcasted_iota(jnp.int32, (BLOCK, BLOCK), 1)
    tiles = []
    for other in range(first, block + 1):
        tile = raw[:, (other - first) * BLOCK : (other - first + 1) * BLOCK]
        if other == block:
            tile = jnp.where(cols <= rows, tile, -1e30)
        else:
            tile = jnp.where(docs[other] == docs[block], tile, -1e30)
        tiles.append(tile)
    masked = jnp.concatenate(tiles, axis=1) if len(tiles) > 1 else tiles[0]
    row_max = jnp.max(masked, axis=1, keepdims=True)
    expo = jnp.exp(masked - row_max)
    return expo, jnp.sum(expo, axis=1, keepdims=True)


def forward_kernel(docs, x_ref, taps_ref, before_ref, mixed_ref, out_ref, padded):
    sources, streams, rows, _ = x_ref.shape
    tokens = sources * rows
    padded[:, 0:PAD, :] = before_ref[...].astype(jnp.float32)
    for m in range(streams):
        padded[m, PAD:, :] = x_ref[:, m].reshape(tokens, HEAD_DIM).astype(jnp.float32)
    for m in range(streams):
        for start in range(0, tokens, BLOCK):
            total = jnp.zeros((BLOCK, HEAD_DIM), jnp.float32)
            for lag in range(KW):
                at = PAD + start - lag
                total = total + taps_ref[m, lag : lag + 1, :] * padded[m, at : at + BLOCK, :]
            mixed_ref[0, m, start : start + BLOCK, :] = total.astype(jnp.bfloat16)
    for block in range(tokens // BLOCK):
        first = max(0, block - STEPS)
        own = slice(block * BLOCK, (block + 1) * BLOCK)
        span = slice(first * BLOCK, (block + 1) * BLOCK)
        expo, row_sum = masked_scores(
            docs, mixed_ref[0, 0, own, :], mixed_ref[0, 1, span, :], block, first
        )
        total = dot(expo.astype(jnp.bfloat16), mixed_ref[0, 2, span, :], ((1,), (0,)))
        per = out_ref.shape[1]
        at = block * BLOCK
        out_ref[at // per, at % per : at % per + BLOCK, :] = (total / row_sum).astype(
            jnp.bfloat16
        )


def forward(docs, x, taps, before, members):
    sources, streams, rows, width = x.shape
    per = width // HEAD_DIM
    tokens = sources * rows
    return pl.pallas_call(
        forward_kernel,
        grid_spec=pltpu.PrefetchScalarGridSpec(
            num_scalar_prefetch=1,
            grid=(per,),
            in_specs=[
                pl.BlockSpec((sources, streams, rows, HEAD_DIM), lambda h, d: (0, 0, 0, h)),
                pl.BlockSpec((streams, KW, HEAD_DIM), lambda h, d: (0, 0, h)),
                pl.BlockSpec((streams, PAD, HEAD_DIM), lambda h, d: (0, 0, h)),
            ],
            out_specs=[
                pl.BlockSpec((1, streams, tokens, HEAD_DIM), lambda h, d: (h, 0, 0, 0)),
                pl.BlockSpec((members, tokens // members, HEAD_DIM), lambda h, d: (0, 0, h)),
            ],
            scratch_shapes=[pltpu.VMEM((streams, tokens + PAD, HEAD_DIM), jnp.float32)],
        ),
        out_shape=[
            jax.ShapeDtypeStruct((per, streams, tokens, HEAD_DIM), jnp.bfloat16),
            jax.ShapeDtypeStruct((members, tokens // members, width), jnp.bfloat16),
        ],
        cost_estimate=estimate(10_000_000_000, 8 * x.size),
        compiler_params=room(16),
        name="forward",
    )(docs, x, taps, before)


def backward_kernel(
    docs,
    x_ref,
    taps_ref,
    before_ref,
    mixed_ref,
    att_ref,
    up_ref,
    grad_ref,
    tapg_ref,
    head_ref,
    tail_ref,
    padded,
    cgrad,
):
    sources, streams, rows, _ = x_ref.shape
    tokens = sources * rows
    per = att_ref.shape[1]
    cgrad[...] = jnp.zeros_like(cgrad)
    for block in range(tokens // BLOCK):
        first = max(0, block - STEPS)
        own = slice(block * BLOCK, (block + 1) * BLOCK)
        span = slice(first * BLOCK, (block + 1) * BLOCK)
        query, keys, values = (
            mixed_ref[0, 0, own, :],
            mixed_ref[0, 1, span, :],
            mixed_ref[0, 2, span, :],
        )
        at = block * BLOCK
        up = up_ref[at // per, at % per : at % per + BLOCK, :]
        att = att_ref[at // per, at % per : at % per + BLOCK, :]
        delta = jnp.sum(up.astype(jnp.float32) * att.astype(jnp.float32), axis=1, keepdims=True)
        expo, row_sum = masked_scores(docs, query, keys, block, first)
        prob = expo / row_sum
        dprob = dot(up, values, ((1,), (1,)))
        dscore = (prob * (dprob - delta) * SCALE).astype(jnp.bfloat16)
        cgrad[0, own, :] = dot(dscore, keys, ((1,), (0,)))
        cgrad[1, span, :] += dot(dscore, query, ((0,), (0,)))
        cgrad[2, span, :] += dot(prob.astype(jnp.bfloat16), up, ((0,), (0,)))
    padded[:, 0:PAD, :] = before_ref[...].astype(jnp.float32)
    head_ref[...] = cgrad[:, 0:PAD, :]
    for m in range(streams):
        padded[m, PAD:, :] = x_ref[:, m].reshape(tokens, HEAD_DIM).astype(jnp.float32)
    for m in range(streams):
        sums = [jnp.zeros((8, HEAD_DIM), jnp.float32) for _ in range(KW)]
        for start in range(0, tokens, BLOCK):
            total = jnp.zeros((BLOCK, HEAD_DIM), jnp.float32)
            here = cgrad[m, start : start + BLOCK, :]
            for lag in range(KW):
                total = (
                    total
                    + taps_ref[m, lag : lag + 1, :]
                    * cgrad[m, start + lag : start + lag + BLOCK, :]
                )
                at = PAD + start - lag
                product = padded[m, at : at + BLOCK, :] * here
                sums[lag] = sums[lag] + jnp.sum(product.reshape(BLOCK // 8, 8, HEAD_DIM), axis=0)
            grad_ref[start // rows : (start + BLOCK) // rows, m] = total.astype(
                jnp.bfloat16
            ).reshape(BLOCK // rows, rows, HEAD_DIM)
        tail_ref[m] = total[BLOCK - PAD :]
        for lag in range(KW):
            tapg_ref[m, lag : lag + 1, :] = jnp.sum(sums[lag], axis=0, keepdims=True)


def backward(docs, x, taps, before, mixed, att, up):
    sources, streams, rows, width = x.shape
    per = width // HEAD_DIM
    tokens = sources * rows
    members = att.shape[0]
    slab = pl.BlockSpec((sources, streams, rows, HEAD_DIM), lambda h, d: (0, 0, 0, h))
    tap = pl.BlockSpec((streams, KW, HEAD_DIM), lambda h, d: (0, 0, h))
    edge = pl.BlockSpec((streams, PAD, HEAD_DIM), lambda h, d: (0, 0, h))
    rowspec = pl.BlockSpec((members, tokens // members, HEAD_DIM), lambda h, d: (0, 0, h))
    return pl.pallas_call(
        backward_kernel,
        grid_spec=pltpu.PrefetchScalarGridSpec(
            num_scalar_prefetch=1,
            grid=(per,),
            in_specs=[
                slab,
                tap,
                edge,
                pl.BlockSpec((1, streams, tokens, HEAD_DIM), lambda h, d: (h, 0, 0, 0)),
                rowspec,
                rowspec,
            ],
            out_specs=[slab, tap, edge, edge],
            scratch_shapes=[
                pltpu.VMEM((streams, tokens + PAD, HEAD_DIM), jnp.float32),
                pltpu.VMEM((streams, tokens + PAD, HEAD_DIM), jnp.float32),
            ],
        ),
        out_shape=[
            jax.ShapeDtypeStruct(x.shape, jnp.bfloat16),
            jax.ShapeDtypeStruct(taps.shape, jnp.float32),
            jax.ShapeDtypeStruct((streams, PAD, width), jnp.float32),
            jax.ShapeDtypeStruct((streams, PAD, width), jnp.float32),
        ],
        cost_estimate=estimate(20_000_000_000, 12 * x.size),
        compiler_params=room(24),
        name="backward",
    )(docs, x, taps, before, mixed, att, up)


def swap(value, axes, groups):
    shape = value.shape
    return lax.all_to_all(
        value.reshape(shape[0], -1, shape[-1]),
        axes,
        split_axis=0,
        concat_axis=0,
        axis_index_groups=groups,
        tiled=True,
    ).reshape(shape)


def across(value, step):
    count = lax.axis_size("ctx")
    return lax.ppermute(value, "ctx", [(i, i ^ step) for i in range(count)])


def gather_columns(piece, members, after):
    count = lax.axis_size("ctx")
    position = lax.axis_index("ctx").astype(jnp.int32)
    streams, taps, width = piece.shape
    if members < count:
        span, held = 1, piece + across(piece, members)
    else:
        span, other = 2, across(piece, 1)
        even = position % 2 == 0
        held = jnp.concatenate(
            [jnp.where(even, piece, other), jnp.where(even, other, piece)], axis=-1
        )
    held, after = lax.optimization_barrier((held, after))
    steps = range(0, members, span)
    pieces = [across(held, step) if step else held for step in steps]

    def kernel(position_ref, *refs):
        o_ref = refs[-1]
        for step in steps:
            column = lax.rem(position_ref[0] ^ step, members) // span
            at = pl.multiple_of(column * span * width, span * width)
            o_ref[:, :, pl.ds(at, span * width)] = refs[step // span][...]

    gathered = pl.pallas_call(
        kernel,
        grid_spec=pltpu.PrefetchScalarGridSpec(
            num_scalar_prefetch=1,
            grid=(1,),
            in_specs=[pl.BlockSpec((streams, taps, span * width), lambda i, p: (0, 0, 0))]
            * len(pieces),
            out_specs=pl.BlockSpec((streams, taps, members * width), lambda i, p: (0, 0, 0)),
        ),
        out_shape=jax.ShapeDtypeStruct((streams, taps, members * width), piece.dtype),
        compiler_params=room(4),
        name="place_columns",
    )(position.reshape(1), *pieces)
    return gathered, after


def by_heads(parts, qkv, filters, doc_ids, upstream):
    count, tp = lax.axis_size("ctx"), lax.axis_size("tp")
    members = count // parts
    rows, streams, _ = qkv.shape
    width = upstream.shape[1] // members
    position = lax.axis_index("ctx")
    every = everywhere = None
    if parts > 1:
        every = [[p * members + c for c in range(members)] for p in range(parts)]
        everywhere = [[c * tp + t for c in group for t in range(tp)] for group in every]
        blocks = doc_ids.shape[0] // parts
        doc_ids = lax.dynamic_slice_in_dim(doc_ids, position // members * blocks, blocks)
    slabs = split_columns(jnp.transpose(qkv, (1, 0, 2)), members, tp, 60)
    x = swap(slabs.reshape((members * tp,) + slabs.shape[2:]), AXES, everywhere)
    up = swap(split_columns(upstream[None], members, 1, 10)[:, 0, 0], "ctx", every)
    taps = lax.dynamic_slice_in_dim(filters, position % members * width, width, 2)
    if parts > 1:
        upward = [(i, i + members) for i in range(count - members)]
        before = lax.ppermute(x[-1, :, rows - PAD :], "ctx", upward)
    else:
        before = jnp.zeros((streams, PAD, width), x.dtype)
    mixed, att = forward(doc_ids, x, taps, before, members)
    attended = join_columns(swap(att, "ctx", every)[:, None, None])[0]
    grad, tap_grad, head, tail = backward(doc_ids, x, taps, before, mixed, att, up)
    if parts > 1:
        after = lax.ppermute(head, "ctx", [(to, source) for source, to in upward])
        after = jnp.concatenate([jnp.zeros_like(after), after], axis=1)
        for lag in range(KW):
            tail = tail + taps[:, lag : lag + 1] * after[:, lag : lag + PAD]
        grad = grad.at[-1, :, rows - PAD :].set(tail.astype(grad.dtype))
    filter_grad, attended = gather_columns(tap_grad, members, attended)
    qkv_grad = join_columns(swap(grad, AXES, everywhere).reshape(slabs.shape))
    return attended, jnp.transpose(qkv_grad, (1, 0, 2)), filter_grad


def from_behind(value, axis, steps):
    count = lax.axis_size(axis)
    first, last = (max(0, -steps), min(count, count - steps))
    return lax.ppermute(value, axis, [(source, source + steps) for source in range(first, last)])


def block_docs(doc_ids, first_block, count):
    start = jnp.maximum(first_block, 0)
    picked = lax.dynamic_slice_in_dim(doc_ids, start, count)
    return jnp.repeat(picked, BLOCK)


def by_ring(qkv, filters, doc_ids, upstream):
    local = lax.all_to_all(qkv, "tp", split_axis=2, concat_axis=0, tiled=True)
    tokens = local.shape[0]
    width = local.shape[2]
    heads = width // HEAD_DIM
    blocks_here = tokens // BLOCK
    logit_scale = HEAD_DIM ** (-0.5)
    position = lax.axis_index("ctx")
    reach = STEPS + 1
    rim = from_behind(local[tokens - (KW - 1) :], "ctx", 1)
    inputs = jnp.concatenate([rim, local], axis=0).astype(jnp.float32)
    mixed = sum(
        (filters[:, lag, :] * inputs[KW - 1 - lag : KW - 1 - lag + tokens] for lag in range(KW))
    )
    mixed = mixed.astype(jnp.bfloat16)
    queries = mixed[:, 0].reshape(tokens, heads, HEAD_DIM)
    key_value = mixed[:, 1:3]
    tiles = [key_value]
    current = key_value
    for distance in range(1, STEPS + 1):
        current = from_behind(current, "ctx", 1)
        tiles.append(current)
    joined = jnp.concatenate(tiles, axis=0)
    keys = joined[:, 0].reshape(reach * tokens, heads, HEAD_DIM)
    values = joined[:, 1].reshape(reach * tokens, heads, HEAD_DIM)
    rows = jnp.arange(tokens)
    query_token = position * tokens + rows
    query_doc = block_docs(doc_ids, position * blocks_here, blocks_here)
    key_tokens = jnp.concatenate(
        [(position - distance) * tokens + rows for distance in range(reach)]
    )
    key_docs = jnp.concatenate(
        [
            block_docs(doc_ids, (position - distance) * blocks_here, blocks_here)
            for distance in range(reach)
        ]
    )
    allowed = (
        (key_tokens[None, :] >= 0)
        & (key_tokens[None, :] <= query_token[:, None])
        & (key_docs[None, :] == query_doc[:, None])
    )
    raw = (
        jnp.einsum("qhd,khd->hqk", queries, keys, preferred_element_type=jnp.float32) * logit_scale
    )
    masked = jnp.where(allowed[None], raw, -1e30)
    row_max = masked.max(axis=2)
    expo = jnp.where(allowed[None], jnp.exp(masked - row_max[:, :, None]), 0.0)
    row_sum = expo.sum(axis=2)
    weighted_values = jnp.einsum(
        "hqk,khd->qhd", expo.astype(jnp.bfloat16), values, preferred_element_type=jnp.float32
    )
    attended = (weighted_values / row_sum.T[:, :, None]).astype(jnp.bfloat16)
    grad_out = upstream.reshape(tokens, heads, HEAD_DIM)
    delta = jnp.sum(grad_out.astype(jnp.float32) * attended.astype(jnp.float32), axis=-1).T
    prob = expo / row_sum[:, :, None]
    value_part = jnp.einsum(
        "hqk,qhd->khd", prob.astype(jnp.bfloat16), grad_out, preferred_element_type=jnp.float32
    )
    probability_gradient = jnp.einsum(
        "qhd,khd->hqk", grad_out, values, preferred_element_type=jnp.float32
    )
    score_gradient = (prob * (probability_gradient - delta[:, :, None]) * logit_scale).astype(
        jnp.bfloat16
    )
    query_gradient_rows = jnp.einsum(
        "hqk,khd->qhd", score_gradient, keys, preferred_element_type=jnp.float32
    )
    key_part = jnp.einsum(
        "hqk,qhd->khd", score_gradient, queries, preferred_element_type=jnp.float32
    )
    stacked = jnp.stack(
        [key_part.reshape(reach, tokens, width), value_part.reshape(reach, tokens, width)], axis=2
    )
    partials = [stacked[distance] for distance in range(reach)]
    carried = partials[STEPS]
    for distance in range(STEPS - 1, -1, -1):
        carried = from_behind(carried, "ctx", -1)
        carried = carried + partials[distance]
    conv_grad = jnp.concatenate([query_gradient_rows.reshape(tokens, 1, width), carried], axis=1)
    grad_edge = from_behind(conv_grad[: KW - 1], "ctx", -1)
    extended = jnp.concatenate([conv_grad, grad_edge], axis=0)
    input_grad = sum((filters[:, lag, :] * extended[lag : lag + tokens] for lag in range(KW)))
    tap_terms = jnp.stack(
        [
            jnp.sum(inputs[KW - 1 - lag : KW - 1 - lag + tokens] * conv_grad, axis=0)
            for lag in range(KW)
        ],
        axis=1,
    )
    filter_grad = lax.psum(tap_terms, "ctx")
    qkv_grad = lax.all_to_all(
        input_grad.astype(jnp.bfloat16), "tp", split_axis=0, concat_axis=2, tiled=True
    )
    return (attended.reshape(tokens, width), qkv_grad, filter_grad)


def solution(mesh):
    count = mesh.shape["ctx"]

    def shards(qkv, filters, doc_ids, upstream):
        tokens, width = upstream.shape
        heads = width // HEAD_DIM
        args = (qkv, filters, doc_ids, upstream)
        even = tokens % BLOCK == 0 and qkv.shape[0] % PAD == 0 and count & (count - 1) == 0
        if heads % count or not even or count < 4:
            return by_ring(*args)
        middle = doc_ids.shape[0] // 2
        apart = doc_ids[middle - 1] != doc_ids[middle]
        return lax.cond(
            apart, functools.partial(by_heads, 2), functools.partial(by_heads, 1), *args
        )

    return jax.shard_map(
        shards,
        mesh=mesh,
        in_specs=(P(("ctx", "tp"), None, None), P(None, None, "tp"), P(), P("ctx", "tp")),
        out_specs=(P("ctx", "tp"), P(("ctx", "tp"), None, None), P(None, None, "tp")),
        check_vma=False,
    )
```

```python
import functools

import jax
import jax.numpy as jnp
from jax import lax
from jax.experimental import pallas as pl
from jax.experimental.pallas import tpu as pltpu
from jax.sharding import PartitionSpec as P

HEAD_DIM = 128
KW = 7
BLOCK = 128
STEPS = 4
PAD = 8
SCALE = HEAD_DIM ** (-0.5)
AXES = ("ctx", "tp")
FORE, BACK, SPREAD = 24, 24, 16


def dot(a, b, dims):
    return lax.dot_general(a, b, (dims, ((), ())), preferred_element_type=jnp.float32)


def room(mebibytes):
    return pltpu.CompilerParams(vmem_limit_bytes=mebibytes << 20)


def estimate(flops, moved):
    return pl.CostEstimate(flops=flops, bytes_accessed=moved, transcendentals=0)


def split_columns(x, members, tp, mebibytes):
    streams, rows, channels = x.shape
    width = channels // tp // members
    steps = 2 if tp % 2 == 0 else 1
    part = tp // steps

    def kernel(x_ref, o_ref):
        for t in range(part):
            for c in range(members):
                at = (t * members + c) * width
                o_ref[c, t] = x_ref[:, :, at : at + width]

    return pl.pallas_call(
        kernel,
        grid=(steps,),
        in_specs=[pl.BlockSpec((streams, rows, part * members * width), lambda i: (0, 0, i))],
        out_specs=pl.BlockSpec((members, part, streams, rows, width), lambda i: (0, i, 0, 0, 0)),
        out_shape=jax.ShapeDtypeStruct((members, tp, streams, rows, width), x.dtype),
        cost_estimate=estimate(0, 4 * x.size),
        compiler_params=room(mebibytes),
        name="split_columns",
    )(x)


def join_columns(x):
    members, tp, streams, rows, width = x.shape
    steps = 2 if tp % 2 == 0 else 1
    part = tp // steps

    def kernel(x_ref, o_ref):
        for t in range(part):
            for c in range(members):
                at = (t * members + c) * width
                o_ref[:, :, at : at + width] = x_ref[c, pl.program_id(0) * part + t]

    return pl.pallas_call(
        kernel,
        grid=(steps,),
        in_specs=[pl.BlockSpec(memory_space=pltpu.VMEM)],
        out_specs=pl.BlockSpec((streams, rows, part * members * width), lambda i: (0, 0, i)),
        out_shape=jax.ShapeDtypeStruct((streams, rows, tp * members * width), x.dtype),
        cost_estimate=estimate(0, 4 * x.size),
        compiler_params=room(10),
        name="join_columns",
    )(x)


def row_blocks(tokens):
    spans, start = [], 0
    for block in range(tokens // BLOCK):
        first = max(0, block - STEPS)
        spans.append((block, first, start))
        start += block + 1 - first
    return spans, start


def forward_kernel(docs, x_ref, taps_ref, before_ref, mixed_ref, prob_ref, out_ref, padded):
    sources, streams, rows, _ = x_ref.shape
    tokens = sources * rows
    head = pl.program_id(0)
    lanes = pl.ds(pl.multiple_of(head * HEAD_DIM, HEAD_DIM), HEAD_DIM)
    padded[:, 0:PAD, :] = before_ref[:, :, lanes].astype(jnp.float32)
    for m in range(streams):
        padded[m, PAD:, :] = x_ref[:, m, :, lanes].reshape(tokens, HEAD_DIM).astype(jnp.float32)
    for m in range(streams):
        for start in range(0, tokens, BLOCK):
            total = jnp.zeros((BLOCK, HEAD_DIM), jnp.float32)
            for lag in range(KW):
                at = PAD + start - lag
                total = total + taps_ref[m, lag : lag + 1, lanes] * padded[m, at : at + BLOCK, :]
            mixed_ref[0, m, start : start + BLOCK, :] = total.astype(jnp.bfloat16)
    below = lax.broadcasted_iota(jnp.int32, (BLOCK, BLOCK), 0) >= lax.broadcasted_iota(
        jnp.int32, (BLOCK, BLOCK), 1
    )
    for block, first, tile in row_blocks(tokens)[0]:
        own = slice(block * BLOCK, (block + 1) * BLOCK)
        span = slice(first * BLOCK, (block + 1) * BLOCK)
        raw = dot(mixed_ref[0, 0, own, :], mixed_ref[0, 1, span, :], ((1,), (1,))) * SCALE
        parts = []
        for other in range(first, block + 1):
            part = raw[:, (other - first) * BLOCK : (other - first + 1) * BLOCK]
            allowed = below if other == block else docs[other] == docs[block]
            parts.append(jnp.where(allowed, part, -1e30))
        masked = jnp.concatenate(parts, axis=1) if len(parts) > 1 else parts[0]
        expo = jnp.exp(masked - jnp.max(masked, axis=1, keepdims=True))
        row_sum = jnp.sum(expo, axis=1, keepdims=True)
        total = dot(expo.astype(jnp.bfloat16), mixed_ref[0, 2, span, :], ((1,), (0,)))
        per = out_ref.shape[1]
        at = block * BLOCK
        out_ref[at // per, at % per : at % per + BLOCK, :] = (total / row_sum).astype(
            jnp.bfloat16
        )
        prob = expo / row_sum
        for n in range(block + 1 - first):
            prob_ref[0, tile + n] = prob[:, n * BLOCK : (n + 1) * BLOCK]


def forward(docs, x, taps, before, members):
    sources, streams, rows, width = x.shape
    per = width // HEAD_DIM
    tokens = sources * rows
    tiles = row_blocks(tokens)[1]
    here = pl.BlockSpec(memory_space=pltpu.VMEM)
    return pl.pallas_call(
        forward_kernel,
        grid_spec=pltpu.PrefetchScalarGridSpec(
            num_scalar_prefetch=1,
            grid=(per,),
            in_specs=[here, here, here],
            out_specs=[
                pl.BlockSpec((1, streams, tokens, HEAD_DIM), lambda h, d: (h, 0, 0, 0)),
                pl.BlockSpec((1, tiles, BLOCK, BLOCK), lambda h, d: (h, 0, 0, 0)),
                pl.BlockSpec((members, tokens // members, HEAD_DIM), lambda h, d: (0, 0, h)),
            ],
            scratch_shapes=[pltpu.VMEM((streams, tokens + PAD, HEAD_DIM), jnp.float32)],
        ),
        out_shape=[
            pltpu.HBM((per, streams, tokens, HEAD_DIM), jnp.bfloat16),
            pltpu.HBM((per, tiles, BLOCK, BLOCK), jnp.float32),
            pltpu.HBM((members, tokens // members, width), jnp.bfloat16),
        ],
        compiler_params=room(FORE),
        cost_estimate=estimate(10_000_000_000, 8 * x.size),
        name="forward",
    )(docs, x, taps, before)


def backward_kernel(
    x_ref, before_ref, mixed_ref, prob_ref, att_ref, up_ref, cgrad_ref, tapg_ref, head_ref
):
    sources, streams, rows, _ = x_ref.shape
    tokens = sources * rows
    per = att_ref.shape[1]
    head = pl.program_id(0)
    lanes = pl.ds(pl.multiple_of(head * HEAD_DIM, HEAD_DIM), HEAD_DIM)
    cgrad = cgrad_ref.at[head]
    cgrad[...] = jnp.zeros(cgrad.shape, jnp.float32)
    for block, first, tile in row_blocks(tokens)[0]:
        own = slice(block * BLOCK, (block + 1) * BLOCK)
        span = slice(first * BLOCK, (block + 1) * BLOCK)
        out = slice(PAD + own.start, PAD + own.stop)
        outs = slice(PAD + span.start, PAD + span.stop)
        query, keys = mixed_ref[0, 0, own, :], mixed_ref[0, 1, span, :]
        at = block * BLOCK
        up = up_ref[at // per, at % per : at % per + BLOCK, lanes]
        att = att_ref[at // per, at % per : at % per + BLOCK, :]
        delta = jnp.sum(up.astype(jnp.float32) * att.astype(jnp.float32), axis=1, keepdims=True)
        tiles = [prob_ref[0, tile + n] for n in range(block + 1 - first)]
        prob = jnp.concatenate(tiles, axis=1) if len(tiles) > 1 else tiles[0]
        dprob = dot(up, mixed_ref[0, 2, span, :], ((1,), (1,)))
        dscore = (prob * (dprob - delta) * SCALE).astype(jnp.bfloat16)
        cgrad[0, out, :] = dot(dscore, keys, ((1,), (0,)))
        cgrad[1, outs, :] += dot(dscore, query, ((0,), (0,)))
        cgrad[2, outs, :] += dot(prob.astype(jnp.bfloat16), up, ((0,), (0,)))
    head_ref[:, :, lanes] = cgrad[:, PAD : 2 * PAD, :]
    span = BLOCK // rows
    for m in range(streams):
        early = before_ref[m, :, lanes].astype(jnp.float32)
        sums = [early * cgrad[m, lag : lag + PAD, :] for lag in range(KW)]
        for start in range(0, tokens, BLOCK):
            at = start // rows
            here = x_ref[at : at + span, m].reshape(BLOCK, HEAD_DIM).astype(jnp.float32)
            for lag in range(KW):
                product = here * cgrad[m, PAD + start + lag : PAD + start + lag + BLOCK, :]
                sums[lag] = sums[lag] + jnp.sum(product.reshape(BLOCK // 8, 8, HEAD_DIM), axis=0)
        for lag in range(KW):
            tapg_ref[m, lag : lag + 1, lanes] = jnp.sum(sums[lag], axis=0, keepdims=True)


def backward(x, before, mixed, prob, att, up):
    sources, streams, rows, width = x.shape
    per = width // HEAD_DIM
    tokens = sources * rows
    members = att.shape[0]
    tiles = prob.shape[1]
    here = pl.BlockSpec(memory_space=pltpu.VMEM)
    return pl.pallas_call(
        backward_kernel,
        grid=(per,),
        in_specs=[
            pl.BlockSpec((sources, streams, rows, HEAD_DIM), lambda h: (0, 0, 0, h)),
            here,
            pl.BlockSpec((1, streams, tokens, HEAD_DIM), lambda h: (h, 0, 0, 0)),
            pl.BlockSpec((1, tiles, BLOCK, BLOCK), lambda h: (h, 0, 0, 0)),
            pl.BlockSpec((members, tokens // members, HEAD_DIM), lambda h: (0, 0, h)),
            here,
        ],
        out_specs=[here, here, here],
        out_shape=[
            jax.ShapeDtypeStruct((per, streams, tokens + 2 * PAD, HEAD_DIM), jnp.float32),
            jax.ShapeDtypeStruct((streams, KW, width), jnp.float32),
            jax.ShapeDtypeStruct((streams, PAD, width), jnp.float32),
        ],
        compiler_params=room(BACK),
        cost_estimate=estimate(20_000_000_000, 12 * x.size),
        name="backward",
    )(x, before, mixed, prob, att, up)


def spread_kernel(cgrad_ref, taps_ref, grad_ref, tail_ref):
    _, streams, rows, _ = grad_ref.shape
    head = pl.program_id(0)
    lanes = pl.ds(pl.multiple_of(head * HEAD_DIM, HEAD_DIM), HEAD_DIM)
    for m in range(streams):
        for start in range(0, cgrad_ref.shape[2] - 2 * PAD, BLOCK):
            total = jnp.zeros((BLOCK, HEAD_DIM), jnp.float32)
            for lag in range(KW):
                at = PAD + start + lag
                total = (
                    total
                    + taps_ref[m, lag : lag + 1, lanes] * cgrad_ref[head, m, at : at + BLOCK, :]
                )
            grad_ref[start // rows : (start + BLOCK) // rows, m] = total.astype(
                jnp.bfloat16
            ).reshape(BLOCK // rows, rows, HEAD_DIM)
        tail_ref[m, :, lanes] = total[BLOCK - PAD :]


def spread(cgrad, taps, rows):
    per, streams, longer, _ = cgrad.shape
    sources, width = (longer - 2 * PAD) // rows, per * HEAD_DIM
    here = pl.BlockSpec(memory_space=pltpu.VMEM)
    return pl.pallas_call(
        spread_kernel,
        grid=(per,),
        in_specs=[here, here],
        out_specs=[
            pl.BlockSpec((sources, streams, rows, HEAD_DIM), lambda h: (0, 0, 0, h)),
            here,
        ],
        out_shape=[
            pltpu.HBM((sources, streams, rows, width), jnp.bfloat16),
            jax.ShapeDtypeStruct((streams, PAD, width), jnp.float32),
        ],
        compiler_params=room(SPREAD),
        cost_estimate=estimate(2_000_000_000, 6 * cgrad.size),
        name="spread",
    )(cgrad, taps)


def swap(value, axes, groups):
    shape = value.shape
    return lax.all_to_all(
        value.reshape(shape[0], -1, shape[-1]),
        axes,
        split_axis=0,
        concat_axis=0,
        axis_index_groups=groups,
        tiled=True,
    ).reshape(shape)


def across(value, step):
    count = lax.axis_size("ctx")
    return lax.ppermute(value, "ctx", [(i, i ^ step) for i in range(count)])


def first_exchange(piece, members):
    if members < lax.axis_size("ctx"):
        return 1, piece + across(piece, members)
    other = across(piece, 1)
    even = lax.axis_index("ctx") % 2 == 0
    return 2, jnp.concatenate(
        [jnp.where(even, piece, other), jnp.where(even, other, piece)], axis=-1
    )


def gather_columns(held, span, members):
    position = lax.axis_index("ctx").astype(jnp.int32)
    streams, taps, wide = held.shape
    steps = range(0, members, span)
    pieces = [across(held, step) if step else held for step in steps]

    def kernel(position_ref, *refs):
        o_ref = refs[-1]
        for step in steps:
            column = lax.rem(position_ref[0] ^ step, members) // span
            o_ref[:, :, pl.ds(pl.multiple_of(column * wide, wide), wide)] = refs[step // span][...]

    columns = members // span * wide
    return pl.pallas_call(
        kernel,
        grid_spec=pltpu.PrefetchScalarGridSpec(
            num_scalar_prefetch=1,
            grid=(1,),
            in_specs=[pl.BlockSpec((streams, taps, wide), lambda i, p: (0, 0, 0))] * len(pieces),
            out_specs=pl.BlockSpec((streams, taps, columns), lambda i, p: (0, 0, 0)),
        ),
        out_shape=jax.ShapeDtypeStruct((streams, taps, columns), held.dtype),
        compiler_params=room(4),
        name="place_columns",
    )(position.reshape(1), *pieces)


def by_heads(parts, qkv, filters, doc_ids, upstream):
    count, tp = lax.axis_size("ctx"), lax.axis_size("tp")
    members = count // parts
    rows, streams, _ = qkv.shape
    width = upstream.shape[1] // members
    position = lax.axis_index("ctx")
    every = everywhere = None
    if parts > 1:
        every = [[p * members + c for c in range(members)] for p in range(parts)]
        everywhere = [[c * tp + t for c in group for t in range(tp)] for group in every]
        blocks = doc_ids.shape[0] // parts
        doc_ids = lax.dynamic_slice_in_dim(doc_ids, position // members * blocks, blocks)
    slabs = split_columns(jnp.transpose(qkv, (1, 0, 2)), members, tp, 60)
    x = swap(slabs.reshape((members * tp,) + slabs.shape[2:]), AXES, everywhere)
    up = swap(split_columns(upstream[None], members, 1, 10)[:, 0, 0], "ctx", every)
    taps = lax.dynamic_slice_in_dim(filters, position % members * width, width, 2)
    if parts > 1:
        upward = [(i, i + members) for i in range(count - members)]
        before = lax.ppermute(x[-1, :, rows - PAD :], "ctx", upward)
    else:
        before = jnp.zeros((streams, PAD, width), x.dtype)
    mixed, prob, att = forward(doc_ids, x, taps, before, members)
    attended = join_columns(swap(att, "ctx", every)[:, None, None])[0]
    away = [pltpu.with_memory_space_constraint(v, pltpu.HBM) for v in (mixed, prob, att)]
    cgrad, tap_grad, head = backward(x, before, *away, up)
    span, held = first_exchange(tap_grad, members)
    grad, tail = spread(cgrad, taps, rows)
    if parts > 1:
        after = lax.ppermute(head, "ctx", [(to, source) for source, to in upward])
        after = jnp.concatenate([jnp.zeros_like(after), after], axis=1)
        for lag in range(KW):
            tail = tail + taps[:, lag : lag + 1] * after[:, lag : lag + PAD]
        grad = grad.at[-1, :, rows - PAD :].set(tail.astype(grad.dtype))
    grad, held = lax.optimization_barrier((grad, held))
    held, attended = lax.optimization_barrier((held, attended))
    filter_grad = gather_columns(held, span, members)
    qkv_grad = join_columns(swap(grad, AXES, everywhere).reshape(slabs.shape))
    return attended, jnp.transpose(qkv_grad, (1, 0, 2)), filter_grad


def from_behind(value, axis, steps):
    count = lax.axis_size(axis)
    first, last = (max(0, -steps), min(count, count - steps))
    return lax.ppermute(value, axis, [(source, source + steps) for source in range(first, last)])


def block_docs(doc_ids, first_block, count):
    start = jnp.maximum(first_block, 0)
    picked = lax.dynamic_slice_in_dim(doc_ids, start, count)
    return jnp.repeat(picked, BLOCK)


def by_ring(qkv, filters, doc_ids, upstream):
    local = lax.all_to_all(qkv, "tp", split_axis=2, concat_axis=0, tiled=True)
    tokens = local.shape[0]
    width = local.shape[2]
    heads = width // HEAD_DIM
    blocks_here = tokens // BLOCK
    logit_scale = HEAD_DIM ** (-0.5)
    position = lax.axis_index("ctx")
    reach = STEPS + 1
    rim = from_behind(local[tokens - (KW - 1) :], "ctx", 1)
    inputs = jnp.concatenate([rim, local], axis=0).astype(jnp.float32)
    mixed = sum(
        (filters[:, lag, :] * inputs[KW - 1 - lag : KW - 1 - lag + tokens] for lag in range(KW))
    )
    mixed = mixed.astype(jnp.bfloat16)
    queries = mixed[:, 0].reshape(tokens, heads, HEAD_DIM)
    key_value = mixed[:, 1:3]
    tiles = [key_value]
    current = key_value
    for distance in range(1, STEPS + 1):
        current = from_behind(current, "ctx", 1)
        tiles.append(current)
    joined = jnp.concatenate(tiles, axis=0)
    keys = joined[:, 0].reshape(reach * tokens, heads, HEAD_DIM)
    values = joined[:, 1].reshape(reach * tokens, heads, HEAD_DIM)
    rows = jnp.arange(tokens)
    query_token = position * tokens + rows
    query_doc = block_docs(doc_ids, position * blocks_here, blocks_here)
    key_tokens = jnp.concatenate(
        [(position - distance) * tokens + rows for distance in range(reach)]
    )
    key_docs = jnp.concatenate(
        [
            block_docs(doc_ids, (position - distance) * blocks_here, blocks_here)
            for distance in range(reach)
        ]
    )
    allowed = (
        (key_tokens[None, :] >= 0)
        & (key_tokens[None, :] <= query_token[:, None])
        & (key_docs[None, :] == query_doc[:, None])
    )
    raw = (
        jnp.einsum("qhd,khd->hqk", queries, keys, preferred_element_type=jnp.float32) * logit_scale
    )
    masked = jnp.where(allowed[None], raw, -1e30)
    row_max = masked.max(axis=2)
    expo = jnp.where(allowed[None], jnp.exp(masked - row_max[:, :, None]), 0.0)
    row_sum = expo.sum(axis=2)
    weighted_values = jnp.einsum(
        "hqk,khd->qhd", expo.astype(jnp.bfloat16), values, preferred_element_type=jnp.float32
    )
    attended = (weighted_values / row_sum.T[:, :, None]).astype(jnp.bfloat16)
    grad_out = upstream.reshape(tokens, heads, HEAD_DIM)
    delta = jnp.sum(grad_out.astype(jnp.float32) * attended.astype(jnp.float32), axis=-1).T
    prob = expo / row_sum[:, :, None]
    value_part = jnp.einsum(
        "hqk,qhd->khd", prob.astype(jnp.bfloat16), grad_out, preferred_element_type=jnp.float32
    )
    probability_gradient = jnp.einsum(
        "qhd,khd->hqk", grad_out, values, preferred_element_type=jnp.float32
    )
    score_gradient = (prob * (probability_gradient - delta[:, :, None]) * logit_scale).astype(
        jnp.bfloat16
    )
    query_gradient_rows = jnp.einsum(
        "hqk,khd->qhd", score_gradient, keys, preferred_element_type=jnp.float32
    )
    key_part = jnp.einsum(
        "hqk,qhd->khd", score_gradient, queries, preferred_element_type=jnp.float32
    )
    stacked = jnp.stack(
        [key_part.reshape(reach, tokens, width), value_part.reshape(reach, tokens, width)], axis=2
    )
    partials = [stacked[distance] for distance in range(reach)]
    carried = partials[STEPS]
    for distance in range(STEPS - 1, -1, -1):
        carried = from_behind(carried, "ctx", -1)
        carried = carried + partials[distance]
    conv_grad = jnp.concatenate([query_gradient_rows.reshape(tokens, 1, width), carried], axis=1)
    grad_edge = from_behind(conv_grad[: KW - 1], "ctx", -1)
    extended = jnp.concatenate([conv_grad, grad_edge], axis=0)
    input_grad = sum((filters[:, lag, :] * extended[lag : lag + tokens] for lag in range(KW)))
    tap_terms = jnp.stack(
        [
            jnp.sum(inputs[KW - 1 - lag : KW - 1 - lag + tokens] * conv_grad, axis=0)
            for lag in range(KW)
        ],
        axis=1,
    )
    filter_grad = lax.psum(tap_terms, "ctx")
    qkv_grad = lax.all_to_all(
        input_grad.astype(jnp.bfloat16), "tp", split_axis=0, concat_axis=2, tiled=True
    )
    return (attended.reshape(tokens, width), qkv_grad, filter_grad)


def solution(mesh):
    count = mesh.shape["ctx"]

    def shards(qkv, filters, doc_ids, upstream):
        tokens, width = upstream.shape
        heads = width // HEAD_DIM
        args = (qkv, filters, doc_ids, upstream)
        even = tokens % BLOCK == 0 and qkv.shape[0] % PAD == 0 and count & (count - 1) == 0
        if heads % count or not even or count < 4:
            return by_ring(*args)
        middle = doc_ids.shape[0] // 2
        apart = doc_ids[middle - 1] != doc_ids[middle]
        return lax.cond(
            apart, functools.partial(by_heads, 2), functools.partial(by_heads, 1), *args
        )

    return jax.shard_map(
        shards,
        mesh=mesh,
        in_specs=(P(("ctx", "tp"), None, None), P(None, None, "tp"), P(), P("ctx", "tp")),
        out_specs=(P("ctx", "tp"), P(("ctx", "tp"), None, None), P(None, None, "tp")),
        check_vma=False,
    )
```

```python
import functools

import jax
import jax.numpy as jnp
from jax import lax
from jax.experimental import pallas as pl
from jax.experimental.pallas import tpu as pltpu
from jax.sharding import PartitionSpec as P

HEAD_DIM = 128
KW = 7
BLOCK = 128
STEPS = 4
PAD = 8
SCALE = HEAD_DIM ** (-0.5)
AXES = ("ctx", "tp")
FORE, BACK, SPREAD = 24, 24, 16


def dot(a, b, dims):
    return lax.dot_general(a, b, (dims, ((), ())), preferred_element_type=jnp.float32)


def room(mebibytes):
    return pltpu.CompilerParams(vmem_limit_bytes=mebibytes << 20)


def estimate(flops, moved):
    return pl.CostEstimate(flops=flops, bytes_accessed=moved, transcendentals=0)


def split_columns(x, members, tp, mebibytes):
    streams, rows, channels = x.shape
    width = channels // tp // members
    steps = 2 if tp % 2 == 0 else 1
    part = tp // steps

    def kernel(x_ref, o_ref):
        for t in range(part):
            for c in range(members):
                at = (t * members + c) * width
                o_ref[c, t] = x_ref[:, :, at : at + width]

    return pl.pallas_call(
        kernel,
        grid=(steps,),
        in_specs=[pl.BlockSpec((streams, rows, part * members * width), lambda i: (0, 0, i))],
        out_specs=pl.BlockSpec((members, part, streams, rows, width), lambda i: (0, i, 0, 0, 0)),
        out_shape=jax.ShapeDtypeStruct((members, tp, streams, rows, width), x.dtype),
        cost_estimate=estimate(0, 4 * x.size),
        compiler_params=room(mebibytes),
        name="split_columns",
    )(x)


def split_rows(x, members, local):
    tokens, channels = x.shape
    width = channels // members

    def kernel(local_ref, x_ref, *o_refs):
        for step in range(members):
            at = pl.multiple_of((local_ref[0] ^ step) * width, width)
            o_refs[step][...] = x_ref[:, pl.ds(at, width)]

    piece = pl.BlockSpec((tokens, width), lambda i, p: (0, 0))
    return pl.pallas_call(
        kernel,
        grid_spec=pltpu.PrefetchScalarGridSpec(
            num_scalar_prefetch=1,
            grid=(1,),
            in_specs=[pl.BlockSpec((tokens, channels), lambda i, p: (0, 0))],
            out_specs=[piece] * members,
        ),
        out_shape=[jax.ShapeDtypeStruct((tokens, width), x.dtype)] * members,
        compiler_params=room(10),
        cost_estimate=estimate(0, 4 * x.size),
        name="split_rows",
    )(local, x)


def join_columns(x):
    members, tp, streams, rows, width = x.shape
    steps = 2 if tp % 2 == 0 else 1
    part = tp // steps

    def kernel(x_ref, o_ref):
        for t in range(part):
            for c in range(members):
                at = (t * members + c) * width
                o_ref[:, :, at : at + width] = x_ref[c, pl.program_id(0) * part + t]

    return pl.pallas_call(
        kernel,
        grid=(steps,),
        in_specs=[pl.BlockSpec(memory_space=pltpu.VMEM)],
        out_specs=pl.BlockSpec((streams, rows, part * members * width), lambda i: (0, 0, i)),
        out_shape=jax.ShapeDtypeStruct((streams, rows, tp * members * width), x.dtype),
        cost_estimate=estimate(0, 4 * x.size),
        compiler_params=room(10),
        name="join_columns",
    )(x)


def row_blocks(tokens):
    spans, start = [], 0
    for block in range(tokens // BLOCK):
        first = max(0, block - STEPS)
        spans.append((block, first, start))
        start += block + 1 - first
    return spans, start


def forward_kernel(docs, x_ref, taps_ref, before_ref, mixed_ref, prob_ref, out_ref, padded):
    sources, streams, rows, _ = x_ref.shape
    tokens = sources * rows
    head = pl.program_id(0)
    lanes = pl.ds(pl.multiple_of(head * HEAD_DIM, HEAD_DIM), HEAD_DIM)
    padded[:, 0:PAD, :] = before_ref[:, :, lanes].astype(jnp.float32)
    for m in range(streams):
        padded[m, PAD:, :] = x_ref[:, m, :, lanes].reshape(tokens, HEAD_DIM).astype(jnp.float32)
    for m in range(streams):
        for start in range(0, tokens, BLOCK):
            total = jnp.zeros((BLOCK, HEAD_DIM), jnp.float32)
            for lag in range(KW):
                at = PAD + start - lag
                total = total + taps_ref[m, lag : lag + 1, lanes] * padded[m, at : at + BLOCK, :]
            mixed_ref[0, m, start : start + BLOCK, :] = total.astype(jnp.bfloat16)
    below = lax.broadcasted_iota(jnp.int32, (BLOCK, BLOCK), 0) >= lax.broadcasted_iota(
        jnp.int32, (BLOCK, BLOCK), 1
    )
    for block, first, tile in row_blocks(tokens)[0]:
        own = slice(block * BLOCK, (block + 1) * BLOCK)
        span = slice(first * BLOCK, (block + 1) * BLOCK)
        raw = dot(mixed_ref[0, 0, own, :], mixed_ref[0, 1, span, :], ((1,), (1,))) * SCALE
        parts = []
        for other in range(first, block + 1):
            part = raw[:, (other - first) * BLOCK : (other - first + 1) * BLOCK]
            allowed = below if other == block else docs[other] == docs[block]
            parts.append(jnp.where(allowed, part, -1e30))
        masked = jnp.concatenate(parts, axis=1) if len(parts) > 1 else parts[0]
        expo = jnp.exp(masked - jnp.max(masked, axis=1, keepdims=True))
        row_sum = jnp.sum(expo, axis=1, keepdims=True)
        total = dot(expo.astype(jnp.bfloat16), mixed_ref[0, 2, span, :], ((1,), (0,)))
        per = out_ref.shape[1]
        at = block * BLOCK
        out_ref[at // per, at % per : at % per + BLOCK, :] = (total / row_sum).astype(
            jnp.bfloat16
        )
        prob = expo / row_sum
        for n in range(block + 1 - first):
            prob_ref[0, tile + n] = prob[:, n * BLOCK : (n + 1) * BLOCK]


def forward(docs, x, taps, before, members):
    sources, streams, rows, width = x.shape
    per = width // HEAD_DIM
    tokens = sources * rows
    tiles = row_blocks(tokens)[1]
    here = pl.BlockSpec(memory_space=pltpu.VMEM)
    return pl.pallas_call(
        forward_kernel,
        grid_spec=pltpu.PrefetchScalarGridSpec(
            num_scalar_prefetch=1,
            grid=(per,),
            in_specs=[here, here, here],
            out_specs=[
                pl.BlockSpec((1, streams, tokens, HEAD_DIM), lambda h, d: (h, 0, 0, 0)),
                pl.BlockSpec((1, tiles, BLOCK, BLOCK), lambda h, d: (h, 0, 0, 0)),
                pl.BlockSpec((members, tokens // members, HEAD_DIM), lambda h, d: (0, 0, h)),
            ],
            scratch_shapes=[pltpu.VMEM((streams, tokens + PAD, HEAD_DIM), jnp.float32)],
        ),
        out_shape=[
            pltpu.HBM((per, streams, tokens, HEAD_DIM), jnp.bfloat16),
            pltpu.HBM((per, tiles, BLOCK, BLOCK), jnp.float32),
            pltpu.HBM((members, tokens // members, width), jnp.bfloat16),
        ],
        compiler_params=room(FORE),
        cost_estimate=estimate(10_000_000_000, 8 * x.size),
        name="forward",
    )(docs, x, taps, before)


def backward_kernel(
    local, x_ref, before_ref, mixed_ref, prob_ref, att_ref, *refs
):
    *up_refs, cgrad_ref, tapg_ref, head_ref, up_ref = refs
    sources, streams, rows, _ = x_ref.shape
    tokens = sources * rows
    per = att_ref.shape[1]
    head = pl.program_id(0)

    @pl.when(head == 0)
    def _():
        for step, piece_ref in enumerate(up_refs):
            up_ref[local[0] ^ step] = piece_ref[...]

    lanes = pl.ds(pl.multiple_of(head * HEAD_DIM, HEAD_DIM), HEAD_DIM)
    cgrad = cgrad_ref.at[head]
    cgrad[...] = jnp.zeros(cgrad.shape, jnp.float32)
    for block, first, tile in row_blocks(tokens)[0]:
        own = slice(block * BLOCK, (block + 1) * BLOCK)
        span = slice(first * BLOCK, (block + 1) * BLOCK)
        out = slice(PAD + own.start, PAD + own.stop)
        outs = slice(PAD + span.start, PAD + span.stop)
        query, keys = mixed_ref[0, 0, own, :], mixed_ref[0, 1, span, :]
        at = block * BLOCK
        up = up_ref[at // per, at % per : at % per + BLOCK, lanes]
        att = att_ref[at // per, at % per : at % per + BLOCK, :]
        delta = jnp.sum(up.astype(jnp.float32) * att.astype(jnp.float32), axis=1, keepdims=True)
        tiles = [prob_ref[0, tile + n] for n in range(block + 1 - first)]
        prob = jnp.concatenate(tiles, axis=1) if len(tiles) > 1 else tiles[0]
        dprob = dot(up, mixed_ref[0, 2, span, :], ((1,), (1,)))
        dscore = (prob * (dprob - delta) * SCALE).astype(jnp.bfloat16)
        cgrad[0, out, :] = dot(dscore, keys, ((1,), (0,)))
        cgrad[1, outs, :] += dot(dscore, query, ((0,), (0,)))
        cgrad[2, outs, :] += dot(prob.astype(jnp.bfloat16), up, ((0,), (0,)))
    head_ref[:, :, lanes] = cgrad[:, PAD : 2 * PAD, :]
    span = BLOCK // rows
    for m in range(streams):
        early = before_ref[m, :, lanes].astype(jnp.float32)
        sums = [early * cgrad[m, lag : lag + PAD, :] for lag in range(KW)]
        for start in range(0, tokens, BLOCK):
            at = start // rows
            here = x_ref[at : at + span, m].reshape(BLOCK, HEAD_DIM).astype(jnp.float32)
            for lag in range(KW):
                product = here * cgrad[m, PAD + start + lag : PAD + start + lag + BLOCK, :]
                sums[lag] = sums[lag] + jnp.sum(product.reshape(BLOCK // 8, 8, HEAD_DIM), axis=0)
        for lag in range(KW):
            tapg_ref[m, lag : lag + 1, lanes] = jnp.sum(sums[lag], axis=0, keepdims=True)


def backward(local, x, before, mixed, prob, att, pieces):
    sources, streams, rows, width = x.shape
    per = width // HEAD_DIM
    tokens = sources * rows
    members = att.shape[0]
    tiles = prob.shape[1]
    here = pl.BlockSpec(memory_space=pltpu.VMEM)
    return pl.pallas_call(
        backward_kernel,
        grid_spec=pltpu.PrefetchScalarGridSpec(
            num_scalar_prefetch=1,
            grid=(per,),
            in_specs=[
                pl.BlockSpec((sources, streams, rows, HEAD_DIM), lambda h, p: (0, 0, 0, h)),
                here,
                pl.BlockSpec((1, streams, tokens, HEAD_DIM), lambda h, p: (h, 0, 0, 0)),
                pl.BlockSpec((1, tiles, BLOCK, BLOCK), lambda h, p: (h, 0, 0, 0)),
                pl.BlockSpec((members, tokens // members, HEAD_DIM), lambda h, p: (0, 0, h)),
            ]
            + [here] * members,
            out_specs=[here, here, here],
            scratch_shapes=[pltpu.VMEM((members, tokens // members, width), jnp.bfloat16)],
        ),
        out_shape=[
            jax.ShapeDtypeStruct((per, streams, tokens + 2 * PAD, HEAD_DIM), jnp.float32),
            jax.ShapeDtypeStruct((streams, KW, width), jnp.float32),
            jax.ShapeDtypeStruct((streams, PAD, width), jnp.float32),
        ],
        compiler_params=room(BACK),
        cost_estimate=estimate(20_000_000_000, 12 * x.size),
        name="backward",
    )(local, x, before, mixed, prob, att, *pieces)


def spread_kernel(cgrad_ref, taps_ref, grad_ref, tail_ref):
    _, streams, rows, _ = grad_ref.shape
    head = pl.program_id(0)
    lanes = pl.ds(pl.multiple_of(head * HEAD_DIM, HEAD_DIM), HEAD_DIM)
    for m in range(streams):
        for start in range(0, cgrad_ref.shape[2] - 2 * PAD, BLOCK):
            total = jnp.zeros((BLOCK, HEAD_DIM), jnp.float32)
            for lag in range(KW):
                at = PAD + start + lag
                total = (
                    total
                    + taps_ref[m, lag : lag + 1, lanes] * cgrad_ref[head, m, at : at + BLOCK, :]
                )
            grad_ref[start // rows : (start + BLOCK) // rows, m] = total.astype(
                jnp.bfloat16
            ).reshape(BLOCK // rows, rows, HEAD_DIM)
        tail_ref[m, :, lanes] = total[BLOCK - PAD :]


def spread(cgrad, taps, rows):
    per, streams, longer, _ = cgrad.shape
    sources, width = (longer - 2 * PAD) // rows, per * HEAD_DIM
    here = pl.BlockSpec(memory_space=pltpu.VMEM)
    return pl.pallas_call(
        spread_kernel,
        grid=(per,),
        in_specs=[here, here],
        out_specs=[
            pl.BlockSpec((sources, streams, rows, HEAD_DIM), lambda h: (0, 0, 0, h)),
            here,
        ],
        out_shape=[
            pltpu.HBM((sources, streams, rows, width), jnp.bfloat16),
            jax.ShapeDtypeStruct((streams, PAD, width), jnp.float32),
        ],
        compiler_params=room(SPREAD),
        cost_estimate=estimate(2_000_000_000, 6 * cgrad.size),
        name="spread",
    )(cgrad, taps)


def swap(value, axes, groups):
    shape = value.shape
    return lax.all_to_all(
        value.reshape(shape[0], -1, shape[-1]),
        axes,
        split_axis=0,
        concat_axis=0,
        axis_index_groups=groups,
        tiled=True,
    ).reshape(shape)


def across(value, step):
    count = lax.axis_size("ctx")
    return lax.ppermute(value, "ctx", [(i, i ^ step) for i in range(count)])


def first_exchange(piece, members):
    if members < lax.axis_size("ctx"):
        return 1, piece + across(piece, members)
    other = across(piece, 1)
    even = lax.axis_index("ctx") % 2 == 0
    return 2, jnp.concatenate(
        [jnp.where(even, piece, other), jnp.where(even, other, piece)], axis=-1
    )


def gather_columns(held, span, members):
    position = lax.axis_index("ctx").astype(jnp.int32)
    streams, taps, wide = held.shape
    steps = range(0, members, span)
    pieces = [across(held, step) if step else held for step in steps]

    def kernel(position_ref, *refs):
        o_ref = refs[-1]
        for step in steps:
            column = lax.rem(position_ref[0] ^ step, members) // span
            o_ref[:, :, pl.ds(pl.multiple_of(column * wide, wide), wide)] = refs[step // span][...]

    columns = members // span * wide
    return pl.pallas_call(
        kernel,
        grid_spec=pltpu.PrefetchScalarGridSpec(
            num_scalar_prefetch=1,
            grid=(1,),
            in_specs=[pl.BlockSpec((streams, taps, wide), lambda i, p: (0, 0, 0))] * len(pieces),
            out_specs=pl.BlockSpec((streams, taps, columns), lambda i, p: (0, 0, 0)),
        ),
        out_shape=jax.ShapeDtypeStruct((streams, taps, columns), held.dtype),
        compiler_params=room(4),
        name="place_columns",
    )(position.reshape(1), *pieces)


def by_heads(parts, qkv, filters, doc_ids, upstream):
    count, tp = lax.axis_size("ctx"), lax.axis_size("tp")
    members = count // parts
    rows, streams, _ = qkv.shape
    width = upstream.shape[1] // members
    position = lax.axis_index("ctx")
    every = everywhere = None
    if parts > 1:
        every = [[p * members + c for c in range(members)] for p in range(parts)]
        everywhere = [[c * tp + t for c in group for t in range(tp)] for group in every]
        blocks = doc_ids.shape[0] // parts
        doc_ids = lax.dynamic_slice_in_dim(doc_ids, position // members * blocks, blocks)
    slabs = split_columns(jnp.transpose(qkv, (1, 0, 2)), members, tp, 60)
    x = swap(slabs.reshape((members * tp,) + slabs.shape[2:]), AXES, everywhere)
    local = (position % members).astype(jnp.int32).reshape(1)
    pieces = split_rows(upstream, members, local)
    pieces = [across(piece, step) if step else piece for step, piece in enumerate(pieces)]
    taps = lax.dynamic_slice_in_dim(filters, position % members * width, width, 2)
    if parts > 1:
        upward = [(i, i + members) for i in range(count - members)]
        before = lax.ppermute(x[-1, :, rows - PAD :], "ctx", upward)
    else:
        before = jnp.zeros((streams, PAD, width), x.dtype)
    mixed, prob, att = forward(doc_ids, x, taps, before, members)
    attended = join_columns(swap(att, "ctx", every)[:, None, None])[0]
    away = [pltpu.with_memory_space_constraint(v, pltpu.HBM) for v in (mixed, prob, att)]
    cgrad, tap_grad, head = backward(local, x, before, *away, pieces)
    span, held = first_exchange(tap_grad, members)
    grad, tail = spread(cgrad, taps, rows)
    if parts > 1:
        after = lax.ppermute(head, "ctx", [(to, source) for source, to in upward])
        after = jnp.concatenate([jnp.zeros_like(after), after], axis=1)
        for lag in range(KW):
            tail = tail + taps[:, lag : lag + 1] * after[:, lag : lag + PAD]
        grad = grad.at[-1, :, rows - PAD :].set(tail.astype(grad.dtype))
    grad, held = lax.optimization_barrier((grad, held))
    held, attended = lax.optimization_barrier((held, attended))
    filter_grad = gather_columns(held, span, members)
    qkv_grad = join_columns(swap(grad, AXES, everywhere).reshape(slabs.shape))
    return attended, jnp.transpose(qkv_grad, (1, 0, 2)), filter_grad


def from_behind(value, axis, steps):
    count = lax.axis_size(axis)
    first, last = (max(0, -steps), min(count, count - steps))
    return lax.ppermute(value, axis, [(source, source + steps) for source in range(first, last)])


def block_docs(doc_ids, first_block, count):
    start = jnp.maximum(first_block, 0)
    picked = lax.dynamic_slice_in_dim(doc_ids, start, count)
    return jnp.repeat(picked, BLOCK)


def by_ring(qkv, filters, doc_ids, upstream):
    local = lax.all_to_all(qkv, "tp", split_axis=2, concat_axis=0, tiled=True)
    tokens = local.shape[0]
    width = local.shape[2]
    heads = width // HEAD_DIM
    blocks_here = tokens // BLOCK
    logit_scale = HEAD_DIM ** (-0.5)
    position = lax.axis_index("ctx")
    reach = STEPS + 1
    rim = from_behind(local[tokens - (KW - 1) :], "ctx", 1)
    inputs = jnp.concatenate([rim, local], axis=0).astype(jnp.float32)
    mixed = sum(
        (filters[:, lag, :] * inputs[KW - 1 - lag : KW - 1 - lag + tokens] for lag in range(KW))
    )
    mixed = mixed.astype(jnp.bfloat16)
    queries = mixed[:, 0].reshape(tokens, heads, HEAD_DIM)
    key_value = mixed[:, 1:3]
    tiles = [key_value]
    current = key_value
    for distance in range(1, STEPS + 1):
        current = from_behind(current, "ctx", 1)
        tiles.append(current)
    joined = jnp.concatenate(tiles, axis=0)
    keys = joined[:, 0].reshape(reach * tokens, heads, HEAD_DIM)
    values = joined[:, 1].reshape(reach * tokens, heads, HEAD_DIM)
    rows = jnp.arange(tokens)
    query_token = position * tokens + rows
    query_doc = block_docs(doc_ids, position * blocks_here, blocks_here)
    key_tokens = jnp.concatenate(
        [(position - distance) * tokens + rows for distance in range(reach)]
    )
    key_docs = jnp.concatenate(
        [
            block_docs(doc_ids, (position - distance) * blocks_here, blocks_here)
            for distance in range(reach)
        ]
    )
    allowed = (
        (key_tokens[None, :] >= 0)
        & (key_tokens[None, :] <= query_token[:, None])
        & (key_docs[None, :] == query_doc[:, None])
    )
    raw = (
        jnp.einsum("qhd,khd->hqk", queries, keys, preferred_element_type=jnp.float32) * logit_scale
    )
    masked = jnp.where(allowed[None], raw, -1e30)
    row_max = masked.max(axis=2)
    expo = jnp.where(allowed[None], jnp.exp(masked - row_max[:, :, None]), 0.0)
    row_sum = expo.sum(axis=2)
    weighted_values = jnp.einsum(
        "hqk,khd->qhd", expo.astype(jnp.bfloat16), values, preferred_element_type=jnp.float32
    )
    attended = (weighted_values / row_sum.T[:, :, None]).astype(jnp.bfloat16)
    grad_out = upstream.reshape(tokens, heads, HEAD_DIM)
    delta = jnp.sum(grad_out.astype(jnp.float32) * attended.astype(jnp.float32), axis=-1).T
    prob = expo / row_sum[:, :, None]
    value_part = jnp.einsum(
        "hqk,qhd->khd", prob.astype(jnp.bfloat16), grad_out, preferred_element_type=jnp.float32
    )
    probability_gradient = jnp.einsum(
        "qhd,khd->hqk", grad_out, values, preferred_element_type=jnp.float32
    )
    score_gradient = (prob * (probability_gradient - delta[:, :, None]) * logit_scale).astype(
        jnp.bfloat16
    )
    query_gradient_rows = jnp.einsum(
        "hqk,khd->qhd", score_gradient, keys, preferred_element_type=jnp.float32
    )
    key_part = jnp.einsum(
        "hqk,qhd->khd", score_gradient, queries, preferred_element_type=jnp.float32
    )
    stacked = jnp.stack(
        [key_part.reshape(reach, tokens, width), value_part.reshape(reach, tokens, width)], axis=2
    )
    partials = [stacked[distance] for distance in range(reach)]
    carried = partials[STEPS]
    for distance in range(STEPS - 1, -1, -1):
        carried = from_behind(carried, "ctx", -1)
        carried = carried + partials[distance]
    conv_grad = jnp.concatenate([query_gradient_rows.reshape(tokens, 1, width), carried], axis=1)
    grad_edge = from_behind(conv_grad[: KW - 1], "ctx", -1)
    extended = jnp.concatenate([conv_grad, grad_edge], axis=0)
    input_grad = sum((filters[:, lag, :] * extended[lag : lag + tokens] for lag in range(KW)))
    tap_terms = jnp.stack(
        [
            jnp.sum(inputs[KW - 1 - lag : KW - 1 - lag + tokens] * conv_grad, axis=0)
            for lag in range(KW)
        ],
        axis=1,
    )
    filter_grad = lax.psum(tap_terms, "ctx")
    qkv_grad = lax.all_to_all(
        input_grad.astype(jnp.bfloat16), "tp", split_axis=0, concat_axis=2, tiled=True
    )
    return (attended.reshape(tokens, width), qkv_grad, filter_grad)


def solution(mesh):
    count = mesh.shape["ctx"]

    def shards(qkv, filters, doc_ids, upstream):
        tokens, width = upstream.shape
        heads = width // HEAD_DIM
        args = (qkv, filters, doc_ids, upstream)
        even = tokens % BLOCK == 0 and qkv.shape[0] % PAD == 0 and count & (count - 1) == 0
        if heads % count or not even or count < 4:
            return by_ring(*args)
        middle = doc_ids.shape[0] // 2
        apart = doc_ids[middle - 1] != doc_ids[middle]
        return lax.cond(
            apart, functools.partial(by_heads, 2), functools.partial(by_heads, 1), *args
        )

    return jax.shard_map(
        shards,
        mesh=mesh,
        in_specs=(P(("ctx", "tp"), None, None), P(None, None, "tp"), P(), P("ctx", "tp")),
        out_specs=(P("ctx", "tp"), P(("ctx", "tp"), None, None), P(None, None, "tp")),
        check_vma=False,
    )
```

```python
import functools
import math

import jax
import jax.numpy as jnp
from jax import lax
from jax.experimental import pallas as pl
from jax.experimental.pallas import tpu as pltpu
from jax.sharding import PartitionSpec as P

HEAD_DIM = 128
KW = 7
BLOCK = 128
STEPS = 4
PAD = 8
SCALE = HEAD_DIM ** (-0.5)
SCALE_LOG2 = SCALE * math.log2(math.e)
AXES = ("ctx", "tp")
FORE, BACK, SPREAD = 24, 24, 16


def dot(a, b, dims):
    return lax.dot_general(a, b, (dims, ((), ())), preferred_element_type=jnp.float32)


def room(mebibytes):
    return pltpu.CompilerParams(vmem_limit_bytes=mebibytes << 20)


def estimate(flops, moved):
    return pl.CostEstimate(flops=flops, bytes_accessed=moved, transcendentals=0)


def split_columns(x, members, tp, mebibytes):
    streams, rows, channels = x.shape
    width = channels // tp // members
    steps = 2 if tp % 2 == 0 else 1
    part = tp // steps

    def kernel(x_ref, o_ref):
        for t in range(part):
            for c in range(members):
                at = (t * members + c) * width
                o_ref[c, t] = x_ref[:, :, at : at + width]

    return pl.pallas_call(
        kernel,
        grid=(steps,),
        in_specs=[pl.BlockSpec((streams, rows, part * members * width), lambda i: (0, 0, i))],
        out_specs=pl.BlockSpec((members, part, streams, rows, width), lambda i: (0, i, 0, 0, 0)),
        out_shape=jax.ShapeDtypeStruct((members, tp, streams, rows, width), x.dtype),
        cost_estimate=estimate(0, 4 * x.size),
        compiler_params=room(mebibytes),
        name="split_columns",
    )(x)


def split_rows(x, members, local):
    tokens, channels = x.shape
    width = channels // members

    def kernel(local_ref, x_ref, *o_refs):
        for step in range(members):
            at = pl.multiple_of((local_ref[0] ^ step) * width, width)
            o_refs[step][...] = x_ref[:, pl.ds(at, width)]

    piece = pl.BlockSpec((tokens, width), lambda i, p: (0, 0))
    return pl.pallas_call(
        kernel,
        grid_spec=pltpu.PrefetchScalarGridSpec(
            num_scalar_prefetch=1,
            grid=(1,),
            in_specs=[pl.BlockSpec((tokens, channels), lambda i, p: (0, 0))],
            out_specs=[piece] * members,
        ),
        out_shape=[jax.ShapeDtypeStruct((tokens, width), x.dtype)] * members,
        compiler_params=room(10),
        cost_estimate=estimate(0, 4 * x.size),
        name="split_rows",
    )(local, x)


def join_columns(x):
    members, tp, streams, rows, width = x.shape
    steps = 2 if tp % 2 == 0 else 1
    part = tp // steps

    def kernel(x_ref, o_ref):
        for t in range(part):
            for c in range(members):
                at = (t * members + c) * width
                o_ref[:, :, at : at + width] = x_ref[c, pl.program_id(0) * part + t]

    return pl.pallas_call(
        kernel,
        grid=(steps,),
        in_specs=[pl.BlockSpec(memory_space=pltpu.VMEM)],
        out_specs=pl.BlockSpec((streams, rows, part * members * width), lambda i: (0, 0, i)),
        out_shape=pltpu.HBM((streams, rows, tp * members * width), x.dtype),
        cost_estimate=estimate(0, 4 * x.size),
        compiler_params=room(10),
        name="join_columns",
    )(x)


def tile_starts(tokens):
    starts, total = [], 0
    for block in range(tokens // BLOCK):
        starts.append(total)
        total += block + 1 - max(0, block - STEPS)
    return starts, total


def row_groups(tokens):
    blocks = tokens // BLOCK
    size = 2 if blocks % 2 == 0 else 1
    for start in range(0, blocks, size):
        yield range(start, start + size), max(0, start - STEPS)


def widened(value, block, group, first):
    before = (max(0, block - STEPS) - first) * BLOCK
    behind = (group[-1] - block) * BLOCK
    parts = [jnp.zeros((BLOCK, before), value.dtype)] if before else []
    parts.append(value)
    if behind:
        parts.append(jnp.zeros((BLOCK, behind), value.dtype))
    return jnp.concatenate(parts, axis=1) if len(parts) > 1 else value


def stacked(parts):
    return jnp.concatenate(parts, axis=0) if len(parts) > 1 else parts[0]


def forward_kernel(docs, x_ref, taps_ref, before_ref, mixed_ref, prob_ref, out_ref, padded):
    sources, streams, rows, _ = x_ref.shape
    tokens = sources * rows
    head = pl.program_id(0)
    lanes = pl.ds(pl.multiple_of(head * HEAD_DIM, HEAD_DIM), HEAD_DIM)
    padded[:, 0:PAD, :] = before_ref[:, :, lanes].astype(jnp.float32)
    for m in range(streams):
        padded[m, PAD:, :] = x_ref[:, m, :, lanes].reshape(tokens, HEAD_DIM).astype(jnp.float32)
    for m in range(streams):
        for start in range(0, tokens, BLOCK):
            total = None
            for lag in range(KW):
                at = PAD + start - lag
                term = taps_ref[m, lag : lag + 1, lanes] * padded[m, at : at + BLOCK, :]
                total = term if total is None else total + term
            mixed_ref[0, m, start : start + BLOCK, :] = total.astype(jnp.bfloat16)
    below = lax.broadcasted_iota(jnp.int32, (BLOCK, BLOCK), 0) >= lax.broadcasted_iota(
        jnp.int32, (BLOCK, BLOCK), 1
    )
    starts = tile_starts(tokens)[0]
    for group, first in row_groups(tokens):
        own = slice(group[0] * BLOCK, (group[-1] + 1) * BLOCK)
        span = slice(first * BLOCK, own.stop)
        raw = dot(mixed_ref[0, 0, own, :], mixed_ref[0, 1, span, :], ((1,), (1,)))
        sheets, inverses = [], []
        for block in group:
            lowest = max(0, block - STEPS)
            mine = raw[(block - group[0]) * BLOCK : (block - group[0] + 1) * BLOCK]
            parts = []
            for other in range(lowest, block + 1):
                part = mine[:, (other - first) * BLOCK : (other - first + 1) * BLOCK]
                allowed = below if other == block else docs[other] == docs[block]
                parts.append(jnp.where(allowed, part, -1e30))
            masked = jnp.concatenate(parts, axis=1) if len(parts) > 1 else parts[0]
            expo = jnp.exp2((masked - jnp.max(masked, axis=1, keepdims=True)) * SCALE_LOG2)
            inverses.append(1.0 / jnp.sum(expo, axis=1, keepdims=True))
            sheets.append(widened(expo.astype(jnp.bfloat16), block, group, first))
            prob = expo * inverses[-1]
            for n in range(block + 1 - lowest):
                prob_ref[0, starts[block] + n] = prob[:, n * BLOCK : (n + 1) * BLOCK]
        total = dot(stacked(sheets), mixed_ref[0, 2, span, :], ((1,), (0,)))
        per = out_ref.shape[1]
        for n, block in enumerate(group):
            at = block * BLOCK
            out_ref[at // per, at % per : at % per + BLOCK, :] = (
                total[n * BLOCK : (n + 1) * BLOCK] * inverses[n]
            ).astype(jnp.bfloat16)


def forward(docs, x, taps, before, members):
    sources, streams, rows, width = x.shape
    per = width // HEAD_DIM
    tokens = sources * rows
    tiles = tile_starts(tokens)[1]
    here = pl.BlockSpec(memory_space=pltpu.VMEM)
    return pl.pallas_call(
        forward_kernel,
        grid_spec=pltpu.PrefetchScalarGridSpec(
            num_scalar_prefetch=1,
            grid=(per,),
            in_specs=[here, here, here],
            out_specs=[
                pl.BlockSpec((1, streams, tokens, HEAD_DIM), lambda h, d: (h, 0, 0, 0)),
                pl.BlockSpec((1, tiles, BLOCK, BLOCK), lambda h, d: (h, 0, 0, 0)),
                pl.BlockSpec((members, tokens // members, HEAD_DIM), lambda h, d: (0, 0, h)),
            ],
            scratch_shapes=[pltpu.VMEM((streams, tokens + PAD, HEAD_DIM), jnp.float32)],
        ),
        out_shape=[
            pltpu.HBM((per, streams, tokens, HEAD_DIM), jnp.bfloat16),
            pltpu.HBM((per, tiles, BLOCK, BLOCK), jnp.float32),
            pltpu.HBM((members, tokens // members, width), jnp.bfloat16),
        ],
        compiler_params=room(FORE),
        cost_estimate=estimate(10_000_000_000, 8 * x.size),
        name="forward",
    )(docs, x, taps, before)


def backward_kernel(
    local, x_ref, before_ref, mixed_ref, prob_ref, att_ref, *refs
):
    *up_refs, cgrad_ref, tapg_ref, head_ref, up_ref = refs
    sources, streams, rows, _ = x_ref.shape
    tokens = sources * rows
    per = att_ref.shape[1]
    head = pl.program_id(0)

    @pl.when(head == 0)
    def _():
        for step, piece_ref in enumerate(up_refs):
            up_ref[local[0] ^ step] = piece_ref[...]

    lanes = pl.ds(pl.multiple_of(head * HEAD_DIM, HEAD_DIM), HEAD_DIM)
    cgrad = cgrad_ref.at[head]
    edge = jnp.zeros((streams, PAD, HEAD_DIM), jnp.float32)
    cgrad[:, 0:PAD, :] = edge
    cgrad[:, PAD + tokens :, :] = edge
    starts = tile_starts(tokens)[0]
    for group, first in row_groups(tokens):
        own = slice(group[0] * BLOCK, (group[-1] + 1) * BLOCK)
        span = slice(first * BLOCK, own.stop)
        query, keys = mixed_ref[0, 0, own, :], mixed_ref[0, 1, span, :]
        ups = [
            up_ref[b * BLOCK // per, b * BLOCK % per : b * BLOCK % per + BLOCK, lanes]
            for b in group
        ]
        up = stacked(ups)
        dprob = dot(up, mixed_ref[0, 2, span, :], ((1,), (1,)))
        probs, dscores = [], []
        for n, block in enumerate(group):
            lowest, at = max(0, block - STEPS), block * BLOCK
            att = att_ref[at // per, at % per : at % per + BLOCK, :]
            delta = jnp.sum(
                ups[n].astype(jnp.float32) * att.astype(jnp.float32), axis=1, keepdims=True
            )
            tiles = [prob_ref[0, starts[block] + k] for k in range(block + 1 - lowest)]
            prob = jnp.concatenate(tiles, axis=1) if len(tiles) > 1 else tiles[0]
            mine = dprob[
                n * BLOCK : (n + 1) * BLOCK,
                (lowest - first) * BLOCK : (block + 1 - first) * BLOCK,
            ]
            dscore = (prob * (mine - delta) * SCALE).astype(jnp.bfloat16)
            dscores.append(widened(dscore, block, group, first))
            probs.append(widened(prob.astype(jnp.bfloat16), block, group, first))
        dscore = stacked(dscores)
        out = slice(PAD + own.start, PAD + own.stop)
        outs = slice(PAD + span.start, PAD + own.start)
        cgrad[0, out, :] = dot(dscore, keys, ((1,), (0,)))
        for m, part in (
            (1, dot(dscore, query, ((0,), (0,)))),
            (2, dot(stacked(probs), up, ((0,), (0,)))),
        ):
            if span.start < own.start:
                cgrad[m, outs, :] += part[: own.start - span.start]
            cgrad[m, out, :] = part[own.start - span.start :]
    head_ref[:, :, lanes] = cgrad[:, PAD : 2 * PAD, :]
    span = BLOCK // rows
    for m in range(streams):
        early = before_ref[m, :, lanes].astype(jnp.float32)
        sums = [early * cgrad[m, lag : lag + PAD, :] for lag in range(KW)]
        for start in range(0, tokens, BLOCK):
            at = start // rows
            here = x_ref[at : at + span, m].reshape(BLOCK, HEAD_DIM).astype(jnp.float32)
            for lag in range(KW):
                product = here * cgrad[m, PAD + start + lag : PAD + start + lag + BLOCK, :]
                sums[lag] = sums[lag] + jnp.sum(product.reshape(BLOCK // 8, 8, HEAD_DIM), axis=0)
        for lag in range(KW):
            tapg_ref[m, lag : lag + 1, lanes] = jnp.sum(sums[lag], axis=0, keepdims=True)


def backward(local, x, before, mixed, prob, att, pieces):
    sources, streams, rows, width = x.shape
    per = width // HEAD_DIM
    tokens = sources * rows
    members = att.shape[0]
    tiles = prob.shape[1]
    here = pl.BlockSpec(memory_space=pltpu.VMEM)
    return pl.pallas_call(
        backward_kernel,
        grid_spec=pltpu.PrefetchScalarGridSpec(
            num_scalar_prefetch=1,
            grid=(per,),
            in_specs=[
                pl.BlockSpec((sources, streams, rows, HEAD_DIM), lambda h, p: (0, 0, 0, h)),
                here,
                pl.BlockSpec((1, streams, tokens, HEAD_DIM), lambda h, p: (h, 0, 0, 0)),
                pl.BlockSpec((1, tiles, BLOCK, BLOCK), lambda h, p: (h, 0, 0, 0)),
                pl.BlockSpec((members, tokens // members, HEAD_DIM), lambda h, p: (0, 0, h)),
            ]
            + [here] * members,
            out_specs=[here, here, here],
            scratch_shapes=[pltpu.VMEM((members, tokens // members, width), jnp.bfloat16)],
        ),
        out_shape=[
            jax.ShapeDtypeStruct((per, streams, tokens + 2 * PAD, HEAD_DIM), jnp.float32),
            jax.ShapeDtypeStruct((streams, KW, width), jnp.float32),
            jax.ShapeDtypeStruct((streams, PAD, width), jnp.float32),
        ],
        compiler_params=room(BACK),
        cost_estimate=estimate(20_000_000_000, 12 * x.size),
        name="backward",
    )(local, x, before, mixed, prob, att, *pieces)


def spread_kernel(cgrad_ref, taps_ref, grad_ref, tail_ref):
    _, streams, rows, _ = grad_ref.shape
    head = pl.program_id(0)
    lanes = pl.ds(pl.multiple_of(head * HEAD_DIM, HEAD_DIM), HEAD_DIM)
    for m in range(streams):
        for start in range(0, cgrad_ref.shape[2] - 2 * PAD, BLOCK):
            total = None
            for lag in range(KW):
                at = PAD + start + lag
                term = taps_ref[m, lag : lag + 1, lanes] * cgrad_ref[head, m, at : at + BLOCK, :]
                total = term if total is None else total + term
            grad_ref[start // rows : (start + BLOCK) // rows, m] = total.astype(
                jnp.bfloat16
            ).reshape(BLOCK // rows, rows, HEAD_DIM)
        tail_ref[m, :, lanes] = total[BLOCK - PAD :]


def spread(cgrad, taps, rows):
    per, streams, longer, _ = cgrad.shape
    sources, width = (longer - 2 * PAD) // rows, per * HEAD_DIM
    here = pl.BlockSpec(memory_space=pltpu.VMEM)
    return pl.pallas_call(
        spread_kernel,
        grid=(per,),
        in_specs=[here, here],
        out_specs=[
            pl.BlockSpec((sources, streams, rows, HEAD_DIM), lambda h: (0, 0, 0, h)),
            here,
        ],
        out_shape=[
            pltpu.HBM((sources, streams, rows, width), jnp.bfloat16),
            jax.ShapeDtypeStruct((streams, PAD, width), jnp.float32),
        ],
        compiler_params=room(SPREAD),
        cost_estimate=estimate(2_000_000_000, 6 * cgrad.size),
        name="spread",
    )(cgrad, taps)


def swap(value, axes, groups):
    shape = value.shape
    return lax.all_to_all(
        value.reshape(shape[0], -1, shape[-1]),
        axes,
        split_axis=0,
        concat_axis=0,
        axis_index_groups=groups,
        tiled=True,
    ).reshape(shape)


def across(value, step):
    count = lax.axis_size("ctx")
    return lax.ppermute(value, "ctx", [(i, i ^ step) for i in range(count)])


def first_exchange(piece, members):
    if members < lax.axis_size("ctx"):
        return 1, piece + across(piece, members)
    other = across(piece, 1)
    even = lax.axis_index("ctx") % 2 == 0
    return 2, jnp.concatenate(
        [jnp.where(even, piece, other), jnp.where(even, other, piece)], axis=-1
    )


def gather_columns(held, span, members):
    position = lax.axis_index("ctx").astype(jnp.int32)
    streams, taps, wide = held.shape
    steps = range(0, members, span)
    pieces = [across(held, step) if step else held for step in steps]

    def kernel(position_ref, *refs):
        o_ref = refs[-1]
        for step in steps:
            column = lax.rem(position_ref[0] ^ step, members) // span
            o_ref[:, :, pl.ds(pl.multiple_of(column * wide, wide), wide)] = refs[step // span][...]

    columns = members // span * wide
    return pl.pallas_call(
        kernel,
        grid_spec=pltpu.PrefetchScalarGridSpec(
            num_scalar_prefetch=1,
            grid=(1,),
            in_specs=[pl.BlockSpec((streams, taps, wide), lambda i, p: (0, 0, 0))] * len(pieces),
            out_specs=pl.BlockSpec((streams, taps, columns), lambda i, p: (0, 0, 0)),
        ),
        out_shape=jax.ShapeDtypeStruct((streams, taps, columns), held.dtype),
        compiler_params=room(4),
        name="place_columns",
    )(position.reshape(1), *pieces)


def by_heads(parts, qkv, filters, doc_ids, upstream):
    count, tp = lax.axis_size("ctx"), lax.axis_size("tp")
    members = count // parts
    rows, streams, _ = qkv.shape
    width = upstream.shape[1] // members
    position = lax.axis_index("ctx")
    every = everywhere = None
    if parts > 1:
        every = [[p * members + c for c in range(members)] for p in range(parts)]
        everywhere = [[c * tp + t for c in group for t in range(tp)] for group in every]
        blocks = doc_ids.shape[0] // parts
        doc_ids = lax.dynamic_slice_in_dim(doc_ids, position // members * blocks, blocks)
    slabs = split_columns(jnp.transpose(qkv, (1, 0, 2)), members, tp, 60)
    x = swap(slabs.reshape((members * tp,) + slabs.shape[2:]), AXES, everywhere)
    local = (position % members).astype(jnp.int32).reshape(1)
    pieces = split_rows(upstream, members, local)
    pieces = [across(piece, step) if step else piece for step, piece in enumerate(pieces)]
    taps = lax.dynamic_slice_in_dim(filters, position % members * width, width, 2)
    if parts > 1:
        upward = [(i, i + members) for i in range(count - members)]
        before = lax.ppermute(x[-1, :, rows - PAD :], "ctx", upward)
    else:
        before = jnp.zeros((streams, PAD, width), x.dtype)
    mixed, prob, att = forward(doc_ids, x, taps, before, members)
    attended = join_columns(swap(att, "ctx", every)[:, None, None])[0]
    away = [pltpu.with_memory_space_constraint(v, pltpu.HBM) for v in (mixed, prob, att)]
    cgrad, tap_grad, head = backward(local, x, before, *away, pieces)
    span, held = first_exchange(tap_grad, members)
    grad, tail = spread(cgrad, taps, rows)
    if parts > 1:
        after = lax.ppermute(head, "ctx", [(to, source) for source, to in upward])
        after = jnp.concatenate([jnp.zeros_like(after), after], axis=1)
        for lag in range(KW):
            tail = tail + taps[:, lag : lag + 1] * after[:, lag : lag + PAD]
        grad = grad.at[-1, :, rows - PAD :].set(tail.astype(grad.dtype))
    grad, held = lax.optimization_barrier((grad, held))
    held, attended = lax.optimization_barrier((held, attended))
    filter_grad = gather_columns(held, span, members)
    qkv_grad = join_columns(swap(grad, AXES, everywhere).reshape(slabs.shape))
    return attended, jnp.transpose(qkv_grad, (1, 0, 2)), filter_grad


def from_behind(value, axis, steps):
    count = lax.axis_size(axis)
    first, last = (max(0, -steps), min(count, count - steps))
    return lax.ppermute(value, axis, [(source, source + steps) for source in range(first, last)])


def block_docs(doc_ids, first_block, count):
    start = jnp.maximum(first_block, 0)
    picked = lax.dynamic_slice_in_dim(doc_ids, start, count)
    return jnp.repeat(picked, BLOCK)


def by_ring(qkv, filters, doc_ids, upstream):
    local = lax.all_to_all(qkv, "tp", split_axis=2, concat_axis=0, tiled=True)
    tokens = local.shape[0]
    width = local.shape[2]
    heads = width // HEAD_DIM
    blocks_here = tokens // BLOCK
    logit_scale = HEAD_DIM ** (-0.5)
    position = lax.axis_index("ctx")
    reach = STEPS + 1
    rim = from_behind(local[tokens - (KW - 1) :], "ctx", 1)
    inputs = jnp.concatenate([rim, local], axis=0).astype(jnp.float32)
    mixed = sum(
        (filters[:, lag, :] * inputs[KW - 1 - lag : KW - 1 - lag + tokens] for lag in range(KW))
    )
    mixed = mixed.astype(jnp.bfloat16)
    queries = mixed[:, 0].reshape(tokens, heads, HEAD_DIM)
    key_value = mixed[:, 1:3]
    tiles = [key_value]
    current = key_value
    for distance in range(1, STEPS + 1):
        current = from_behind(current, "ctx", 1)
        tiles.append(current)
    joined = jnp.concatenate(tiles, axis=0)
    keys = joined[:, 0].reshape(reach * tokens, heads, HEAD_DIM)
    values = joined[:, 1].reshape(reach * tokens, heads, HEAD_DIM)
    rows = jnp.arange(tokens)
    query_token = position * tokens + rows
    query_doc = block_docs(doc_ids, position * blocks_here, blocks_here)
    key_tokens = jnp.concatenate(
        [(position - distance) * tokens + rows for distance in range(reach)]
    )
    key_docs = jnp.concatenate(
        [
            block_docs(doc_ids, (position - distance) * blocks_here, blocks_here)
            for distance in range(reach)
        ]
    )
    allowed = (
        (key_tokens[None, :] >= 0)
        & (key_tokens[None, :] <= query_token[:, None])
        & (key_docs[None, :] == query_doc[:, None])
    )
    raw = (
        jnp.einsum("qhd,khd->hqk", queries, keys, preferred_element_type=jnp.float32) * logit_scale
    )
    masked = jnp.where(allowed[None], raw, -1e30)
    row_max = masked.max(axis=2)
    expo = jnp.where(allowed[None], jnp.exp(masked - row_max[:, :, None]), 0.0)
    row_sum = expo.sum(axis=2)
    weighted_values = jnp.einsum(
        "hqk,khd->qhd", expo.astype(jnp.bfloat16), values, preferred_element_type=jnp.float32
    )
    attended = (weighted_values / row_sum.T[:, :, None]).astype(jnp.bfloat16)
    grad_out = upstream.reshape(tokens, heads, HEAD_DIM)
    delta = jnp.sum(grad_out.astype(jnp.float32) * attended.astype(jnp.float32), axis=-1).T
    prob = expo / row_sum[:, :, None]
    value_part = jnp.einsum(
        "hqk,qhd->khd", prob.astype(jnp.bfloat16), grad_out, preferred_element_type=jnp.float32
    )
    probability_gradient = jnp.einsum(
        "qhd,khd->hqk", grad_out, values, preferred_element_type=jnp.float32
    )
    score_gradient = (prob * (probability_gradient - delta[:, :, None]) * logit_scale).astype(
        jnp.bfloat16
    )
    query_gradient_rows = jnp.einsum(
        "hqk,khd->qhd", score_gradient, keys, preferred_element_type=jnp.float32
    )
    key_part = jnp.einsum(
        "hqk,qhd->khd", score_gradient, queries, preferred_element_type=jnp.float32
    )
    stacked = jnp.stack(
        [key_part.reshape(reach, tokens, width), value_part.reshape(reach, tokens, width)], axis=2
    )
    partials = [stacked[distance] for distance in range(reach)]
    carried = partials[STEPS]
    for distance in range(STEPS - 1, -1, -1):
        carried = from_behind(carried, "ctx", -1)
        carried = carried + partials[distance]
    conv_grad = jnp.concatenate([query_gradient_rows.reshape(tokens, 1, width), carried], axis=1)
    grad_edge = from_behind(conv_grad[: KW - 1], "ctx", -1)
    extended = jnp.concatenate([conv_grad, grad_edge], axis=0)
    input_grad = sum((filters[:, lag, :] * extended[lag : lag + tokens] for lag in range(KW)))
    tap_terms = jnp.stack(
        [
            jnp.sum(inputs[KW - 1 - lag : KW - 1 - lag + tokens] * conv_grad, axis=0)
            for lag in range(KW)
        ],
        axis=1,
    )
    filter_grad = lax.psum(tap_terms, "ctx")
    qkv_grad = lax.all_to_all(
        input_grad.astype(jnp.bfloat16), "tp", split_axis=0, concat_axis=2, tiled=True
    )
    return (attended.reshape(tokens, width), qkv_grad, filter_grad)


def solution(mesh):
    count = mesh.shape["ctx"]

    def shards(qkv, filters, doc_ids, upstream):
        tokens, width = upstream.shape
        heads = width // HEAD_DIM
        args = (qkv, filters, doc_ids, upstream)
        even = tokens % BLOCK == 0 and qkv.shape[0] % PAD == 0 and count & (count - 1) == 0
        if heads % count or not even or count < 4:
            return by_ring(*args)
        middle = doc_ids.shape[0] // 2
        apart = doc_ids[middle - 1] != doc_ids[middle]
        return lax.cond(
            apart, functools.partial(by_heads, 2), functools.partial(by_heads, 1), *args
        )

    return jax.shard_map(
        shards,
        mesh=mesh,
        in_specs=(P(("ctx", "tp"), None, None), P(None, None, "tp"), P(), P("ctx", "tp")),
        out_specs=(P("ctx", "tp"), P(("ctx", "tp"), None, None), P(None, None, "tp")),
        check_vma=False,
    )
```

```python
import functools
import math

import jax
import jax.numpy as jnp
from jax import lax
from jax.experimental import pallas as pl
from jax.experimental.pallas import tpu as pltpu
from jax.sharding import PartitionSpec as P

HEAD_DIM = 128
KW = 7
BLOCK = 128
STEPS = 4
PAD = 8
SCALE = HEAD_DIM ** (-0.5)
SCALE_LOG2 = SCALE * math.log2(math.e)
AXES = ("ctx", "tp")
FORE, BACK, SPREAD = 24, 24, 16


def dot(a, b, dims):
    return lax.dot_general(a, b, (dims, ((), ())), preferred_element_type=jnp.float32)


def room(mebibytes):
    return pltpu.CompilerParams(vmem_limit_bytes=mebibytes << 20)


def estimate(flops, moved):
    return pl.CostEstimate(flops=flops, bytes_accessed=moved, transcendentals=0)


def split_columns(x, members, tp, mebibytes):
    streams, rows, channels = x.shape
    width = channels // tp // members
    steps = 2 if tp % 2 == 0 else 1
    part = tp // steps

    def kernel(x_ref, o_ref):
        for t in range(part):
            for c in range(members):
                at = (t * members + c) * width
                o_ref[c, t] = x_ref[:, :, at : at + width]

    return pl.pallas_call(
        kernel,
        grid=(steps,),
        in_specs=[pl.BlockSpec((streams, rows, part * members * width), lambda i: (0, 0, i))],
        out_specs=pl.BlockSpec((members, part, streams, rows, width), lambda i: (0, i, 0, 0, 0)),
        out_shape=jax.ShapeDtypeStruct((members, tp, streams, rows, width), x.dtype),
        cost_estimate=estimate(0, 4 * x.size),
        compiler_params=room(mebibytes),
        name="split_columns",
    )(x)


def split_rows(x, members, local):
    tokens, channels = x.shape
    width = channels // members

    def kernel(local_ref, x_ref, *o_refs):
        for step in range(members):
            at = pl.multiple_of((local_ref[0] ^ step) * width, width)
            o_refs[step][...] = x_ref[:, pl.ds(at, width)]

    piece = pl.BlockSpec((tokens, width), lambda i, p: (0, 0))
    return pl.pallas_call(
        kernel,
        grid_spec=pltpu.PrefetchScalarGridSpec(
            num_scalar_prefetch=1,
            grid=(1,),
            in_specs=[pl.BlockSpec((tokens, channels), lambda i, p: (0, 0))],
            out_specs=[piece] * members,
        ),
        out_shape=[jax.ShapeDtypeStruct((tokens, width), x.dtype)] * members,
        compiler_params=room(10),
        cost_estimate=estimate(0, 4 * x.size),
        name="split_rows",
    )(local, x)


def join_columns(x):
    members, tp, streams, rows, width = x.shape
    steps = 2 if tp % 2 == 0 else 1
    part = tp // steps

    def kernel(x_ref, o_ref):
        for t in range(part):
            for c in range(members):
                at = (t * members + c) * width
                o_ref[:, :, at : at + width] = x_ref[c, pl.program_id(0) * part + t]

    return pl.pallas_call(
        kernel,
        grid=(steps,),
        in_specs=[pl.BlockSpec(memory_space=pltpu.VMEM)],
        out_specs=pl.BlockSpec((streams, rows, part * members * width), lambda i: (0, 0, i)),
        out_shape=pltpu.HBM((streams, rows, tp * members * width), x.dtype),
        cost_estimate=estimate(0, 4 * x.size),
        compiler_params=room(10),
        name="join_columns",
    )(x)


def tile_starts(tokens):
    starts, total = [], 0
    for block in range(tokens // BLOCK):
        starts.append(total)
        total += block + 1 - max(0, block - STEPS)
    return starts, total


def row_groups(tokens):
    blocks = tokens // BLOCK
    size = 2 if blocks % 2 == 0 else 1
    for start in range(0, blocks, size):
        yield range(start, start + size), max(0, start - STEPS)


def widened(value, block, group, first):
    before = (max(0, block - STEPS) - first) * BLOCK
    behind = (group[-1] - block) * BLOCK
    parts = [jnp.zeros((BLOCK, before), value.dtype)] if before else []
    parts.append(value)
    if behind:
        parts.append(jnp.zeros((BLOCK, behind), value.dtype))
    return jnp.concatenate(parts, axis=1) if len(parts) > 1 else value


def stacked(parts):
    return jnp.concatenate(parts, axis=0) if len(parts) > 1 else parts[0]


def forward_kernel(docs, x_ref, taps_ref, before_ref, mixed_ref, prob_ref, out_ref, padded):
    sources, streams, rows, _ = x_ref.shape
    tokens = sources * rows
    head = pl.program_id(0)
    lanes = pl.ds(pl.multiple_of(head * HEAD_DIM, HEAD_DIM), HEAD_DIM)
    padded[:, 0:PAD, :] = before_ref[:, :, lanes].astype(jnp.float32)
    for m in range(streams):
        padded[m, PAD:, :] = x_ref[:, m, :, lanes].reshape(tokens, HEAD_DIM).astype(jnp.float32)
    for m in range(streams):
        for start in range(0, tokens, BLOCK):
            total = None
            for lag in range(KW):
                at = PAD + start - lag
                term = taps_ref[m, lag : lag + 1, lanes] * padded[m, at : at + BLOCK, :]
                total = term if total is None else total + term
            mixed_ref[0, m, start : start + BLOCK, :] = total.astype(jnp.bfloat16)
    below = lax.broadcasted_iota(jnp.int32, (BLOCK, BLOCK), 0) >= lax.broadcasted_iota(
        jnp.int32, (BLOCK, BLOCK), 1
    )
    starts = tile_starts(tokens)[0]
    for group, first in row_groups(tokens):
        own = slice(group[0] * BLOCK, (group[-1] + 1) * BLOCK)
        span = slice(first * BLOCK, own.stop)
        raw = dot(mixed_ref[0, 0, own, :], mixed_ref[0, 1, span, :], ((1,), (1,)))
        sheets, inverses = [], []
        for block in group:
            lowest = max(0, block - STEPS)
            mine = raw[(block - group[0]) * BLOCK : (block - group[0] + 1) * BLOCK]
            parts = []
            for other in range(lowest, block + 1):
                part = mine[:, (other - first) * BLOCK : (other - first + 1) * BLOCK]
                allowed = below if other == block else docs[other] == docs[block]
                parts.append(jnp.where(allowed, part, -1e30))
            masked = jnp.concatenate(parts, axis=1) if len(parts) > 1 else parts[0]
            expo = jnp.exp2((masked - jnp.max(masked, axis=1, keepdims=True)) * SCALE_LOG2)
            inverses.append(1.0 / jnp.sum(expo, axis=1, keepdims=True))
            sheets.append(widened(expo.astype(jnp.bfloat16), block, group, first))
            prob = expo * inverses[-1]
            for n in range(block + 1 - lowest):
                prob_ref[0, starts[block] + n] = prob[:, n * BLOCK : (n + 1) * BLOCK]
        total = dot(stacked(sheets), mixed_ref[0, 2, span, :], ((1,), (0,)))
        per = out_ref.shape[1]
        for n, block in enumerate(group):
            at = block * BLOCK
            out_ref[at // per, at % per : at % per + BLOCK, :] = (
                total[n * BLOCK : (n + 1) * BLOCK] * inverses[n]
            ).astype(jnp.bfloat16)


def forward(docs, x, taps, before, members):
    sources, streams, rows, width = x.shape
    per = width // HEAD_DIM
    tokens = sources * rows
    tiles = tile_starts(tokens)[1]
    here = pl.BlockSpec(memory_space=pltpu.VMEM)
    return pl.pallas_call(
        forward_kernel,
        grid_spec=pltpu.PrefetchScalarGridSpec(
            num_scalar_prefetch=1,
            grid=(per,),
            in_specs=[here, here, here],
            out_specs=[
                pl.BlockSpec((1, streams, tokens, HEAD_DIM), lambda h, d: (h, 0, 0, 0)),
                pl.BlockSpec((1, tiles, BLOCK, BLOCK), lambda h, d: (h, 0, 0, 0)),
                pl.BlockSpec((members, tokens // members, HEAD_DIM), lambda h, d: (0, 0, h)),
            ],
            scratch_shapes=[pltpu.VMEM((streams, tokens + PAD, HEAD_DIM), jnp.float32)],
        ),
        out_shape=[
            pltpu.HBM((per, streams, tokens, HEAD_DIM), jnp.bfloat16),
            pltpu.HBM((per, tiles, BLOCK, BLOCK), jnp.float32),
            pltpu.HBM((members, tokens // members, width), jnp.bfloat16),
        ],
        compiler_params=room(FORE),
        cost_estimate=estimate(10_000_000_000, 8 * x.size),
        name="forward",
    )(docs, x, taps, before)


def backward_kernel(
    local, x_ref, before_ref, mixed_ref, prob_ref, att_ref, *refs
):
    *up_refs, cgrad_ref, extra_ref, up_ref = refs
    sources, streams, rows, _ = x_ref.shape
    tokens = sources * rows
    per = att_ref.shape[1]
    head = pl.program_id(0)

    @pl.when(head == 0)
    def _():
        for step, piece_ref in enumerate(up_refs):
            up_ref[local[0] ^ step] = piece_ref[...]

    lanes = pl.ds(pl.multiple_of(head * HEAD_DIM, HEAD_DIM), HEAD_DIM)
    cgrad = cgrad_ref.at[head]
    edge = jnp.zeros((streams, PAD, HEAD_DIM), jnp.float32)
    cgrad[:, 0:PAD, :] = edge
    cgrad[:, PAD + tokens :, :] = edge
    starts = tile_starts(tokens)[0]
    for group, first in row_groups(tokens):
        own = slice(group[0] * BLOCK, (group[-1] + 1) * BLOCK)
        span = slice(first * BLOCK, own.stop)
        query, keys = mixed_ref[0, 0, own, :], mixed_ref[0, 1, span, :]
        ups = [
            up_ref[b * BLOCK // per, b * BLOCK % per : b * BLOCK % per + BLOCK, lanes]
            for b in group
        ]
        up = stacked(ups)
        dprob = dot(up, mixed_ref[0, 2, span, :], ((1,), (1,)))
        probs, dscores = [], []
        for n, block in enumerate(group):
            lowest, at = max(0, block - STEPS), block * BLOCK
            att = att_ref[at // per, at % per : at % per + BLOCK, :]
            delta = jnp.sum(
                ups[n].astype(jnp.float32) * att.astype(jnp.float32), axis=1, keepdims=True
            )
            tiles = [prob_ref[0, starts[block] + k] for k in range(block + 1 - lowest)]
            prob = jnp.concatenate(tiles, axis=1) if len(tiles) > 1 else tiles[0]
            mine = dprob[
                n * BLOCK : (n + 1) * BLOCK,
                (lowest - first) * BLOCK : (block + 1 - first) * BLOCK,
            ]
            dscore = (prob * (mine - delta) * SCALE).astype(jnp.bfloat16)
            dscores.append(widened(dscore, block, group, first))
            probs.append(widened(prob.astype(jnp.bfloat16), block, group, first))
        dscore = stacked(dscores)
        out = slice(PAD + own.start, PAD + own.stop)
        outs = slice(PAD + span.start, PAD + own.start)
        cgrad[0, out, :] = dot(dscore, keys, ((1,), (0,)))
        for m, part in (
            (1, dot(dscore, query, ((0,), (0,)))),
            (2, dot(stacked(probs), up, ((0,), (0,)))),
        ):
            if span.start < own.start:
                cgrad[m, outs, :] += part[: own.start - span.start]
            cgrad[m, out, :] = part[own.start - span.start :]
    extra_ref[:, 0:PAD, lanes] = cgrad[:, PAD : 2 * PAD, :]
    extra_ref[:, PAD + KW :, lanes] = edge[:, KW:]
    span = BLOCK // rows
    for m in range(streams):
        early = before_ref[m, :, lanes].astype(jnp.float32)
        sums = [early * cgrad[m, lag : lag + PAD, :] for lag in range(KW)]
        for start in range(0, tokens, BLOCK):
            at = start // rows
            here = x_ref[at : at + span, m].reshape(BLOCK, HEAD_DIM).astype(jnp.float32)
            for lag in range(KW):
                product = here * cgrad[m, PAD + start + lag : PAD + start + lag + BLOCK, :]
                sums[lag] = sums[lag] + jnp.sum(product.reshape(BLOCK // 8, 8, HEAD_DIM), axis=0)
        for lag in range(KW):
            extra_ref[m, PAD + lag : PAD + lag + 1, lanes] = jnp.sum(
                sums[lag], axis=0, keepdims=True
            )


def backward(local, x, before, mixed, prob, att, pieces):
    sources, streams, rows, width = x.shape
    per = width // HEAD_DIM
    tokens = sources * rows
    members = att.shape[0]
    tiles = prob.shape[1]
    here = pl.BlockSpec(memory_space=pltpu.VMEM)
    return pl.pallas_call(
        backward_kernel,
        grid_spec=pltpu.PrefetchScalarGridSpec(
            num_scalar_prefetch=1,
            grid=(per,),
            in_specs=[
                pl.BlockSpec((sources, streams, rows, HEAD_DIM), lambda h, p: (0, 0, 0, h)),
                here,
                pl.BlockSpec((1, streams, tokens, HEAD_DIM), lambda h, p: (h, 0, 0, 0)),
                pl.BlockSpec((1, tiles, BLOCK, BLOCK), lambda h, p: (h, 0, 0, 0)),
                pl.BlockSpec((members, tokens // members, HEAD_DIM), lambda h, p: (0, 0, h)),
            ]
            + [here] * members,
            out_specs=[here, here],
            scratch_shapes=[pltpu.VMEM((members, tokens // members, width), jnp.bfloat16)],
        ),
        out_shape=[
            jax.ShapeDtypeStruct((per, streams, tokens + 2 * PAD, HEAD_DIM), jnp.float32),
            jax.ShapeDtypeStruct((streams, 2 * PAD, width), jnp.float32),
        ],
        compiler_params=room(BACK),
        cost_estimate=estimate(20_000_000_000, 12 * x.size),
        name="backward",
    )(local, x, before, mixed, prob, att, *pieces)


def spread_kernel(cgrad_ref, taps_ref, grad_ref, tail_ref):
    _, streams, rows, _ = grad_ref.shape
    head = pl.program_id(0)
    lanes = pl.ds(pl.multiple_of(head * HEAD_DIM, HEAD_DIM), HEAD_DIM)
    for m in range(streams):
        for start in range(0, cgrad_ref.shape[2] - 2 * PAD, BLOCK):
            total = None
            for lag in range(KW):
                at = PAD + start + lag
                term = taps_ref[m, lag : lag + 1, lanes] * cgrad_ref[head, m, at : at + BLOCK, :]
                total = term if total is None else total + term
            grad_ref[start // rows : (start + BLOCK) // rows, m] = total.astype(
                jnp.bfloat16
            ).reshape(BLOCK // rows, rows, HEAD_DIM)
        tail_ref[m, :, lanes] = total[BLOCK - PAD :]


def spread(cgrad, taps, rows):
    per, streams, longer, _ = cgrad.shape
    sources, width = (longer - 2 * PAD) // rows, per * HEAD_DIM
    here = pl.BlockSpec(memory_space=pltpu.VMEM)
    return pl.pallas_call(
        spread_kernel,
        grid=(per,),
        in_specs=[here, here],
        out_specs=[
            pl.BlockSpec((sources, streams, rows, HEAD_DIM), lambda h: (0, 0, 0, h)),
            here,
        ],
        out_shape=[
            pltpu.HBM((sources, streams, rows, width), jnp.bfloat16),
            jax.ShapeDtypeStruct((streams, PAD, width), jnp.float32),
        ],
        compiler_params=room(SPREAD),
        cost_estimate=estimate(2_000_000_000, 6 * cgrad.size),
        name="spread",
    )(cgrad, taps)


def swap(value, axes, groups):
    shape = value.shape
    return lax.all_to_all(
        value.reshape(shape[0], -1, shape[-1]),
        axes,
        split_axis=0,
        concat_axis=0,
        axis_index_groups=groups,
        tiled=True,
    ).reshape(shape)


def across(value, step):
    count = lax.axis_size("ctx")
    return lax.ppermute(value, "ctx", [(i, i ^ step) for i in range(count)])


def beside_neighbour(piece):
    other = across(piece, 1)
    even = lax.axis_index("ctx") % 2 == 0
    return jnp.concatenate(
        [jnp.where(even, piece, other), jnp.where(even, other, piece)], axis=-1
    )


def gather_columns(held, span, members):
    position = lax.axis_index("ctx").astype(jnp.int32)
    streams, taps, wide = held.shape
    steps = range(0, members, span)
    pieces = [across(held, step) if step else held for step in steps]

    def kernel(position_ref, *refs):
        o_ref = refs[-1]
        for step in steps:
            column = lax.rem(position_ref[0] ^ step, members) // span
            o_ref[:, :, pl.ds(pl.multiple_of(column * wide, wide), wide)] = refs[step // span][
                ...
            ].astype(jnp.float32)

    columns = members // span * wide
    return pl.pallas_call(
        kernel,
        grid_spec=pltpu.PrefetchScalarGridSpec(
            num_scalar_prefetch=1,
            grid=(1,),
            in_specs=[pl.BlockSpec((streams, taps, wide), lambda i, p: (0, 0, 0))] * len(pieces),
            out_specs=pl.BlockSpec((streams, taps, columns), lambda i, p: (0, 0, 0)),
        ),
        out_shape=jax.ShapeDtypeStruct((streams, taps, columns), jnp.float32),
        compiler_params=room(4),
        name="place_columns",
    )(position.reshape(1), *pieces)


def by_heads(parts, qkv, filters, doc_ids, upstream):
    count, tp = lax.axis_size("ctx"), lax.axis_size("tp")
    members = count // parts
    rows, streams, _ = qkv.shape
    width = upstream.shape[1] // members
    position = lax.axis_index("ctx")
    every = everywhere = None
    if parts > 1:
        every = [[p * members + c for c in range(members)] for p in range(parts)]
        everywhere = [[c * tp + t for c in group for t in range(tp)] for group in every]
        blocks = doc_ids.shape[0] // parts
        doc_ids = lax.dynamic_slice_in_dim(doc_ids, position // members * blocks, blocks)
    slabs = split_columns(jnp.transpose(qkv, (1, 0, 2)), members, tp, 60)
    x = swap(slabs.reshape((members * tp,) + slabs.shape[2:]), AXES, everywhere)
    local = (position % members).astype(jnp.int32).reshape(1)
    pieces = split_rows(upstream, members, local)
    pieces = [across(piece, step) if step else piece for step, piece in enumerate(pieces)]
    taps = lax.dynamic_slice_in_dim(filters, position % members * width, width, 2)
    if parts > 1:
        upward = [(i, i + members) for i in range(count - members)]
        before = lax.ppermute(x[-1, :, rows - PAD :], "ctx", upward)
    else:
        before = jnp.zeros((streams, PAD, width), x.dtype)
    mixed, prob, att = forward(doc_ids, x, taps, before, members)
    attended = join_columns(swap(att, "ctx", every)[:, None, None])[0]
    away = [pltpu.with_memory_space_constraint(v, pltpu.HBM) for v in (mixed, prob, att)]
    cgrad, extra = backward(local, x, before, *away, pieces)
    if parts > 1:
        other = across(extra, members)
        span, held = 1, (extra + other)[:, PAD : PAD + KW].astype(jnp.bfloat16)
    else:
        span, held = 2, beside_neighbour(extra[:, PAD : PAD + KW].astype(jnp.bfloat16))
    grad, tail = spread(cgrad, taps, rows)
    if parts > 1:
        after = jnp.where(position < members, other[:, 0:PAD], 0.0)
        after = jnp.concatenate([jnp.zeros_like(after), after], axis=1)
        for lag in range(KW):
            tail = tail + taps[:, lag : lag + 1] * after[:, lag : lag + PAD]
        grad = grad.at[-1, :, rows - PAD :].set(tail.astype(grad.dtype))
    grad, held = lax.optimization_barrier((grad, held))
    held, attended = lax.optimization_barrier((held, attended))
    filter_grad = gather_columns(held, span, members)
    qkv_grad = join_columns(swap(grad, AXES, everywhere).reshape(slabs.shape))
    return attended, jnp.transpose(qkv_grad, (1, 0, 2)), filter_grad


def from_behind(value, axis, steps):
    count = lax.axis_size(axis)
    first, last = (max(0, -steps), min(count, count - steps))
    return lax.ppermute(value, axis, [(source, source + steps) for source in range(first, last)])


def block_docs(doc_ids, first_block, count):
    start = jnp.maximum(first_block, 0)
    picked = lax.dynamic_slice_in_dim(doc_ids, start, count)
    return jnp.repeat(picked, BLOCK)


def by_ring(qkv, filters, doc_ids, upstream):
    local = lax.all_to_all(qkv, "tp", split_axis=2, concat_axis=0, tiled=True)
    tokens = local.shape[0]
    width = local.shape[2]
    heads = width // HEAD_DIM
    blocks_here = tokens // BLOCK
    logit_scale = HEAD_DIM ** (-0.5)
    position = lax.axis_index("ctx")
    reach = STEPS + 1
    rim = from_behind(local[tokens - (KW - 1) :], "ctx", 1)
    inputs = jnp.concatenate([rim, local], axis=0).astype(jnp.float32)
    mixed = sum(
        (filters[:, lag, :] * inputs[KW - 1 - lag : KW - 1 - lag + tokens] for lag in range(KW))
    )
    mixed = mixed.astype(jnp.bfloat16)
    queries = mixed[:, 0].reshape(tokens, heads, HEAD_DIM)
    key_value = mixed[:, 1:3]
    tiles = [key_value]
    current = key_value
    for distance in range(1, STEPS + 1):
        current = from_behind(current, "ctx", 1)
        tiles.append(current)
    joined = jnp.concatenate(tiles, axis=0)
    keys = joined[:, 0].reshape(reach * tokens, heads, HEAD_DIM)
    values = joined[:, 1].reshape(reach * tokens, heads, HEAD_DIM)
    rows = jnp.arange(tokens)
    query_token = position * tokens + rows
    query_doc = block_docs(doc_ids, position * blocks_here, blocks_here)
    key_tokens = jnp.concatenate(
        [(position - distance) * tokens + rows for distance in range(reach)]
    )
    key_docs = jnp.concatenate(
        [
            block_docs(doc_ids, (position - distance) * blocks_here, blocks_here)
            for distance in range(reach)
        ]
    )
    allowed = (
        (key_tokens[None, :] >= 0)
        & (key_tokens[None, :] <= query_token[:, None])
        & (key_docs[None, :] == query_doc[:, None])
    )
    raw = (
        jnp.einsum("qhd,khd->hqk", queries, keys, preferred_element_type=jnp.float32) * logit_scale
    )
    masked = jnp.where(allowed[None], raw, -1e30)
    row_max = masked.max(axis=2)
    expo = jnp.where(allowed[None], jnp.exp(masked - row_max[:, :, None]), 0.0)
    row_sum = expo.sum(axis=2)
    weighted_values = jnp.einsum(
        "hqk,khd->qhd", expo.astype(jnp.bfloat16), values, preferred_element_type=jnp.float32
    )
    attended = (weighted_values / row_sum.T[:, :, None]).astype(jnp.bfloat16)
    grad_out = upstream.reshape(tokens, heads, HEAD_DIM)
    delta = jnp.sum(grad_out.astype(jnp.float32) * attended.astype(jnp.float32), axis=-1).T
    prob = expo / row_sum[:, :, None]
    value_part = jnp.einsum(
        "hqk,qhd->khd", prob.astype(jnp.bfloat16), grad_out, preferred_element_type=jnp.float32
    )
    probability_gradient = jnp.einsum(
        "qhd,khd->hqk", grad_out, values, preferred_element_type=jnp.float32
    )
    score_gradient = (prob * (probability_gradient - delta[:, :, None]) * logit_scale).astype(
        jnp.bfloat16
    )
    query_gradient_rows = jnp.einsum(
        "hqk,khd->qhd", score_gradient, keys, preferred_element_type=jnp.float32
    )
    key_part = jnp.einsum(
        "hqk,qhd->khd", score_gradient, queries, preferred_element_type=jnp.float32
    )
    stacked = jnp.stack(
        [key_part.reshape(reach, tokens, width), value_part.reshape(reach, tokens, width)], axis=2
    )
    partials = [stacked[distance] for distance in range(reach)]
    carried = partials[STEPS]
    for distance in range(STEPS - 1, -1, -1):
        carried = from_behind(carried, "ctx", -1)
        carried = carried + partials[distance]
    conv_grad = jnp.concatenate([query_gradient_rows.reshape(tokens, 1, width), carried], axis=1)
    grad_edge = from_behind(conv_grad[: KW - 1], "ctx", -1)
    extended = jnp.concatenate([conv_grad, grad_edge], axis=0)
    input_grad = sum((filters[:, lag, :] * extended[lag : lag + tokens] for lag in range(KW)))
    tap_terms = jnp.stack(
        [
            jnp.sum(inputs[KW - 1 - lag : KW - 1 - lag + tokens] * conv_grad, axis=0)
            for lag in range(KW)
        ],
        axis=1,
    )
    filter_grad = lax.psum(tap_terms, "ctx")
    qkv_grad = lax.all_to_all(
        input_grad.astype(jnp.bfloat16), "tp", split_axis=0, concat_axis=2, tiled=True
    )
    return (attended.reshape(tokens, width), qkv_grad, filter_grad)


def solution(mesh):
    count = mesh.shape["ctx"]

    def shards(qkv, filters, doc_ids, upstream):
        tokens, width = upstream.shape
        heads = width // HEAD_DIM
        args = (qkv, filters, doc_ids, upstream)
        even = tokens % BLOCK == 0 and qkv.shape[0] % PAD == 0 and count & (count - 1) == 0
        if heads % count or not even or count < 4:
            return by_ring(*args)
        middle = doc_ids.shape[0] // 2
        apart = doc_ids[middle - 1] != doc_ids[middle]
        return lax.cond(
            apart, functools.partial(by_heads, 2), functools.partial(by_heads, 1), *args
        )

    return jax.shard_map(
        shards,
        mesh=mesh,
        in_specs=(P(("ctx", "tp"), None, None), P(None, None, "tp"), P(), P("ctx", "tp")),
        out_specs=(P("ctx", "tp"), P(("ctx", "tp"), None, None), P(None, None, "tp")),
        check_vma=False,
    )
```

```python
import functools
import math

import jax
import jax.numpy as jnp
from jax import lax
from jax.experimental import pallas as pl
from jax.experimental.pallas import tpu as pltpu
from jax.sharding import PartitionSpec as P

HEAD_DIM = 128
KW = 7
BLOCK = 128
STEPS = 4
PAD = 8
SCALE = HEAD_DIM ** (-0.5)
SCALE_LOG2 = SCALE * math.log2(math.e)
AXES = ("ctx", "tp")
FORE, BACK, SPREAD = 24, 24, 16


def dot(a, b, dims):
    return lax.dot_general(a, b, (dims, ((), ())), preferred_element_type=jnp.float32)


def room(mebibytes):
    return pltpu.CompilerParams(vmem_limit_bytes=mebibytes << 20)


def estimate(flops, moved):
    return pl.CostEstimate(flops=flops, bytes_accessed=moved, transcendentals=0)


def split_columns(docs, x, width):
    streams, rows, channels = x.shape
    count = channels // width
    steps = 2 if count % 2 == 0 else 1
    part = count // steps
    middle = docs.shape[0] // 2

    def kernel(docs_ref, x_ref, o_ref, apart_ref):
        apart_ref[0] = (docs_ref[middle - 1] != docs_ref[middle]).astype(jnp.int32)
        for n in range(part):
            o_ref[n] = x_ref[:, :, n * width : (n + 1) * width]

    return pl.pallas_call(
        kernel,
        grid_spec=pltpu.PrefetchScalarGridSpec(
            num_scalar_prefetch=1,
            grid=(steps,),
            in_specs=[pl.BlockSpec((streams, rows, part * width), lambda i, d: (0, 0, i))],
            out_specs=[
                pl.BlockSpec((part, streams, rows, width), lambda i, d: (i, 0, 0, 0)),
                pl.BlockSpec(memory_space=pltpu.SMEM),
            ],
        ),
        out_shape=[
            jax.ShapeDtypeStruct((count, streams, rows, width), x.dtype),
            jax.ShapeDtypeStruct((1,), jnp.int32),
        ],
        compiler_params=room(60),
        cost_estimate=estimate(0, 4 * x.size),
        name="split_columns",
    )(docs, x)


def split_rows(x, members, local):
    tokens, channels = x.shape
    width = channels // members

    def kernel(local_ref, x_ref, *o_refs):
        for step in range(members):
            at = pl.multiple_of((local_ref[0] ^ step) * width, width)
            o_refs[step][...] = x_ref[:, pl.ds(at, width)]

    piece = pl.BlockSpec((tokens, width), lambda i, p: (0, 0))
    return pl.pallas_call(
        kernel,
        grid_spec=pltpu.PrefetchScalarGridSpec(
            num_scalar_prefetch=1,
            grid=(1,),
            in_specs=[pl.BlockSpec((tokens, channels), lambda i, p: (0, 0))],
            out_specs=[piece] * members,
        ),
        out_shape=[jax.ShapeDtypeStruct((tokens, width), x.dtype)] * members,
        compiler_params=room(10),
        cost_estimate=estimate(0, 4 * x.size),
        name="split_rows",
    )(local, x)


def join_columns(x):
    count, streams, rows, width = x.shape
    steps = 2 if count % 2 == 0 else 1
    part = count // steps

    def kernel(x_ref, o_ref):
        for n in range(part):
            o_ref[:, :, n * width : (n + 1) * width] = x_ref[pl.program_id(0) * part + n]

    return pl.pallas_call(
        kernel,
        grid=(steps,),
        in_specs=[pl.BlockSpec(memory_space=pltpu.VMEM)],
        out_specs=pl.BlockSpec((streams, rows, part * width), lambda i: (0, 0, i)),
        out_shape=pltpu.HBM((streams, rows, count * width), x.dtype),
        compiler_params=room(10),
        cost_estimate=estimate(0, 4 * x.size),
        name="join_columns",
    )(x)


def tile_starts(tokens):
    starts, total = [], 0
    for block in range(tokens // BLOCK):
        starts.append(total)
        total += block + 1 - max(0, block - STEPS)
    return starts, total


def row_groups(tokens):
    blocks = tokens // BLOCK
    size = 2 if blocks % 2 == 0 else 1
    for start in range(0, blocks, size):
        yield range(start, start + size), max(0, start - STEPS)


def widened(value, block, group, first):
    before = (max(0, block - STEPS) - first) * BLOCK
    behind = (group[-1] - block) * BLOCK
    parts = [jnp.zeros((BLOCK, before), value.dtype)] if before else []
    parts.append(value)
    if behind:
        parts.append(jnp.zeros((BLOCK, behind), value.dtype))
    return jnp.concatenate(parts, axis=1) if len(parts) > 1 else value


def stacked(parts):
    return jnp.concatenate(parts, axis=0) if len(parts) > 1 else parts[0]


def forward_kernel(docs, x_ref, taps_ref, before_ref, mixed_ref, prob_ref, out_ref, padded):
    tp, owners, _, streams, rows, wide = x_ref.shape
    chunk = tp * rows
    tokens = owners * chunk
    head = pl.program_id(0)
    lanes = pl.ds(pl.multiple_of(head * HEAD_DIM, HEAD_DIM), HEAD_DIM)
    each = wide // HEAD_DIM
    slab = head // each
    inner = pl.ds(pl.multiple_of(head % each * HEAD_DIM, HEAD_DIM), HEAD_DIM)
    padded[:, 0:PAD, :] = before_ref[:, :, lanes].astype(jnp.float32)
    for m in range(streams):
        for c in range(owners):
            mine = x_ref[:, c, slab, m, :, inner].reshape(chunk, HEAD_DIM)
            padded[m, PAD + c * chunk : PAD + (c + 1) * chunk, :] = mine.astype(jnp.float32)
    for m in range(streams):
        for start in range(0, tokens, BLOCK):
            total = None
            for lag in range(KW):
                at = PAD + start - lag
                term = taps_ref[m, lag : lag + 1, lanes] * padded[m, at : at + BLOCK, :]
                total = term if total is None else total + term
            mixed_ref[0, m, start : start + BLOCK, :] = total.astype(jnp.bfloat16)
    below = lax.broadcasted_iota(jnp.int32, (BLOCK, BLOCK), 0) >= lax.broadcasted_iota(
        jnp.int32, (BLOCK, BLOCK), 1
    )
    starts = tile_starts(tokens)[0]
    for group, first in row_groups(tokens):
        own = slice(group[0] * BLOCK, (group[-1] + 1) * BLOCK)
        span = slice(first * BLOCK, own.stop)
        raw = dot(mixed_ref[0, 0, own, :], mixed_ref[0, 1, span, :], ((1,), (1,)))
        sheets, inverses = [], []
        for block in group:
            lowest = max(0, block - STEPS)
            mine = raw[(block - group[0]) * BLOCK : (block - group[0] + 1) * BLOCK]
            parts = []
            for other in range(lowest, block + 1):
                part = mine[:, (other - first) * BLOCK : (other - first + 1) * BLOCK]
                allowed = below if other == block else docs[other] == docs[block]
                parts.append(jnp.where(allowed, part, -1e30))
            masked = jnp.concatenate(parts, axis=1) if len(parts) > 1 else parts[0]
            expo = jnp.exp2((masked - jnp.max(masked, axis=1, keepdims=True)) * SCALE_LOG2)
            inverses.append(1.0 / jnp.sum(expo, axis=1, keepdims=True))
            sheets.append(widened(expo.astype(jnp.bfloat16), block, group, first))
            prob = expo * inverses[-1]
            for n in range(block + 1 - lowest):
                prob_ref[0, starts[block] + n] = prob[:, n * BLOCK : (n + 1) * BLOCK]
        total = dot(stacked(sheets), mixed_ref[0, 2, span, :], ((1,), (0,)))
        per = out_ref.shape[1]
        for n, block in enumerate(group):
            at = block * BLOCK
            out_ref[at // per, at % per : at % per + BLOCK, :] = (
                total[n * BLOCK : (n + 1) * BLOCK] * inverses[n]
            ).astype(jnp.bfloat16)


def forward(docs, x, taps, before, members):
    tp, _, slabs, streams, rows, wide = x.shape
    width = slabs * wide
    per = width // HEAD_DIM
    tokens = tp * members * rows
    tiles = tile_starts(tokens)[1]
    here = pl.BlockSpec(memory_space=pltpu.VMEM)
    return pl.pallas_call(
        forward_kernel,
        grid_spec=pltpu.PrefetchScalarGridSpec(
            num_scalar_prefetch=1,
            grid=(per,),
            in_specs=[here, here, here],
            out_specs=[
                pl.BlockSpec((1, streams, tokens, HEAD_DIM), lambda h, d: (h, 0, 0, 0)),
                pl.BlockSpec((1, tiles, BLOCK, BLOCK), lambda h, d: (h, 0, 0, 0)),
                pl.BlockSpec((members, tokens // members, HEAD_DIM), lambda h, d: (0, 0, h)),
            ],
            scratch_shapes=[pltpu.VMEM((streams, tokens + PAD, HEAD_DIM), jnp.float32)],
        ),
        out_shape=[
            pltpu.HBM((per, streams, tokens, HEAD_DIM), jnp.bfloat16),
            pltpu.HBM((per, tiles, BLOCK, BLOCK), jnp.float32),
            pltpu.HBM((members, tokens // members, width), jnp.bfloat16),
        ],
        compiler_params=room(FORE),
        cost_estimate=estimate(10_000_000_000, 8 * x.size),
        name="forward",
    )(docs, x, taps, before)


def backward_kernel(
    local, x_ref, before_ref, mixed_ref, prob_ref, att_ref, *refs
):
    *up_refs, cgrad_ref, extra_ref, up_ref = refs
    tp, owners, _, streams, rows, _ = x_ref.shape
    chunk = tp * rows
    tokens = owners * chunk
    per = att_ref.shape[1]
    head = pl.program_id(0)

    @pl.when(head == 0)
    def _():
        for step, piece_ref in enumerate(up_refs):
            up_ref[local[0] ^ step] = piece_ref[...]

    lanes = pl.ds(pl.multiple_of(head * HEAD_DIM, HEAD_DIM), HEAD_DIM)
    cgrad = cgrad_ref.at[head]
    edge = jnp.zeros((streams, PAD, HEAD_DIM), jnp.float32)
    cgrad[:, 0:PAD, :] = edge
    cgrad[:, PAD + tokens :, :] = edge
    starts = tile_starts(tokens)[0]
    for group, first in row_groups(tokens):
        own = slice(group[0] * BLOCK, (group[-1] + 1) * BLOCK)
        span = slice(first * BLOCK, own.stop)
        query, keys = mixed_ref[0, 0, own, :], mixed_ref[0, 1, span, :]
        ups = [
            up_ref[b * BLOCK // per, b * BLOCK % per : b * BLOCK % per + BLOCK, lanes]
            for b in group
        ]
        up = stacked(ups)
        dprob = dot(up, mixed_ref[0, 2, span, :], ((1,), (1,)))
        probs, dscores = [], []
        for n, block in enumerate(group):
            lowest, at = max(0, block - STEPS), block * BLOCK
            att = att_ref[at // per, at % per : at % per + BLOCK, :]
            delta = jnp.sum(
                ups[n].astype(jnp.float32) * att.astype(jnp.float32), axis=1, keepdims=True
            )
            tiles = [prob_ref[0, starts[block] + k] for k in range(block + 1 - lowest)]
            prob = jnp.concatenate(tiles, axis=1) if len(tiles) > 1 else tiles[0]
            mine = dprob[
                n * BLOCK : (n + 1) * BLOCK,
                (lowest - first) * BLOCK : (block + 1 - first) * BLOCK,
            ]
            dscore = (prob * (mine - delta) * SCALE).astype(jnp.bfloat16)
            dscores.append(widened(dscore, block, group, first))
            probs.append(widened(prob.astype(jnp.bfloat16), block, group, first))
        dscore = stacked(dscores)
        out = slice(PAD + own.start, PAD + own.stop)
        outs = slice(PAD + span.start, PAD + own.start)
        cgrad[0, out, :] = dot(dscore, keys, ((1,), (0,)))
        for m, part in (
            (1, dot(dscore, query, ((0,), (0,)))),
            (2, dot(stacked(probs), up, ((0,), (0,)))),
        ):
            if span.start < own.start:
                cgrad[m, outs, :] += part[: own.start - span.start]
            cgrad[m, out, :] = part[own.start - span.start :]
    extra_ref[:, 0:PAD, lanes] = cgrad[:, PAD : 2 * PAD, :]
    extra_ref[:, PAD + KW :, lanes] = edge[:, KW:]
    for m in range(streams):
        early = before_ref[m, :, lanes].astype(jnp.float32)
        sums = [early * cgrad[m, lag : lag + PAD, :] for lag in range(KW)]
        for c in range(owners):
            here = x_ref[:, c, 0, m].reshape(chunk, HEAD_DIM).astype(jnp.float32)
            for lag in range(KW):
                at = PAD + c * chunk + lag
                product = here * cgrad[m, at : at + chunk, :]
                sums[lag] = sums[lag] + jnp.sum(product.reshape(chunk // 8, 8, HEAD_DIM), axis=0)
        for lag in range(KW):
            extra_ref[m, PAD + lag : PAD + lag + 1, lanes] = jnp.sum(
                sums[lag], axis=0, keepdims=True
            )


def backward(local, x, before, mixed, prob, att, pieces):
    tp, members, slabs, streams, rows, wide = x.shape
    width = slabs * wide
    per, each = width // HEAD_DIM, wide // HEAD_DIM
    tokens = tp * members * rows
    tiles = prob.shape[1]
    here = pl.BlockSpec(memory_space=pltpu.VMEM)
    return pl.pallas_call(
        backward_kernel,
        grid_spec=pltpu.PrefetchScalarGridSpec(
            num_scalar_prefetch=1,
            grid=(per,),
            in_specs=[
                pl.BlockSpec(
                    (tp, members, 1, streams, rows, HEAD_DIM),
                    lambda h, p: (0, 0, h // each, 0, 0, h % each),
                ),
                here,
                pl.BlockSpec((1, streams, tokens, HEAD_DIM), lambda h, p: (h, 0, 0, 0)),
                pl.BlockSpec((1, tiles, BLOCK, BLOCK), lambda h, p: (h, 0, 0, 0)),
                pl.BlockSpec((members, tokens // members, HEAD_DIM), lambda h, p: (0, 0, h)),
            ]
            + [here] * members,
            out_specs=[here, here],
            scratch_shapes=[pltpu.VMEM((members, tokens // members, width), jnp.bfloat16)],
        ),
        out_shape=[
            jax.ShapeDtypeStruct((per, streams, tokens + 2 * PAD, HEAD_DIM), jnp.float32),
            jax.ShapeDtypeStruct((streams, 2 * PAD, width), jnp.float32),
        ],
        compiler_params=room(BACK),
        cost_estimate=estimate(20_000_000_000, 12 * x.size),
        name="backward",
    )(local, x, before, mixed, prob, att, *pieces)


def spread_kernel(cgrad_ref, taps_ref, grad_ref, tail_ref):
    tp, owners, _, streams, rows, _ = grad_ref.shape
    chunk = tp * rows
    head = pl.program_id(0)
    lanes = pl.ds(pl.multiple_of(head * HEAD_DIM, HEAD_DIM), HEAD_DIM)
    for m in range(streams):
        for c in range(owners):
            total = None
            for lag in range(KW):
                at = PAD + c * chunk + lag
                term = taps_ref[m, lag : lag + 1, lanes] * cgrad_ref[head, m, at : at + chunk, :]
                total = term if total is None else total + term
            grad_ref[:, c, 0, m] = total.astype(jnp.bfloat16).reshape(tp, rows, HEAD_DIM)
        tail_ref[m, :, lanes] = total[chunk - PAD :]


def spread(cgrad, taps, shape):
    tp, members, slabs, streams, rows, wide = shape
    each = wide // HEAD_DIM
    here = pl.BlockSpec(memory_space=pltpu.VMEM)
    return pl.pallas_call(
        spread_kernel,
        grid=(slabs * each,),
        in_specs=[here, here],
        out_specs=[
            pl.BlockSpec(
                (tp, members, 1, streams, rows, HEAD_DIM),
                lambda h: (0, 0, h // each, 0, 0, h % each),
            ),
            here,
        ],
        out_shape=[
            pltpu.HBM(shape, jnp.bfloat16),
            jax.ShapeDtypeStruct((streams, PAD, slabs * wide), jnp.float32),
        ],
        compiler_params=room(SPREAD),
        cost_estimate=estimate(2_000_000_000, 6 * cgrad.size),
        name="spread",
    )(cgrad, taps)


def swap(value, axes, groups):
    shape = value.shape
    return lax.all_to_all(
        value.reshape(shape[0], -1, shape[-1]),
        axes,
        split_axis=0,
        concat_axis=0,
        axis_index_groups=groups,
        tiled=True,
    ).reshape(shape)


def across(value, step):
    count = lax.axis_size("ctx")
    return lax.ppermute(value, "ctx", [(i, i ^ step) for i in range(count)])


def beside_neighbour(piece):
    other = across(piece, 1)
    even = lax.axis_index("ctx") % 2 == 0
    return jnp.concatenate(
        [jnp.where(even, piece, other), jnp.where(even, other, piece)], axis=-1
    )


def gather_columns(held, span, members):
    position = lax.axis_index("ctx").astype(jnp.int32)
    streams, taps, wide = held.shape
    steps = range(0, members, span)
    pieces = [across(held, step) if step else held for step in steps]

    def kernel(position_ref, *refs):
        o_ref = refs[-1]
        for step in steps:
            column = lax.rem(position_ref[0] ^ step, members) // span
            o_ref[:, :, pl.ds(pl.multiple_of(column * wide, wide), wide)] = refs[step // span][
                ...
            ].astype(jnp.float32)

    columns = members // span * wide
    return pl.pallas_call(
        kernel,
        grid_spec=pltpu.PrefetchScalarGridSpec(
            num_scalar_prefetch=1,
            grid=(1,),
            in_specs=[pl.BlockSpec((streams, taps, wide), lambda i, p: (0, 0, 0))] * len(pieces),
            out_specs=pl.BlockSpec((streams, taps, columns), lambda i, p: (0, 0, 0)),
        ),
        out_shape=jax.ShapeDtypeStruct((streams, taps, columns), jnp.float32),
        compiler_params=room(4),
        name="place_columns",
    )(position.reshape(1), *pieces)


def by_heads(parts, slabs, filters, doc_ids, upstream):
    count, tp = lax.axis_size("ctx"), lax.axis_size("tp")
    members = count // parts
    blocks, streams, rows, wide = slabs.shape
    width = parts * wide
    position = lax.axis_index("ctx")
    groups = [
        [(p * members + c) * tp + t for t in range(tp) for c in range(members)]
        for p in range(parts)
    ]
    every = [[p * members + c for c in range(members)] for p in range(parts)]
    if parts > 1:
        docs = doc_ids.shape[0] // parts
        doc_ids = lax.dynamic_slice_in_dim(doc_ids, position // members * docs, docs)
    shape = (tp, members, parts, streams, rows, wide)
    x = swap(slabs.reshape(tp * members, -1, wide), AXES, groups).reshape(shape)
    local = (position % members).astype(jnp.int32).reshape(1)
    pieces = split_rows(upstream, members, local)
    pieces = [across(piece, step) if step else piece for step, piece in enumerate(pieces)]
    taps = lax.dynamic_slice_in_dim(filters, position % members * width, width, 2)
    if parts > 1:
        upward = [(i, i + members) for i in range(count - members)]
        last = jnp.transpose(x[-1, -1, :, :, rows - PAD :], (1, 2, 0, 3))
        before = lax.ppermute(last.reshape(streams, PAD, width), "ctx", upward)
    else:
        before = jnp.zeros((streams, PAD, width), x.dtype)
    mixed, prob, att = forward(doc_ids, x, taps, before, members)
    attended = join_columns(swap(att, "ctx", every)[:, None])[0]
    away = [pltpu.with_memory_space_constraint(v, pltpu.HBM) for v in (mixed, prob, att)]
    cgrad, extra = backward(local, x, before, *away, pieces)
    if parts > 1:
        other = across(extra, members)
        span, held = 1, (extra + other)[:, PAD : PAD + KW].astype(jnp.bfloat16)
    else:
        span, held = 2, beside_neighbour(extra[:, PAD : PAD + KW].astype(jnp.bfloat16))
    grad, tail = spread(cgrad, taps, shape)
    if parts > 1:
        after = jnp.where(position < members, other[:, 0:PAD], 0.0)
        after = jnp.concatenate([jnp.zeros_like(after), after], axis=1)
        for lag in range(KW):
            tail = tail + taps[:, lag : lag + 1] * after[:, lag : lag + PAD]
        tail = tail.astype(grad.dtype).reshape(streams, PAD, parts, wide)
        grad = grad.at[-1, -1, :, :, rows - PAD :].set(jnp.transpose(tail, (2, 0, 1, 3)))
    grad, held = lax.optimization_barrier((grad, held))
    held, attended = lax.optimization_barrier((held, attended))
    filter_grad = gather_columns(held, span, members)
    grad = swap(grad.reshape(tp * members, -1, wide), AXES, groups)
    qkv_grad = join_columns(grad.reshape(slabs.shape))
    return attended, jnp.transpose(qkv_grad, (1, 0, 2)), filter_grad


def from_behind(value, axis, steps):
    count = lax.axis_size(axis)
    first, last = (max(0, -steps), min(count, count - steps))
    return lax.ppermute(value, axis, [(source, source + steps) for source in range(first, last)])


def block_docs(doc_ids, first_block, count):
    start = jnp.maximum(first_block, 0)
    picked = lax.dynamic_slice_in_dim(doc_ids, start, count)
    return jnp.repeat(picked, BLOCK)


def by_ring(qkv, filters, doc_ids, upstream):
    local = lax.all_to_all(qkv, "tp", split_axis=2, concat_axis=0, tiled=True)
    tokens = local.shape[0]
    width = local.shape[2]
    heads = width // HEAD_DIM
    blocks_here = tokens // BLOCK
    logit_scale = HEAD_DIM ** (-0.5)
    position = lax.axis_index("ctx")
    reach = STEPS + 1
    rim = from_behind(local[tokens - (KW - 1) :], "ctx", 1)
    inputs = jnp.concatenate([rim, local], axis=0).astype(jnp.float32)
    mixed = sum(
        (filters[:, lag, :] * inputs[KW - 1 - lag : KW - 1 - lag + tokens] for lag in range(KW))
    )
    mixed = mixed.astype(jnp.bfloat16)
    queries = mixed[:, 0].reshape(tokens, heads, HEAD_DIM)
    key_value = mixed[:, 1:3]
    tiles = [key_value]
    current = key_value
    for distance in range(1, STEPS + 1):
        current = from_behind(current, "ctx", 1)
        tiles.append(current)
    joined = jnp.concatenate(tiles, axis=0)
    keys = joined[:, 0].reshape(reach * tokens, heads, HEAD_DIM)
    values = joined[:, 1].reshape(reach * tokens, heads, HEAD_DIM)
    rows = jnp.arange(tokens)
    query_token = position * tokens + rows
    query_doc = block_docs(doc_ids, position * blocks_here, blocks_here)
    key_tokens = jnp.concatenate(
        [(position - distance) * tokens + rows for distance in range(reach)]
    )
    key_docs = jnp.concatenate(
        [
            block_docs(doc_ids, (position - distance) * blocks_here, blocks_here)
            for distance in range(reach)
        ]
    )
    allowed = (
        (key_tokens[None, :] >= 0)
        & (key_tokens[None, :] <= query_token[:, None])
        & (key_docs[None, :] == query_doc[:, None])
    )
    raw = (
        jnp.einsum("qhd,khd->hqk", queries, keys, preferred_element_type=jnp.float32) * logit_scale
    )
    masked = jnp.where(allowed[None], raw, -1e30)
    row_max = masked.max(axis=2)
    expo = jnp.where(allowed[None], jnp.exp(masked - row_max[:, :, None]), 0.0)
    row_sum = expo.sum(axis=2)
    weighted_values = jnp.einsum(
        "hqk,khd->qhd", expo.astype(jnp.bfloat16), values, preferred_element_type=jnp.float32
    )
    attended = (weighted_values / row_sum.T[:, :, None]).astype(jnp.bfloat16)
    grad_out = upstream.reshape(tokens, heads, HEAD_DIM)
    delta = jnp.sum(grad_out.astype(jnp.float32) * attended.astype(jnp.float32), axis=-1).T
    prob = expo / row_sum[:, :, None]
    value_part = jnp.einsum(
        "hqk,qhd->khd", prob.astype(jnp.bfloat16), grad_out, preferred_element_type=jnp.float32
    )
    probability_gradient = jnp.einsum(
        "qhd,khd->hqk", grad_out, values, preferred_element_type=jnp.float32
    )
    score_gradient = (prob * (probability_gradient - delta[:, :, None]) * logit_scale).astype(
        jnp.bfloat16
    )
    query_gradient_rows = jnp.einsum(
        "hqk,khd->qhd", score_gradient, keys, preferred_element_type=jnp.float32
    )
    key_part = jnp.einsum(
        "hqk,qhd->khd", score_gradient, queries, preferred_element_type=jnp.float32
    )
    stacked = jnp.stack(
        [key_part.reshape(reach, tokens, width), value_part.reshape(reach, tokens, width)], axis=2
    )
    partials = [stacked[distance] for distance in range(reach)]
    carried = partials[STEPS]
    for distance in range(STEPS - 1, -1, -1):
        carried = from_behind(carried, "ctx", -1)
        carried = carried + partials[distance]
    conv_grad = jnp.concatenate([query_gradient_rows.reshape(tokens, 1, width), carried], axis=1)
    grad_edge = from_behind(conv_grad[: KW - 1], "ctx", -1)
    extended = jnp.concatenate([conv_grad, grad_edge], axis=0)
    input_grad = sum((filters[:, lag, :] * extended[lag : lag + tokens] for lag in range(KW)))
    tap_terms = jnp.stack(
        [
            jnp.sum(inputs[KW - 1 - lag : KW - 1 - lag + tokens] * conv_grad, axis=0)
            for lag in range(KW)
        ],
        axis=1,
    )
    filter_grad = lax.psum(tap_terms, "ctx")
    qkv_grad = lax.all_to_all(
        input_grad.astype(jnp.bfloat16), "tp", split_axis=0, concat_axis=2, tiled=True
    )
    return (attended.reshape(tokens, width), qkv_grad, filter_grad)


def solution(mesh):
    count = mesh.shape["ctx"]

    def shards(qkv, filters, doc_ids, upstream):
        tokens, width = upstream.shape
        heads = width // HEAD_DIM
        even = tokens % BLOCK == 0 and qkv.shape[0] % PAD == 0 and count & (count - 1) == 0
        if heads % count or not even or count < 4:
            return by_ring(qkv, filters, doc_ids, upstream)
        slabs, apart = split_columns(doc_ids, jnp.transpose(qkv, (1, 0, 2)), width // count)
        forms = [functools.partial(by_heads, parts) for parts in (1, 2)]
        return lax.switch(apart[0], forms, slabs, filters, doc_ids, upstream)

    return jax.shard_map(
        shards,
        mesh=mesh,
        in_specs=(P(("ctx", "tp"), None, None), P(None, None, "tp"), P(), P("ctx", "tp")),
        out_specs=(P("ctx", "tp"), P(("ctx", "tp"), None, None), P(None, None, "tp")),
        check_vma=False,
    )
```

```python
import functools
import math

import jax
import jax.numpy as jnp
from jax import lax
from jax.experimental import pallas as pl
from jax.experimental.pallas import tpu as pltpu
from jax.sharding import PartitionSpec as P

HEAD_DIM = 128
KW = 7
BLOCK = 128
STEPS = 4
PAD = 8
SCALE = HEAD_DIM ** (-0.5)
SCALE_LOG2 = SCALE * math.log2(math.e)
AXES = ("ctx", "tp")
FORE, BACK, SPREAD = 24, 24, 16


def dot(a, b, dims):
    return lax.dot_general(a, b, (dims, ((), ())), preferred_element_type=jnp.float32)


def room(mebibytes):
    return pltpu.CompilerParams(vmem_limit_bytes=mebibytes << 20)


def estimate(flops, moved):
    return pl.CostEstimate(flops=flops, bytes_accessed=moved, transcendentals=0)


def split_columns(docs, x, width):
    streams, rows, channels = x.shape
    count = channels // width
    steps = 2 if count % 2 == 0 else 1
    part = count // steps
    middle = docs.shape[0] // 2

    def kernel(docs_ref, x_ref, o_ref, apart_ref):
        apart_ref[0] = (docs_ref[middle - 1] != docs_ref[middle]).astype(jnp.int32)
        for n in range(part):
            o_ref[n] = x_ref[:, :, n * width : (n + 1) * width]

    return pl.pallas_call(
        kernel,
        grid_spec=pltpu.PrefetchScalarGridSpec(
            num_scalar_prefetch=1,
            grid=(steps,),
            in_specs=[pl.BlockSpec((streams, rows, part * width), lambda i, d: (0, 0, i))],
            out_specs=[
                pl.BlockSpec((part, streams, rows, width), lambda i, d: (i, 0, 0, 0)),
                pl.BlockSpec(memory_space=pltpu.SMEM),
            ],
        ),
        out_shape=[
            jax.ShapeDtypeStruct((count, streams, rows, width), x.dtype),
            jax.ShapeDtypeStruct((1,), jnp.int32),
        ],
        compiler_params=room(60),
        cost_estimate=estimate(0, 4 * x.size),
        name="split_columns",
    )(docs, x)


def split_rows(x, members, local):
    tokens, channels = x.shape
    width = channels // members

    def kernel(local_ref, x_ref, *o_refs):
        for step in range(members):
            at = pl.multiple_of((local_ref[0] ^ step) * width, width)
            o_refs[step][...] = x_ref[:, pl.ds(at, width)]

    piece = pl.BlockSpec((tokens, width), lambda i, p: (0, 0))
    return pl.pallas_call(
        kernel,
        grid_spec=pltpu.PrefetchScalarGridSpec(
            num_scalar_prefetch=1,
            grid=(1,),
            in_specs=[pl.BlockSpec((tokens, channels), lambda i, p: (0, 0))],
            out_specs=[piece] * members,
        ),
        out_shape=[jax.ShapeDtypeStruct((tokens, width), x.dtype)] * members,
        compiler_params=room(10),
        cost_estimate=estimate(0, 4 * x.size),
        name="split_rows",
    )(local, x)


def join_columns(x):
    count, streams, rows, width = x.shape
    steps = 2 if count % 2 == 0 else 1
    part = count // steps

    def kernel(x_ref, o_ref):
        for n in range(part):
            o_ref[:, :, n * width : (n + 1) * width] = x_ref[pl.program_id(0) * part + n]

    return pl.pallas_call(
        kernel,
        grid=(steps,),
        in_specs=[pl.BlockSpec(memory_space=pltpu.VMEM)],
        out_specs=pl.BlockSpec((streams, rows, part * width), lambda i: (0, 0, i)),
        out_shape=pltpu.HBM((streams, rows, count * width), x.dtype),
        compiler_params=room(10),
        cost_estimate=estimate(0, 4 * x.size),
        name="join_columns",
    )(x)


def tile_starts(tokens):
    starts, total = [], 0
    for block in range(tokens // BLOCK):
        starts.append(total)
        total += block + 1 - max(0, block - STEPS)
    return starts, total


def row_groups(tokens):
    blocks = tokens // BLOCK
    size = 2 if blocks % 2 == 0 else 1
    for start in range(0, blocks, size):
        yield range(start, start + size), max(0, start - STEPS)


def widened(value, block, group, first):
    before = (max(0, block - STEPS) - first) * BLOCK
    behind = (group[-1] - block) * BLOCK
    parts = [jnp.zeros((BLOCK, before), value.dtype)] if before else []
    parts.append(value)
    if behind:
        parts.append(jnp.zeros((BLOCK, behind), value.dtype))
    return jnp.concatenate(parts, axis=1) if len(parts) > 1 else value


def stacked(parts):
    return jnp.concatenate(parts, axis=0) if len(parts) > 1 else parts[0]


def forward_kernel(docs, x_ref, taps_ref, before_ref, mixed_ref, prob_ref, out_ref, padded):
    tp, owners, _, streams, rows, wide = x_ref.shape
    chunk = tp * rows
    tokens = owners * chunk
    head = pl.program_id(0)
    lanes = pl.ds(pl.multiple_of(head * HEAD_DIM, HEAD_DIM), HEAD_DIM)
    each = wide // HEAD_DIM
    slab = head // each
    inner = pl.ds(pl.multiple_of(head % each * HEAD_DIM, HEAD_DIM), HEAD_DIM)
    padded[:, 0:PAD, :] = before_ref[:, :, lanes].astype(jnp.float32)
    for m in range(streams):
        for c in range(owners):
            mine = x_ref[:, c, slab, m, :, inner].reshape(chunk, HEAD_DIM)
            padded[m, PAD + c * chunk : PAD + (c + 1) * chunk, :] = mine.astype(jnp.float32)
    for m in range(streams):
        for start in range(0, tokens, BLOCK):
            total = None
            for lag in range(KW):
                at = PAD + start - lag
                term = taps_ref[m, lag : lag + 1, lanes] * padded[m, at : at + BLOCK, :]
                total = term if total is None else total + term
            mixed_ref[0, m, start : start + BLOCK, :] = total.astype(jnp.bfloat16)
    below = lax.broadcasted_iota(jnp.int32, (BLOCK, BLOCK), 0) >= lax.broadcasted_iota(
        jnp.int32, (BLOCK, BLOCK), 1
    )
    starts = tile_starts(tokens)[0]
    for group, first in row_groups(tokens):
        own = slice(group[0] * BLOCK, (group[-1] + 1) * BLOCK)
        span = slice(first * BLOCK, own.stop)
        raw = dot(mixed_ref[0, 0, own, :], mixed_ref[0, 1, span, :], ((1,), (1,)))
        sheets, inverses = [], []
        for block in group:
            lowest = max(0, block - STEPS)
            mine = raw[(block - group[0]) * BLOCK : (block - group[0] + 1) * BLOCK]
            parts = []
            for other in range(lowest, block + 1):
                part = mine[:, (other - first) * BLOCK : (other - first + 1) * BLOCK]
                allowed = below if other == block else docs[other] == docs[block]
                parts.append(jnp.where(allowed, part, -1e30))
            masked = jnp.concatenate(parts, axis=1) if len(parts) > 1 else parts[0]
            expo = jnp.exp2((masked - jnp.max(masked, axis=1, keepdims=True)) * SCALE_LOG2)
            inverses.append(1.0 / jnp.sum(expo, axis=1, keepdims=True))
            sheets.append(widened(expo.astype(jnp.bfloat16), block, group, first))
            prob = expo * inverses[-1]
            for n in range(block + 1 - lowest):
                prob_ref[0, starts[block] + n] = prob[:, n * BLOCK : (n + 1) * BLOCK]
        total = dot(stacked(sheets), mixed_ref[0, 2, span, :], ((1,), (0,)))
        per = out_ref.shape[1]
        for n, block in enumerate(group):
            at = block * BLOCK
            out_ref[at // per, at % per : at % per + BLOCK, :] = (
                total[n * BLOCK : (n + 1) * BLOCK] * inverses[n]
            ).astype(jnp.bfloat16)


def forward(docs, x, taps, before, members):
    tp, _, slabs, streams, rows, wide = x.shape
    width = slabs * wide
    per = width // HEAD_DIM
    tokens = tp * members * rows
    tiles = tile_starts(tokens)[1]
    here = pl.BlockSpec(memory_space=pltpu.VMEM)
    return pl.pallas_call(
        forward_kernel,
        grid_spec=pltpu.PrefetchScalarGridSpec(
            num_scalar_prefetch=1,
            grid=(per,),
            in_specs=[here, here, here],
            out_specs=[
                pl.BlockSpec((1, streams, tokens, HEAD_DIM), lambda h, d: (h, 0, 0, 0)),
                pl.BlockSpec((1, tiles, BLOCK, BLOCK), lambda h, d: (h, 0, 0, 0)),
                pl.BlockSpec((members, tokens // members, HEAD_DIM), lambda h, d: (0, 0, h)),
            ],
            scratch_shapes=[pltpu.VMEM((streams, tokens + PAD, HEAD_DIM), jnp.float32)],
        ),
        out_shape=[
            pltpu.HBM((per, streams, tokens, HEAD_DIM), jnp.bfloat16),
            pltpu.HBM((per, tiles, BLOCK, BLOCK), jnp.float32),
            pltpu.HBM((members, tokens // members, width), jnp.bfloat16),
        ],
        compiler_params=room(FORE),
        cost_estimate=estimate(10_000_000_000, 8 * x.size),
        name="forward",
    )(docs, x, taps, before)


def backward_kernel(
    local, x_ref, before_ref, mixed_ref, prob_ref, att_ref, *refs
):
    *up_refs, cgrad_ref, extra_ref, up_ref, extra = refs
    tp, owners, _, streams, rows, _ = x_ref.shape
    chunk = tp * rows
    tokens = owners * chunk
    per = att_ref.shape[1]
    head = pl.program_id(0)

    @pl.when(head == 0)
    def _():
        for step, piece_ref in enumerate(up_refs):
            up_ref[local[0] ^ step] = piece_ref[...]

    lanes = pl.ds(pl.multiple_of(head * HEAD_DIM, HEAD_DIM), HEAD_DIM)
    cgrad = cgrad_ref.at[head]
    edge = jnp.zeros((streams, PAD, HEAD_DIM), jnp.float32)
    cgrad[:, 0:PAD, :] = edge
    cgrad[:, PAD + tokens :, :] = edge
    starts = tile_starts(tokens)[0]
    for group, first in row_groups(tokens):
        own = slice(group[0] * BLOCK, (group[-1] + 1) * BLOCK)
        span = slice(first * BLOCK, own.stop)
        query, keys = mixed_ref[0, 0, own, :], mixed_ref[0, 1, span, :]
        ups = [
            up_ref[b * BLOCK // per, b * BLOCK % per : b * BLOCK % per + BLOCK, lanes]
            for b in group
        ]
        up = stacked(ups)
        dprob = dot(up, mixed_ref[0, 2, span, :], ((1,), (1,)))
        probs, dscores = [], []
        for n, block in enumerate(group):
            lowest, at = max(0, block - STEPS), block * BLOCK
            att = att_ref[at // per, at % per : at % per + BLOCK, :]
            delta = jnp.sum(
                ups[n].astype(jnp.float32) * att.astype(jnp.float32), axis=1, keepdims=True
            )
            tiles = [prob_ref[0, starts[block] + k] for k in range(block + 1 - lowest)]
            prob = jnp.concatenate(tiles, axis=1) if len(tiles) > 1 else tiles[0]
            mine = dprob[
                n * BLOCK : (n + 1) * BLOCK,
                (lowest - first) * BLOCK : (block + 1 - first) * BLOCK,
            ]
            dscore = (prob * (mine - delta) * SCALE).astype(jnp.bfloat16)
            dscores.append(widened(dscore, block, group, first))
            probs.append(widened(prob.astype(jnp.bfloat16), block, group, first))
        dscore = stacked(dscores)
        out = slice(PAD + own.start, PAD + own.stop)
        outs = slice(PAD + span.start, PAD + own.start)
        cgrad[0, out, :] = dot(dscore, keys, ((1,), (0,)))
        for m, part in (
            (1, dot(dscore, query, ((0,), (0,)))),
            (2, dot(stacked(probs), up, ((0,), (0,)))),
        ):
            if span.start < own.start:
                cgrad[m, outs, :] += part[: own.start - span.start]
            cgrad[m, out, :] = part[own.start - span.start :]
    extra[:, 0:PAD, :] = cgrad[:, PAD : 2 * PAD, :]
    extra[:, PAD + KW :, :] = edge[:, KW:]
    for m in range(streams):
        early = before_ref[m, :, lanes].astype(jnp.float32)
        sums = [early * cgrad[m, lag : lag + PAD, :] for lag in range(KW)]
        for c in range(owners):
            here = x_ref[:, c, 0, m].reshape(chunk, HEAD_DIM).astype(jnp.float32)
            for lag in range(KW):
                at = PAD + c * chunk + lag
                product = here * cgrad[m, at : at + chunk, :]
                sums[lag] = sums[lag] + jnp.sum(product.reshape(chunk // 8, 8, HEAD_DIM), axis=0)
        for lag in range(KW):
            extra[m, PAD + lag : PAD + lag + 1, :] = jnp.sum(sums[lag], axis=0, keepdims=True)
    extra_ref[:, :, lanes] = extra[...].astype(jnp.bfloat16)


def backward(local, x, before, mixed, prob, att, pieces):
    tp, members, slabs, streams, rows, wide = x.shape
    width = slabs * wide
    per, each = width // HEAD_DIM, wide // HEAD_DIM
    tokens = tp * members * rows
    tiles = prob.shape[1]
    here = pl.BlockSpec(memory_space=pltpu.VMEM)
    return pl.pallas_call(
        backward_kernel,
        grid_spec=pltpu.PrefetchScalarGridSpec(
            num_scalar_prefetch=1,
            grid=(per,),
            in_specs=[
                pl.BlockSpec(
                    (tp, members, 1, streams, rows, HEAD_DIM),
                    lambda h, p: (0, 0, h // each, 0, 0, h % each),
                ),
                here,
                pl.BlockSpec((1, streams, tokens, HEAD_DIM), lambda h, p: (h, 0, 0, 0)),
                pl.BlockSpec((1, tiles, BLOCK, BLOCK), lambda h, p: (h, 0, 0, 0)),
                pl.BlockSpec((members, tokens // members, HEAD_DIM), lambda h, p: (0, 0, h)),
            ]
            + [here] * members,
            out_specs=[here, here],
            scratch_shapes=[
                pltpu.VMEM((members, tokens // members, width), jnp.bfloat16),
                pltpu.VMEM((streams, 2 * PAD, HEAD_DIM), jnp.float32),
            ],
        ),
        out_shape=[
            jax.ShapeDtypeStruct((per, streams, tokens + 2 * PAD, HEAD_DIM), jnp.float32),
            jax.ShapeDtypeStruct((streams, 2 * PAD, width), jnp.bfloat16),
        ],
        compiler_params=room(BACK),
        cost_estimate=estimate(20_000_000_000, 12 * x.size),
        name="backward",
    )(local, x, before, mixed, prob, att, *pieces)


def spread_kernel(cgrad_ref, taps_ref, grad_ref, tail_ref):
    tp, owners, _, streams, rows, _ = grad_ref.shape
    chunk = tp * rows
    head = pl.program_id(0)
    lanes = pl.ds(pl.multiple_of(head * HEAD_DIM, HEAD_DIM), HEAD_DIM)
    for m in range(streams):
        for c in range(owners):
            total = None
            for lag in range(KW):
                at = PAD + c * chunk + lag
                term = taps_ref[m, lag : lag + 1, lanes] * cgrad_ref[head, m, at : at + chunk, :]
                total = term if total is None else total + term
            grad_ref[:, c, 0, m] = total.astype(jnp.bfloat16).reshape(tp, rows, HEAD_DIM)
        tail_ref[m, :, lanes] = total[chunk - PAD :]


def spread(cgrad, taps, shape):
    tp, members, slabs, streams, rows, wide = shape
    each = wide // HEAD_DIM
    here = pl.BlockSpec(memory_space=pltpu.VMEM)
    return pl.pallas_call(
        spread_kernel,
        grid=(slabs * each,),
        in_specs=[here, here],
        out_specs=[
            pl.BlockSpec(
                (tp, members, 1, streams, rows, HEAD_DIM),
                lambda h: (0, 0, h // each, 0, 0, h % each),
            ),
            here,
        ],
        out_shape=[
            pltpu.HBM(shape, jnp.bfloat16),
            jax.ShapeDtypeStruct((streams, PAD, slabs * wide), jnp.float32),
        ],
        compiler_params=room(SPREAD),
        cost_estimate=estimate(2_000_000_000, 6 * cgrad.size),
        name="spread",
    )(cgrad, taps)


def swap(value, axes, groups):
    shape = value.shape
    return lax.all_to_all(
        value.reshape(shape[0], -1, shape[-1]),
        axes,
        split_axis=0,
        concat_axis=0,
        axis_index_groups=groups,
        tiled=True,
    ).reshape(shape)


def across(value, step):
    count = lax.axis_size("ctx")
    return lax.ppermute(value, "ctx", [(i, i ^ step) for i in range(count)])


def beside_neighbour(piece):
    other = across(piece, 1)
    even = lax.axis_index("ctx") % 2 == 0
    return jnp.concatenate(
        [jnp.where(even, piece, other), jnp.where(even, other, piece)], axis=-1
    )


def gather_columns(held, span, members):
    position = lax.axis_index("ctx").astype(jnp.int32)
    streams, taps, wide = held.shape
    steps = range(0, members, span)
    pieces = [across(held, step) if step else held for step in steps]

    def kernel(position_ref, *refs):
        o_ref = refs[-1]
        for step in steps:
            column = lax.rem(position_ref[0] ^ step, members) // span
            o_ref[:, :, pl.ds(pl.multiple_of(column * wide, wide), wide)] = refs[step // span][
                ...
            ].astype(jnp.float32)

    columns = members // span * wide
    return pl.pallas_call(
        kernel,
        grid_spec=pltpu.PrefetchScalarGridSpec(
            num_scalar_prefetch=1,
            grid=(1,),
            in_specs=[pl.BlockSpec((streams, taps, wide), lambda i, p: (0, 0, 0))] * len(pieces),
            out_specs=pl.BlockSpec((streams, taps, columns), lambda i, p: (0, 0, 0)),
        ),
        out_shape=jax.ShapeDtypeStruct((streams, taps, columns), jnp.float32),
        compiler_params=room(4),
        name="place_columns",
    )(position.reshape(1), *pieces)


def by_heads(parts, slabs, filters, doc_ids, upstream):
    count, tp = lax.axis_size("ctx"), lax.axis_size("tp")
    members = count // parts
    blocks, streams, rows, wide = slabs.shape
    width = parts * wide
    position = lax.axis_index("ctx")
    groups = [
        [(p * members + c) * tp + t for t in range(tp) for c in range(members)]
        for p in range(parts)
    ]
    every = [[p * members + c for c in range(members)] for p in range(parts)]
    if parts > 1:
        docs = doc_ids.shape[0] // parts
        doc_ids = lax.dynamic_slice_in_dim(doc_ids, position // members * docs, docs)
    shape = (tp, members, parts, streams, rows, wide)
    x = swap(slabs.reshape(tp * members, -1, wide), AXES, groups).reshape(shape)
    local = (position % members).astype(jnp.int32).reshape(1)
    pieces = split_rows(upstream, members, local)
    pieces = [across(piece, step) if step else piece for step, piece in enumerate(pieces)]
    taps = lax.dynamic_slice_in_dim(filters, position % members * width, width, 2)
    if parts > 1:
        upward = [(i, i + members) for i in range(count - members)]
        last = jnp.transpose(x[-1, -1, :, :, rows - PAD :], (1, 2, 0, 3))
        before = lax.ppermute(last.reshape(streams, PAD, width), "ctx", upward)
    else:
        before = jnp.zeros((streams, PAD, width), x.dtype)
    mixed, prob, att = forward(doc_ids, x, taps, before, members)
    attended = join_columns(swap(att, "ctx", every)[:, None])[0]
    away = [pltpu.with_memory_space_constraint(v, pltpu.HBM) for v in (mixed, prob, att)]
    cgrad, extra = backward(local, x, before, *away, pieces)
    if parts > 1:
        other = across(extra, members)
        both = extra.astype(jnp.float32) + other.astype(jnp.float32)
        span, held = 1, both[:, PAD : PAD + KW].astype(jnp.bfloat16)
    else:
        span, held = 2, beside_neighbour(extra[:, PAD : PAD + KW])
    grad, tail = spread(cgrad, taps, shape)
    if parts > 1:
        after = jnp.where(position < members, other[:, 0:PAD].astype(jnp.float32), 0.0)
        after = jnp.concatenate([jnp.zeros_like(after), after], axis=1)
        for lag in range(KW):
            tail = tail + taps[:, lag : lag + 1] * after[:, lag : lag + PAD]
        tail = tail.astype(grad.dtype).reshape(streams, PAD, parts, wide)
        grad = grad.at[-1, -1, :, :, rows - PAD :].set(jnp.transpose(tail, (2, 0, 1, 3)))
    grad, held = lax.optimization_barrier((grad, held))
    held, attended = lax.optimization_barrier((held, attended))
    filter_grad = gather_columns(held, span, members)
    grad = swap(grad.reshape(tp * members, -1, wide), AXES, groups)
    qkv_grad = join_columns(grad.reshape(slabs.shape))
    return attended, jnp.transpose(qkv_grad, (1, 0, 2)), filter_grad


def from_behind(value, axis, steps):
    count = lax.axis_size(axis)
    first, last = (max(0, -steps), min(count, count - steps))
    return lax.ppermute(value, axis, [(source, source + steps) for source in range(first, last)])


def block_docs(doc_ids, first_block, count):
    start = jnp.maximum(first_block, 0)
    picked = lax.dynamic_slice_in_dim(doc_ids, start, count)
    return jnp.repeat(picked, BLOCK)


def by_ring(qkv, filters, doc_ids, upstream):
    local = lax.all_to_all(qkv, "tp", split_axis=2, concat_axis=0, tiled=True)
    tokens = local.shape[0]
    width = local.shape[2]
    heads = width // HEAD_DIM
    blocks_here = tokens // BLOCK
    logit_scale = HEAD_DIM ** (-0.5)
    position = lax.axis_index("ctx")
    reach = STEPS + 1
    rim = from_behind(local[tokens - (KW - 1) :], "ctx", 1)
    inputs = jnp.concatenate([rim, local], axis=0).astype(jnp.float32)
    mixed = sum(
        (filters[:, lag, :] * inputs[KW - 1 - lag : KW - 1 - lag + tokens] for lag in range(KW))
    )
    mixed = mixed.astype(jnp.bfloat16)
    queries = mixed[:, 0].reshape(tokens, heads, HEAD_DIM)
    key_value = mixed[:, 1:3]
    tiles = [key_value]
    current = key_value
    for distance in range(1, STEPS + 1):
        current = from_behind(current, "ctx", 1)
        tiles.append(current)
    joined = jnp.concatenate(tiles, axis=0)
    keys = joined[:, 0].reshape(reach * tokens, heads, HEAD_DIM)
    values = joined[:, 1].reshape(reach * tokens, heads, HEAD_DIM)
    rows = jnp.arange(tokens)
    query_token = position * tokens + rows
    query_doc = block_docs(doc_ids, position * blocks_here, blocks_here)
    key_tokens = jnp.concatenate(
        [(position - distance) * tokens + rows for distance in range(reach)]
    )
    key_docs = jnp.concatenate(
        [
            block_docs(doc_ids, (position - distance) * blocks_here, blocks_here)
            for distance in range(reach)
        ]
    )
    allowed = (
        (key_tokens[None, :] >= 0)
        & (key_tokens[None, :] <= query_token[:, None])
        & (key_docs[None, :] == query_doc[:, None])
    )
    raw = (
        jnp.einsum("qhd,khd->hqk", queries, keys, preferred_element_type=jnp.float32) * logit_scale
    )
    masked = jnp.where(allowed[None], raw, -1e30)
    row_max = masked.max(axis=2)
    expo = jnp.where(allowed[None], jnp.exp(masked - row_max[:, :, None]), 0.0)
    row_sum = expo.sum(axis=2)
    weighted_values = jnp.einsum(
        "hqk,khd->qhd", expo.astype(jnp.bfloat16), values, preferred_element_type=jnp.float32
    )
    attended = (weighted_values / row_sum.T[:, :, None]).astype(jnp.bfloat16)
    grad_out = upstream.reshape(tokens, heads, HEAD_DIM)
    delta = jnp.sum(grad_out.astype(jnp.float32) * attended.astype(jnp.float32), axis=-1).T
    prob = expo / row_sum[:, :, None]
    value_part = jnp.einsum(
        "hqk,qhd->khd", prob.astype(jnp.bfloat16), grad_out, preferred_element_type=jnp.float32
    )
    probability_gradient = jnp.einsum(
        "qhd,khd->hqk", grad_out, values, preferred_element_type=jnp.float32
    )
    score_gradient = (prob * (probability_gradient - delta[:, :, None]) * logit_scale).astype(
        jnp.bfloat16
    )
    query_gradient_rows = jnp.einsum(
        "hqk,khd->qhd", score_gradient, keys, preferred_element_type=jnp.float32
    )
    key_part = jnp.einsum(
        "hqk,qhd->khd", score_gradient, queries, preferred_element_type=jnp.float32
    )
    stacked = jnp.stack(
        [key_part.reshape(reach, tokens, width), value_part.reshape(reach, tokens, width)], axis=2
    )
    partials = [stacked[distance] for distance in range(reach)]
    carried = partials[STEPS]
    for distance in range(STEPS - 1, -1, -1):
        carried = from_behind(carried, "ctx", -1)
        carried = carried + partials[distance]
    conv_grad = jnp.concatenate([query_gradient_rows.reshape(tokens, 1, width), carried], axis=1)
    grad_edge = from_behind(conv_grad[: KW - 1], "ctx", -1)
    extended = jnp.concatenate([conv_grad, grad_edge], axis=0)
    input_grad = sum((filters[:, lag, :] * extended[lag : lag + tokens] for lag in range(KW)))
    tap_terms = jnp.stack(
        [
            jnp.sum(inputs[KW - 1 - lag : KW - 1 - lag + tokens] * conv_grad, axis=0)
            for lag in range(KW)
        ],
        axis=1,
    )
    filter_grad = lax.psum(tap_terms, "ctx")
    qkv_grad = lax.all_to_all(
        input_grad.astype(jnp.bfloat16), "tp", split_axis=0, concat_axis=2, tiled=True
    )
    return (attended.reshape(tokens, width), qkv_grad, filter_grad)


def solution(mesh):
    count = mesh.shape["ctx"]

    def shards(qkv, filters, doc_ids, upstream):
        tokens, width = upstream.shape
        heads = width // HEAD_DIM
        even = tokens % BLOCK == 0 and qkv.shape[0] % PAD == 0 and count & (count - 1) == 0
        if heads % count or not even or count < 4:
            return by_ring(qkv, filters, doc_ids, upstream)
        slabs, apart = split_columns(doc_ids, jnp.transpose(qkv, (1, 0, 2)), width // count)
        forms = [functools.partial(by_heads, parts) for parts in (1, 2)]
        return lax.switch(apart[0], forms, slabs, filters, doc_ids, upstream)

    return jax.shard_map(
        shards,
        mesh=mesh,
        in_specs=(P(("ctx", "tp"), None, None), P(None, None, "tp"), P(), P("ctx", "tp")),
        out_specs=(P("ctx", "tp"), P(("ctx", "tp"), None, None), P(None, None, "tp")),
        check_vma=False,
    )
```

```python
import functools
import math

import jax
import jax.numpy as jnp
from jax import lax
from jax.experimental import pallas as pl
from jax.experimental.pallas import tpu as pltpu
from jax.sharding import PartitionSpec as P

HEAD_DIM = 128
KW = 7
BLOCK = 128
STEPS = 4
PAD = 8
SCALE = HEAD_DIM ** (-0.5)
SCALE_LOG2 = SCALE * math.log2(math.e)
AXES = ("ctx", "tp")
FORE, BACK, SPREAD = 24, 24, 16


def dot(a, b, dims):
    return lax.dot_general(a, b, (dims, ((), ())), preferred_element_type=jnp.float32)


def room(mebibytes):
    return pltpu.CompilerParams(vmem_limit_bytes=mebibytes << 20)


def estimate(flops, moved):
    return pl.CostEstimate(flops=flops, bytes_accessed=moved, transcendentals=0)


def split_columns(docs, x, width):
    streams, rows, channels = x.shape
    count = channels // width
    steps = 2 if count % 2 == 0 else 1
    part = count // steps
    middle = docs.shape[0] // 2

    def kernel(docs_ref, x_ref, o_ref, apart_ref):
        apart_ref[0] = (docs_ref[middle - 1] != docs_ref[middle]).astype(jnp.int32)
        for n in range(part):
            o_ref[n] = x_ref[:, :, n * width : (n + 1) * width]

    return pl.pallas_call(
        kernel,
        grid=(steps,),
        in_specs=[
            pl.BlockSpec(memory_space=pltpu.SMEM),
            pl.BlockSpec((streams, rows, part * width), lambda i: (0, 0, i)),
        ],
        out_specs=[
            pl.BlockSpec((part, streams, rows, width), lambda i: (i, 0, 0, 0)),
            pl.BlockSpec(memory_space=pltpu.SMEM),
        ],
        out_shape=[
            jax.ShapeDtypeStruct((count, streams, rows, width), x.dtype),
            jax.ShapeDtypeStruct((1,), jnp.int32),
        ],
        compiler_params=room(60),
        cost_estimate=estimate(0, 4 * x.size),
        name="split_columns",
    )(docs, x)


def split_rows(x, members, local):
    tokens, channels = x.shape
    width = channels // members

    def kernel(local_ref, x_ref, *o_refs):
        for step in range(members):
            at = pl.multiple_of((local_ref[0] ^ step) * width, width)
            o_refs[step][...] = x_ref[:, pl.ds(at, width)]

    piece = pl.BlockSpec((tokens, width), lambda i, p: (0, 0))
    return pl.pallas_call(
        kernel,
        grid_spec=pltpu.PrefetchScalarGridSpec(
            num_scalar_prefetch=1,
            grid=(1,),
            in_specs=[pl.BlockSpec((tokens, channels), lambda i, p: (0, 0))],
            out_specs=[piece] * members,
        ),
        out_shape=[jax.ShapeDtypeStruct((tokens, width), x.dtype)] * members,
        compiler_params=room(10),
        cost_estimate=estimate(0, 4 * x.size),
        name="split_rows",
    )(local, x)


def join_columns(x):
    count, streams, rows, width = x.shape
    steps = 2 if count % 2 == 0 else 1
    part = count // steps

    def kernel(x_ref, o_ref):
        for n in range(part):
            o_ref[:, :, n * width : (n + 1) * width] = x_ref[pl.program_id(0) * part + n]

    return pl.pallas_call(
        kernel,
        grid=(steps,),
        in_specs=[pl.BlockSpec(memory_space=pltpu.VMEM)],
        out_specs=pl.BlockSpec((streams, rows, part * width), lambda i: (0, 0, i)),
        out_shape=pltpu.HBM((streams, rows, count * width), x.dtype),
        compiler_params=room(10),
        cost_estimate=estimate(0, 4 * x.size),
        name="join_columns",
    )(x)


def tile_starts(tokens):
    starts, total = [], 0
    for block in range(tokens // BLOCK):
        starts.append(total)
        total += block + 1 - max(0, block - STEPS)
    return starts, total


def row_groups(tokens, size):
    blocks = tokens // BLOCK
    size = size if blocks % size == 0 else 1
    for start in range(0, blocks, size):
        yield range(start, start + size), max(0, start - STEPS)


def widened(value, block, group, first):
    before = (max(0, block - STEPS) - first) * BLOCK
    behind = (group[-1] - block) * BLOCK
    parts = [jnp.zeros((BLOCK, before), value.dtype)] if before else []
    parts.append(value)
    if behind:
        parts.append(jnp.zeros((BLOCK, behind), value.dtype))
    return jnp.concatenate(parts, axis=1) if len(parts) > 1 else value


def stacked(parts):
    return jnp.concatenate(parts, axis=0) if len(parts) > 1 else parts[0]


def forward_kernel(docs, x_ref, taps_ref, before_ref, mixed_ref, prob_ref, out_ref, padded):
    tp, owners, _, streams, rows, wide = x_ref.shape
    chunk = tp * rows
    tokens = owners * chunk
    head = pl.program_id(0)
    lanes = pl.ds(pl.multiple_of(head * HEAD_DIM, HEAD_DIM), HEAD_DIM)
    each = wide // HEAD_DIM
    slab = head // each
    inner = pl.ds(pl.multiple_of(head % each * HEAD_DIM, HEAD_DIM), HEAD_DIM)
    padded[:, 0:PAD, :] = before_ref[:, :, lanes].astype(jnp.float32)
    for m in range(streams):
        for c in range(owners):
            mine = x_ref[:, c, slab, m, :, inner].reshape(chunk, HEAD_DIM)
            padded[m, PAD + c * chunk : PAD + (c + 1) * chunk, :] = mine.astype(jnp.float32)
    for m in range(streams):
        for start in range(0, tokens, BLOCK):
            total = None
            for lag in range(KW):
                at = PAD + start - lag
                term = taps_ref[m, lag : lag + 1, lanes] * padded[m, at : at + BLOCK, :]
                total = term if total is None else total + term
            mixed_ref[0, m, start : start + BLOCK, :] = total.astype(jnp.bfloat16)
    below = lax.broadcasted_iota(jnp.int32, (BLOCK, BLOCK), 0) >= lax.broadcasted_iota(
        jnp.int32, (BLOCK, BLOCK), 1
    )
    starts = tile_starts(tokens)[0]
    for group, first in row_groups(tokens, 2):
        own = slice(group[0] * BLOCK, (group[-1] + 1) * BLOCK)
        span = slice(first * BLOCK, own.stop)
        raw = dot(mixed_ref[0, 0, own, :], mixed_ref[0, 1, span, :], ((1,), (1,)))
        sheets, inverses = [], []
        for block in group:
            lowest = max(0, block - STEPS)
            mine = raw[(block - group[0]) * BLOCK : (block - group[0] + 1) * BLOCK]
            parts = []
            for other in range(lowest, block + 1):
                part = mine[:, (other - first) * BLOCK : (other - first + 1) * BLOCK]
                allowed = below if other == block else docs[other] == docs[block]
                parts.append(jnp.where(allowed, part, -1e30))
            masked = jnp.concatenate(parts, axis=1) if len(parts) > 1 else parts[0]
            expo = jnp.exp2((masked - jnp.max(masked, axis=1, keepdims=True)) * SCALE_LOG2)
            inverses.append(1.0 / jnp.sum(expo, axis=1, keepdims=True))
            sheets.append(widened(expo.astype(jnp.bfloat16), block, group, first))
            prob = expo * inverses[-1]
            for n in range(block + 1 - lowest):
                prob_ref[0, starts[block] + n] = prob[:, n * BLOCK : (n + 1) * BLOCK]
        total = dot(stacked(sheets), mixed_ref[0, 2, span, :], ((1,), (0,)))
        per = out_ref.shape[1]
        for n, block in enumerate(group):
            at = block * BLOCK
            out_ref[at // per, at % per : at % per + BLOCK, :] = (
                total[n * BLOCK : (n + 1) * BLOCK] * inverses[n]
            ).astype(jnp.bfloat16)


def forward(docs, x, taps, before, members):
    tp, _, slabs, streams, rows, wide = x.shape
    width = slabs * wide
    per = width // HEAD_DIM
    tokens = tp * members * rows
    tiles = tile_starts(tokens)[1]
    here = pl.BlockSpec(memory_space=pltpu.VMEM)
    return pl.pallas_call(
        forward_kernel,
        grid_spec=pltpu.PrefetchScalarGridSpec(
            num_scalar_prefetch=1,
            grid=(per,),
            in_specs=[here, here, here],
            out_specs=[
                pl.BlockSpec((1, streams, tokens, HEAD_DIM), lambda h, d: (h, 0, 0, 0)),
                pl.BlockSpec((1, tiles, BLOCK, BLOCK), lambda h, d: (h, 0, 0, 0)),
                pl.BlockSpec((members, tokens // members, HEAD_DIM), lambda h, d: (0, 0, h)),
            ],
            scratch_shapes=[pltpu.VMEM((streams, tokens + PAD, HEAD_DIM), jnp.float32)],
        ),
        out_shape=[
            pltpu.HBM((per, streams, tokens, HEAD_DIM), jnp.bfloat16),
            pltpu.HBM((per, tiles, BLOCK, BLOCK), jnp.float32),
            pltpu.HBM((members, tokens // members, width), jnp.bfloat16),
        ],
        compiler_params=room(FORE),
        cost_estimate=estimate(10_000_000_000, 8 * x.size),
        name="forward",
    )(docs, x, taps, before)


def backward_kernel(
    local, x_ref, before_ref, mixed_ref, prob_ref, att_ref, *refs
):
    *up_refs, cgrad_ref, extra_ref, up_ref, extra = refs
    tp, owners, _, streams, rows, _ = x_ref.shape
    chunk = tp * rows
    tokens = owners * chunk
    per = att_ref.shape[1]
    head = pl.program_id(0)

    @pl.when(head == 0)
    def _():
        for step, piece_ref in enumerate(up_refs):
            up_ref[local[0] ^ step] = piece_ref[...]

    lanes = pl.ds(pl.multiple_of(head * HEAD_DIM, HEAD_DIM), HEAD_DIM)
    cgrad = cgrad_ref.at[head]
    edge = jnp.zeros((streams, PAD, HEAD_DIM), jnp.float32)
    cgrad[:, 0:PAD, :] = edge
    cgrad[:, PAD + tokens :, :] = edge
    starts = tile_starts(tokens)[0]
    for group, first in row_groups(tokens, 4 if tokens == 4 * BLOCK else 2):
        own = slice(group[0] * BLOCK, (group[-1] + 1) * BLOCK)
        span = slice(first * BLOCK, own.stop)
        query, keys = mixed_ref[0, 0, own, :], mixed_ref[0, 1, span, :]
        ups = [
            up_ref[b * BLOCK // per, b * BLOCK % per : b * BLOCK % per + BLOCK, lanes]
            for b in group
        ]
        up = stacked(ups)
        dprob = dot(up, mixed_ref[0, 2, span, :], ((1,), (1,)))
        probs, dscores = [], []
        for n, block in enumerate(group):
            lowest, at = max(0, block - STEPS), block * BLOCK
            att = att_ref[at // per, at % per : at % per + BLOCK, :]
            delta = jnp.sum(
                ups[n].astype(jnp.float32) * att.astype(jnp.float32), axis=1, keepdims=True
            )
            tiles = [prob_ref[0, starts[block] + k] for k in range(block + 1 - lowest)]
            prob = jnp.concatenate(tiles, axis=1) if len(tiles) > 1 else tiles[0]
            mine = dprob[
                n * BLOCK : (n + 1) * BLOCK,
                (lowest - first) * BLOCK : (block + 1 - first) * BLOCK,
            ]
            dscore = (prob * (mine - delta) * SCALE).astype(jnp.bfloat16)
            dscores.append(widened(dscore, block, group, first))
            probs.append(widened(prob.astype(jnp.bfloat16), block, group, first))
        dscore = stacked(dscores)
        out = slice(PAD + own.start, PAD + own.stop)
        outs = slice(PAD + span.start, PAD + own.start)
        cgrad[0, out, :] = dot(dscore, keys, ((1,), (0,)))
        for m, part in (
            (1, dot(dscore, query, ((0,), (0,)))),
            (2, dot(stacked(probs), up, ((0,), (0,)))),
        ):
            if span.start < own.start:
                cgrad[m, outs, :] += part[: own.start - span.start]
            cgrad[m, out, :] = part[own.start - span.start :]
    extra[:, 0:PAD, :] = cgrad[:, PAD : 2 * PAD, :]
    extra[:, PAD + KW :, :] = edge[:, KW:]
    for m in range(streams):
        early = before_ref[m, :, lanes].astype(jnp.float32)
        sums = [early * cgrad[m, lag : lag + PAD, :] for lag in range(KW)]
        for c in range(owners):
            here = x_ref[:, c, 0, m].reshape(chunk, HEAD_DIM).astype(jnp.float32)
            for lag in range(KW):
                at = PAD + c * chunk + lag
                product = here * cgrad[m, at : at + chunk, :]
                sums[lag] = sums[lag] + jnp.sum(product.reshape(chunk // 8, 8, HEAD_DIM), axis=0)
        for lag in range(KW):
            extra[m, PAD + lag : PAD + lag + 1, :] = jnp.sum(sums[lag], axis=0, keepdims=True)
    extra_ref[:, :, lanes] = extra[...].astype(jnp.bfloat16)


def backward(local, x, before, mixed, prob, att, pieces):
    tp, members, slabs, streams, rows, wide = x.shape
    width = slabs * wide
    per, each = width // HEAD_DIM, wide // HEAD_DIM
    tokens = tp * members * rows
    tiles = prob.shape[1]
    here = pl.BlockSpec(memory_space=pltpu.VMEM)
    return pl.pallas_call(
        backward_kernel,
        grid_spec=pltpu.PrefetchScalarGridSpec(
            num_scalar_prefetch=1,
            grid=(per,),
            in_specs=[
                pl.BlockSpec(
                    (tp, members, 1, streams, rows, HEAD_DIM),
                    lambda h, p: (0, 0, h // each, 0, 0, h % each),
                ),
                here,
                pl.BlockSpec((1, streams, tokens, HEAD_DIM), lambda h, p: (h, 0, 0, 0)),
                pl.BlockSpec((1, tiles, BLOCK, BLOCK), lambda h, p: (h, 0, 0, 0)),
                pl.BlockSpec((members, tokens // members, HEAD_DIM), lambda h, p: (0, 0, h)),
            ]
            + [here] * members,
            out_specs=[here, here],
            scratch_shapes=[
                pltpu.VMEM((members, tokens // members, width), jnp.bfloat16),
                pltpu.VMEM((streams, 2 * PAD, HEAD_DIM), jnp.float32),
            ],
        ),
        out_shape=[
            jax.ShapeDtypeStruct((per, streams, tokens + 2 * PAD, HEAD_DIM), jnp.float32),
            jax.ShapeDtypeStruct((streams, 2 * PAD, width), jnp.bfloat16),
        ],
        compiler_params=room(BACK),
        cost_estimate=estimate(20_000_000_000, 12 * x.size),
        name="backward",
    )(local, x, before, mixed, prob, att, *pieces)


def spread_kernel(cgrad_ref, taps_ref, grad_ref, tail_ref):
    tp, owners, _, streams, rows, _ = grad_ref.shape
    chunk = tp * rows
    head = pl.program_id(0)
    lanes = pl.ds(pl.multiple_of(head * HEAD_DIM, HEAD_DIM), HEAD_DIM)
    for m in range(streams):
        for c in range(owners):
            total = None
            for lag in range(KW):
                at = PAD + c * chunk + lag
                term = taps_ref[m, lag : lag + 1, lanes] * cgrad_ref[head, m, at : at + chunk, :]
                total = term if total is None else total + term
            grad_ref[:, c, 0, m] = total.astype(jnp.bfloat16).reshape(tp, rows, HEAD_DIM)
        tail_ref[m, :, lanes] = total[chunk - PAD :]


def spread(cgrad, taps, shape):
    tp, members, slabs, streams, rows, wide = shape
    each = wide // HEAD_DIM
    here = pl.BlockSpec(memory_space=pltpu.VMEM)
    return pl.pallas_call(
        spread_kernel,
        grid=(slabs * each,),
        in_specs=[here, here],
        out_specs=[
            pl.BlockSpec(
                (tp, members, 1, streams, rows, HEAD_DIM),
                lambda h: (0, 0, h // each, 0, 0, h % each),
            ),
            here,
        ],
        out_shape=[
            pltpu.HBM(shape, jnp.bfloat16),
            jax.ShapeDtypeStruct((streams, PAD, slabs * wide), jnp.float32),
        ],
        compiler_params=room(SPREAD),
        cost_estimate=estimate(2_000_000_000, 6 * cgrad.size),
        name="spread",
    )(cgrad, taps)


def swap(value, axes, groups):
    shape = value.shape
    return lax.all_to_all(
        value.reshape(shape[0], -1, shape[-1]),
        axes,
        split_axis=0,
        concat_axis=0,
        axis_index_groups=groups,
        tiled=True,
    ).reshape(shape)


def across(value, step):
    count = lax.axis_size("ctx")
    return lax.ppermute(value, "ctx", [(i, i ^ step) for i in range(count)])


def beside_neighbour(piece):
    other = across(piece, 1)
    even = lax.axis_index("ctx") % 2 == 0
    return jnp.concatenate(
        [jnp.where(even, piece, other), jnp.where(even, other, piece)], axis=-1
    )


def gather_columns(held, span, members):
    position = lax.axis_index("ctx").astype(jnp.int32)
    streams, taps, wide = held.shape
    steps = range(0, members, span)
    pieces = [across(held, step) if step else held for step in steps]

    def kernel(position_ref, *refs):
        o_ref = refs[-1]
        for step in steps:
            column = lax.rem(position_ref[0] ^ step, members) // span
            o_ref[:, :, pl.ds(pl.multiple_of(column * wide, wide), wide)] = refs[step // span][
                ...
            ].astype(jnp.float32)

    columns = members // span * wide
    return pl.pallas_call(
        kernel,
        grid_spec=pltpu.PrefetchScalarGridSpec(
            num_scalar_prefetch=1,
            grid=(1,),
            in_specs=[pl.BlockSpec((streams, taps, wide), lambda i, p: (0, 0, 0))] * len(pieces),
            out_specs=pl.BlockSpec((streams, taps, columns), lambda i, p: (0, 0, 0)),
        ),
        out_shape=jax.ShapeDtypeStruct((streams, taps, columns), jnp.float32),
        compiler_params=room(4),
        name="place_columns",
    )(position.reshape(1), *pieces)


def by_heads(parts, slabs, filters, doc_ids, upstream):
    count, tp = lax.axis_size("ctx"), lax.axis_size("tp")
    members = count // parts
    blocks, streams, rows, wide = slabs.shape
    width = parts * wide
    position = lax.axis_index("ctx")
    groups = [
        [(p * members + c) * tp + t for t in range(tp) for c in range(members)]
        for p in range(parts)
    ]
    every = [[p * members + c for c in range(members)] for p in range(parts)]
    if parts > 1:
        docs = doc_ids.shape[0] // parts
        doc_ids = lax.dynamic_slice_in_dim(doc_ids, position // members * docs, docs)
    shape = (tp, members, parts, streams, rows, wide)
    x = swap(slabs.reshape(tp * members, -1, wide), AXES, groups).reshape(shape)
    local = (position % members).astype(jnp.int32).reshape(1)
    pieces = split_rows(upstream, members, local)
    pieces = [across(piece, step) if step else piece for step, piece in enumerate(pieces)]
    taps = lax.dynamic_slice_in_dim(filters, position % members * width, width, 2)
    if parts > 1:
        upward = [(i, i + members) for i in range(count - members)]
        last = jnp.transpose(x[-1, -1, :, :, rows - PAD :], (1, 2, 0, 3))
        before = lax.ppermute(last.reshape(streams, PAD, width), "ctx", upward)
    else:
        before = jnp.zeros((streams, PAD, width), x.dtype)
    mixed, prob, att = forward(doc_ids, x, taps, before, members)
    attended = join_columns(swap(att, "ctx", every)[:, None])[0]
    away = [pltpu.with_memory_space_constraint(v, pltpu.HBM) for v in (mixed, prob, att)]
    cgrad, extra = backward(local, x, before, *away, pieces)
    if parts > 1:
        other = across(extra, members)
        both = extra.astype(jnp.float32) + other.astype(jnp.float32)
        span, held = 1, both[:, PAD : PAD + KW].astype(jnp.bfloat16)
    else:
        span, held = 2, beside_neighbour(extra[:, PAD : PAD + KW])
    grad, tail = spread(cgrad, taps, shape)
    if parts > 1:
        after = jnp.where(position < members, other[:, 0:PAD].astype(jnp.float32), 0.0)
        after = jnp.concatenate([jnp.zeros_like(after), after], axis=1)
        for lag in range(KW):
            tail = tail + taps[:, lag : lag + 1] * after[:, lag : lag + PAD]
        tail = tail.astype(grad.dtype).reshape(streams, PAD, parts, wide)
        grad = grad.at[-1, -1, :, :, rows - PAD :].set(jnp.transpose(tail, (2, 0, 1, 3)))
    grad, held = lax.optimization_barrier((grad, held))
    held, attended = lax.optimization_barrier((held, attended))
    filter_grad = gather_columns(held, span, members)
    grad = swap(grad.reshape(tp * members, -1, wide), AXES, groups)
    qkv_grad = join_columns(grad.reshape(slabs.shape))
    return attended, jnp.transpose(qkv_grad, (1, 0, 2)), filter_grad


def from_behind(value, axis, steps):
    count = lax.axis_size(axis)
    first, last = (max(0, -steps), min(count, count - steps))
    return lax.ppermute(value, axis, [(source, source + steps) for source in range(first, last)])


def block_docs(doc_ids, first_block, count):
    start = jnp.maximum(first_block, 0)
    picked = lax.dynamic_slice_in_dim(doc_ids, start, count)
    return jnp.repeat(picked, BLOCK)


def by_ring(qkv, filters, doc_ids, upstream):
    local = lax.all_to_all(qkv, "tp", split_axis=2, concat_axis=0, tiled=True)
    tokens = local.shape[0]
    width = local.shape[2]
    heads = width // HEAD_DIM
    blocks_here = tokens // BLOCK
    logit_scale = HEAD_DIM ** (-0.5)
    position = lax.axis_index("ctx")
    reach = STEPS + 1
    rim = from_behind(local[tokens - (KW - 1) :], "ctx", 1)
    inputs = jnp.concatenate([rim, local], axis=0).astype(jnp.float32)
    mixed = sum(
        (filters[:, lag, :] * inputs[KW - 1 - lag : KW - 1 - lag + tokens] for lag in range(KW))
    )
    mixed = mixed.astype(jnp.bfloat16)
    queries = mixed[:, 0].reshape(tokens, heads, HEAD_DIM)
    key_value = mixed[:, 1:3]
    tiles = [key_value]
    current = key_value
    for distance in range(1, STEPS + 1):
        current = from_behind(current, "ctx", 1)
        tiles.append(current)
    joined = jnp.concatenate(tiles, axis=0)
    keys = joined[:, 0].reshape(reach * tokens, heads, HEAD_DIM)
    values = joined[:, 1].reshape(reach * tokens, heads, HEAD_DIM)
    rows = jnp.arange(tokens)
    query_token = position * tokens + rows
    query_doc = block_docs(doc_ids, position * blocks_here, blocks_here)
    key_tokens = jnp.concatenate(
        [(position - distance) * tokens + rows for distance in range(reach)]
    )
    key_docs = jnp.concatenate(
        [
            block_docs(doc_ids, (position - distance) * blocks_here, blocks_here)
            for distance in range(reach)
        ]
    )
    allowed = (
        (key_tokens[None, :] >= 0)
        & (key_tokens[None, :] <= query_token[:, None])
        & (key_docs[None, :] == query_doc[:, None])
    )
    raw = (
        jnp.einsum("qhd,khd->hqk", queries, keys, preferred_element_type=jnp.float32) * logit_scale
    )
    masked = jnp.where(allowed[None], raw, -1e30)
    row_max = masked.max(axis=2)
    expo = jnp.where(allowed[None], jnp.exp(masked - row_max[:, :, None]), 0.0)
    row_sum = expo.sum(axis=2)
    weighted_values = jnp.einsum(
        "hqk,khd->qhd", expo.astype(jnp.bfloat16), values, preferred_element_type=jnp.float32
    )
    attended = (weighted_values / row_sum.T[:, :, None]).astype(jnp.bfloat16)
    grad_out = upstream.reshape(tokens, heads, HEAD_DIM)
    delta = jnp.sum(grad_out.astype(jnp.float32) * attended.astype(jnp.float32), axis=-1).T
    prob = expo / row_sum[:, :, None]
    value_part = jnp.einsum(
        "hqk,qhd->khd", prob.astype(jnp.bfloat16), grad_out, preferred_element_type=jnp.float32
    )
    probability_gradient = jnp.einsum(
        "qhd,khd->hqk", grad_out, values, preferred_element_type=jnp.float32
    )
    score_gradient = (prob * (probability_gradient - delta[:, :, None]) * logit_scale).astype(
        jnp.bfloat16
    )
    query_gradient_rows = jnp.einsum(
        "hqk,khd->qhd", score_gradient, keys, preferred_element_type=jnp.float32
    )
    key_part = jnp.einsum(
        "hqk,qhd->khd", score_gradient, queries, preferred_element_type=jnp.float32
    )
    stacked = jnp.stack(
        [key_part.reshape(reach, tokens, width), value_part.reshape(reach, tokens, width)], axis=2
    )
    partials = [stacked[distance] for distance in range(reach)]
    carried = partials[STEPS]
    for distance in range(STEPS - 1, -1, -1):
        carried = from_behind(carried, "ctx", -1)
        carried = carried + partials[distance]
    conv_grad = jnp.concatenate([query_gradient_rows.reshape(tokens, 1, width), carried], axis=1)
    grad_edge = from_behind(conv_grad[: KW - 1], "ctx", -1)
    extended = jnp.concatenate([conv_grad, grad_edge], axis=0)
    input_grad = sum((filters[:, lag, :] * extended[lag : lag + tokens] for lag in range(KW)))
    tap_terms = jnp.stack(
        [
            jnp.sum(inputs[KW - 1 - lag : KW - 1 - lag + tokens] * conv_grad, axis=0)
            for lag in range(KW)
        ],
        axis=1,
    )
    filter_grad = lax.psum(tap_terms, "ctx")
    qkv_grad = lax.all_to_all(
        input_grad.astype(jnp.bfloat16), "tp", split_axis=0, concat_axis=2, tiled=True
    )
    return (attended.reshape(tokens, width), qkv_grad, filter_grad)


def solution(mesh):
    count = mesh.shape["ctx"]

    def shards(qkv, filters, doc_ids, upstream):
        tokens, width = upstream.shape
        heads = width // HEAD_DIM
        even = tokens % BLOCK == 0 and qkv.shape[0] % PAD == 0 and count & (count - 1) == 0
        if heads % count or not even or count < 4:
            return by_ring(qkv, filters, doc_ids, upstream)
        slabs, apart = split_columns(doc_ids, jnp.transpose(qkv, (1, 0, 2)), width // count)
        forms = [functools.partial(by_heads, parts) for parts in (1, 2)]
        return lax.switch(apart[0], forms, slabs, filters, doc_ids, upstream)

    return jax.shard_map(
        shards,
        mesh=mesh,
        in_specs=(P(("ctx", "tp"), None, None), P(None, None, "tp"), P(), P("ctx", "tp")),
        out_specs=(P("ctx", "tp"), P(("ctx", "tp"), None, None), P(None, None, "tp")),
        check_vma=False,
    )
```

```python
import functools
import math

import jax
import jax.numpy as jnp
from jax import lax
from jax.experimental import pallas as pl
from jax.experimental.pallas import tpu as pltpu
from jax.sharding import PartitionSpec as P

HEAD_DIM = 128
KW = 7
BLOCK = 128
STEPS = 4
PAD = 8
SCALE = HEAD_DIM ** (-0.5)
SCALE_LOG2 = SCALE * math.log2(math.e)
AXES = ("ctx", "tp")
FORE, BACK, SPREAD = 24, 24, 16


def dot(a, b, dims):
    return lax.dot_general(a, b, (dims, ((), ())), preferred_element_type=jnp.float32)


def room(mebibytes):
    return pltpu.CompilerParams(vmem_limit_bytes=mebibytes << 20)


def estimate(flops, moved):
    return pl.CostEstimate(flops=flops, bytes_accessed=moved, transcendentals=0)


def split_columns(docs, x, width):
    streams, rows, channels = x.shape
    count = channels // width
    steps = 2 if count % 2 == 0 else 1
    part = count // steps
    middle = docs.shape[0] // 2

    def kernel(docs_ref, x_ref, o_ref, apart_ref):
        apart_ref[0] = (docs_ref[middle - 1] != docs_ref[middle]).astype(jnp.int32)
        for n in range(part):
            o_ref[n] = x_ref[:, :, n * width : (n + 1) * width]

    return pl.pallas_call(
        kernel,
        grid=(steps,),
        in_specs=[
            pl.BlockSpec(memory_space=pltpu.SMEM),
            pl.BlockSpec((streams, rows, part * width), lambda i: (0, 0, i)),
        ],
        out_specs=[
            pl.BlockSpec((part, streams, rows, width), lambda i: (i, 0, 0, 0)),
            pl.BlockSpec(memory_space=pltpu.SMEM),
        ],
        out_shape=[
            jax.ShapeDtypeStruct((count, streams, rows, width), x.dtype),
            jax.ShapeDtypeStruct((1,), jnp.int32),
        ],
        compiler_params=room(60),
        cost_estimate=estimate(0, 4 * x.size),
        name="split_columns",
    )(docs, x)


def split_rows(x, members, local):
    tokens, channels = x.shape
    width = channels // members

    def kernel(local_ref, x_ref, *o_refs):
        for step in range(members):
            at = pl.multiple_of((local_ref[0] ^ step) * width, width)
            o_refs[step][...] = x_ref[:, pl.ds(at, width)]

    piece = pl.BlockSpec((tokens, width), lambda i, p: (0, 0))
    return pl.pallas_call(
        kernel,
        grid_spec=pltpu.PrefetchScalarGridSpec(
            num_scalar_prefetch=1,
            grid=(1,),
            in_specs=[pl.BlockSpec((tokens, channels), lambda i, p: (0, 0))],
            out_specs=[piece] * members,
        ),
        out_shape=[jax.ShapeDtypeStruct((tokens, width), x.dtype)] * members,
        compiler_params=room(10),
        cost_estimate=estimate(0, 4 * x.size),
        name="split_rows",
    )(local, x)


def join_columns(x):
    count, streams, rows, width = x.shape
    steps = 2 if count % 2 == 0 else 1
    part = count // steps

    def kernel(x_ref, o_ref):
        for n in range(part):
            o_ref[:, :, n * width : (n + 1) * width] = x_ref[pl.program_id(0) * part + n]

    return pl.pallas_call(
        kernel,
        grid=(steps,),
        in_specs=[pl.BlockSpec(memory_space=pltpu.VMEM)],
        out_specs=pl.BlockSpec((streams, rows, part * width), lambda i: (0, 0, i)),
        out_shape=pltpu.HBM((streams, rows, count * width), x.dtype),
        compiler_params=room(10),
        cost_estimate=estimate(0, 4 * x.size),
        name="join_columns",
    )(x)


def tile_starts(tokens):
    starts, total = [], 0
    for block in range(tokens // BLOCK):
        starts.append(total)
        total += block + 1 - max(0, block - STEPS)
    return starts, total


def row_groups(tokens, size):
    blocks = tokens // BLOCK
    size = size if blocks % size == 0 else 1
    for start in range(0, blocks, size):
        yield range(start, start + size), max(0, start - STEPS)


def widened(value, block, group, first):
    before = (max(0, block - STEPS) - first) * BLOCK
    behind = (group[-1] - block) * BLOCK
    parts = [jnp.zeros((BLOCK, before), value.dtype)] if before else []
    parts.append(value)
    if behind:
        parts.append(jnp.zeros((BLOCK, behind), value.dtype))
    return jnp.concatenate(parts, axis=1) if len(parts) > 1 else value


def stacked(parts):
    return jnp.concatenate(parts, axis=0) if len(parts) > 1 else parts[0]


def forward_kernel(docs, x_ref, taps_ref, before_ref, mixed_ref, prob_ref, out_ref, padded):
    tp, owners, _, streams, rows, wide = x_ref.shape
    chunk = tp * rows
    tokens = owners * chunk
    head = pl.program_id(0)
    lanes = pl.ds(pl.multiple_of(head * HEAD_DIM, HEAD_DIM), HEAD_DIM)
    each = wide // HEAD_DIM
    slab = head // each
    inner = pl.ds(pl.multiple_of(head % each * HEAD_DIM, HEAD_DIM), HEAD_DIM)
    padded[:, 0:PAD, :] = before_ref[:, :, lanes].astype(jnp.float32)
    for m in range(streams):
        for c in range(owners):
            mine = x_ref[:, c, slab, m, :, inner].reshape(chunk, HEAD_DIM)
            padded[m, PAD + c * chunk : PAD + (c + 1) * chunk, :] = mine.astype(jnp.float32)
    for m in range(streams):
        for start in range(0, tokens, BLOCK):
            total = None
            for lag in range(KW):
                at = PAD + start - lag
                term = taps_ref[m, lag : lag + 1, lanes] * padded[m, at : at + BLOCK, :]
                total = term if total is None else total + term
            mixed_ref[0, m, start : start + BLOCK, :] = total.astype(jnp.bfloat16)
    below = lax.broadcasted_iota(jnp.int32, (BLOCK, BLOCK), 0) >= lax.broadcasted_iota(
        jnp.int32, (BLOCK, BLOCK), 1
    )
    starts = tile_starts(tokens)[0]
    for group, first in row_groups(tokens, 2):
        own = slice(group[0] * BLOCK, (group[-1] + 1) * BLOCK)
        span = slice(first * BLOCK, own.stop)
        raw = dot(mixed_ref[0, 0, own, :], mixed_ref[0, 1, span, :], ((1,), (1,)))
        sheets, inverses = [], []
        for block in group:
            lowest = max(0, block - STEPS)
            mine = raw[(block - group[0]) * BLOCK : (block - group[0] + 1) * BLOCK]
            parts = []
            for other in range(lowest, block + 1):
                part = mine[:, (other - first) * BLOCK : (other - first + 1) * BLOCK]
                allowed = below if other == block else docs[other] == docs[block]
                parts.append(jnp.where(allowed, part, -1e30))
            masked = jnp.concatenate(parts, axis=1) if len(parts) > 1 else parts[0]
            expo = jnp.exp2((masked - jnp.max(masked, axis=1, keepdims=True)) * SCALE_LOG2)
            inverses.append(1.0 / jnp.sum(expo, axis=1, keepdims=True))
            sheets.append(widened(expo.astype(jnp.bfloat16), block, group, first))
            prob = (expo * inverses[-1]).astype(jnp.bfloat16)
            for n in range(block + 1 - lowest):
                prob_ref[0, starts[block] + n] = prob[:, n * BLOCK : (n + 1) * BLOCK]
        total = dot(stacked(sheets), mixed_ref[0, 2, span, :], ((1,), (0,)))
        per = out_ref.shape[1]
        for n, block in enumerate(group):
            at = block * BLOCK
            out_ref[at // per, at % per : at % per + BLOCK, :] = (
                total[n * BLOCK : (n + 1) * BLOCK] * inverses[n]
            ).astype(jnp.bfloat16)


def forward(docs, x, taps, before, members):
    tp, _, slabs, streams, rows, wide = x.shape
    width = slabs * wide
    per = width // HEAD_DIM
    tokens = tp * members * rows
    tiles = tile_starts(tokens)[1]
    here = pl.BlockSpec(memory_space=pltpu.VMEM)
    return pl.pallas_call(
        forward_kernel,
        grid_spec=pltpu.PrefetchScalarGridSpec(
            num_scalar_prefetch=1,
            grid=(per,),
            in_specs=[here, here, here],
            out_specs=[
                pl.BlockSpec((1, streams, tokens, HEAD_DIM), lambda h, d: (h, 0, 0, 0)),
                pl.BlockSpec((1, tiles, BLOCK, BLOCK), lambda h, d: (h, 0, 0, 0)),
                pl.BlockSpec((members, tokens // members, HEAD_DIM), lambda h, d: (0, 0, h)),
            ],
            scratch_shapes=[pltpu.VMEM((streams, tokens + PAD, HEAD_DIM), jnp.float32)],
        ),
        out_shape=[
            pltpu.HBM((per, streams, tokens, HEAD_DIM), jnp.bfloat16),
            pltpu.HBM((per, tiles, BLOCK, BLOCK), jnp.bfloat16),
            pltpu.HBM((members, tokens // members, width), jnp.bfloat16),
        ],
        compiler_params=room(FORE),
        cost_estimate=estimate(10_000_000_000, 8 * x.size),
        name="forward",
    )(docs, x, taps, before)


def backward_kernel(
    local, x_ref, before_ref, mixed_ref, prob_ref, att_ref, *refs
):
    *up_refs, cgrad_ref, extra_ref, up_ref, extra = refs
    tp, owners, _, streams, rows, _ = x_ref.shape
    chunk = tp * rows
    tokens = owners * chunk
    per = att_ref.shape[1]
    head = pl.program_id(0)

    @pl.when(head == 0)
    def _():
        for step, piece_ref in enumerate(up_refs):
            up_ref[local[0] ^ step] = piece_ref[...]

    lanes = pl.ds(pl.multiple_of(head * HEAD_DIM, HEAD_DIM), HEAD_DIM)
    cgrad = cgrad_ref.at[head]
    edge = jnp.zeros((streams, PAD, HEAD_DIM), jnp.float32)
    cgrad[:, 0:PAD, :] = edge
    cgrad[:, PAD + tokens :, :] = edge
    starts = tile_starts(tokens)[0]
    for group, first in row_groups(tokens, 4 if tokens == 4 * BLOCK else 2):
        own = slice(group[0] * BLOCK, (group[-1] + 1) * BLOCK)
        span = slice(first * BLOCK, own.stop)
        query, keys = mixed_ref[0, 0, own, :], mixed_ref[0, 1, span, :]
        ups = [
            up_ref[b * BLOCK // per, b * BLOCK % per : b * BLOCK % per + BLOCK, lanes]
            for b in group
        ]
        up = stacked(ups)
        dprob = dot(up, mixed_ref[0, 2, span, :], ((1,), (1,)))
        probs, dscores = [], []
        for n, block in enumerate(group):
            lowest, at = max(0, block - STEPS), block * BLOCK
            att = att_ref[at // per, at % per : at % per + BLOCK, :]
            delta = jnp.sum(
                ups[n].astype(jnp.float32) * att.astype(jnp.float32), axis=1, keepdims=True
            )
            tiles = [prob_ref[0, starts[block] + k] for k in range(block + 1 - lowest)]
            prob = jnp.concatenate(tiles, axis=1) if len(tiles) > 1 else tiles[0]
            mine = dprob[
                n * BLOCK : (n + 1) * BLOCK,
                (lowest - first) * BLOCK : (block + 1 - first) * BLOCK,
            ]
            dscore = (prob.astype(jnp.float32) * (mine - delta) * SCALE).astype(jnp.bfloat16)
            dscores.append(widened(dscore, block, group, first))
            probs.append(widened(prob, block, group, first))
        dscore = stacked(dscores)
        out = slice(PAD + own.start, PAD + own.stop)
        outs = slice(PAD + span.start, PAD + own.start)
        cgrad[0, out, :] = dot(dscore, keys, ((1,), (0,)))
        for m, part in (
            (1, dot(dscore, query, ((0,), (0,)))),
            (2, dot(stacked(probs), up, ((0,), (0,)))),
        ):
            if span.start < own.start:
                cgrad[m, outs, :] += part[: own.start - span.start]
            cgrad[m, out, :] = part[own.start - span.start :]
    extra[:, 0:PAD, :] = cgrad[:, PAD : 2 * PAD, :]
    extra[:, PAD + KW :, :] = edge[:, KW:]
    for m in range(streams):
        early = before_ref[m, :, lanes].astype(jnp.float32)
        sums = [early * cgrad[m, lag : lag + PAD, :] for lag in range(KW)]
        for c in range(owners):
            here = x_ref[:, c, 0, m].reshape(chunk, HEAD_DIM).astype(jnp.float32)
            for lag in range(KW):
                at = PAD + c * chunk + lag
                product = here * cgrad[m, at : at + chunk, :]
                sums[lag] = sums[lag] + jnp.sum(product.reshape(chunk // 8, 8, HEAD_DIM), axis=0)
        for lag in range(KW):
            extra[m, PAD + lag : PAD + lag + 1, :] = jnp.sum(sums[lag], axis=0, keepdims=True)
    extra_ref[:, :, lanes] = extra[...].astype(jnp.bfloat16)


def backward(local, x, before, mixed, prob, att, pieces):
    tp, members, slabs, streams, rows, wide = x.shape
    width = slabs * wide
    per, each = width // HEAD_DIM, wide // HEAD_DIM
    tokens = tp * members * rows
    tiles = prob.shape[1]
    here = pl.BlockSpec(memory_space=pltpu.VMEM)
    return pl.pallas_call(
        backward_kernel,
        grid_spec=pltpu.PrefetchScalarGridSpec(
            num_scalar_prefetch=1,
            grid=(per,),
            in_specs=[
                pl.BlockSpec(
                    (tp, members, 1, streams, rows, HEAD_DIM),
                    lambda h, p: (0, 0, h // each, 0, 0, h % each),
                ),
                here,
                pl.BlockSpec((1, streams, tokens, HEAD_DIM), lambda h, p: (h, 0, 0, 0)),
                pl.BlockSpec((1, tiles, BLOCK, BLOCK), lambda h, p: (h, 0, 0, 0)),
                pl.BlockSpec((members, tokens // members, HEAD_DIM), lambda h, p: (0, 0, h)),
            ]
            + [here] * members,
            out_specs=[here, here],
            scratch_shapes=[
                pltpu.VMEM((members, tokens // members, width), jnp.bfloat16),
                pltpu.VMEM((streams, 2 * PAD, HEAD_DIM), jnp.float32),
            ],
        ),
        out_shape=[
            jax.ShapeDtypeStruct((per, streams, tokens + 2 * PAD, HEAD_DIM), jnp.float32),
            jax.ShapeDtypeStruct((streams, 2 * PAD, width), jnp.bfloat16),
        ],
        compiler_params=room(BACK),
        cost_estimate=estimate(20_000_000_000, 12 * x.size),
        name="backward",
    )(local, x, before, mixed, prob, att, *pieces)


def spread_kernel(cgrad_ref, taps_ref, grad_ref, tail_ref):
    tp, owners, _, streams, rows, _ = grad_ref.shape
    chunk = tp * rows
    head = pl.program_id(0)
    lanes = pl.ds(pl.multiple_of(head * HEAD_DIM, HEAD_DIM), HEAD_DIM)
    for m in range(streams):
        for c in range(owners):
            total = None
            for lag in range(KW):
                at = PAD + c * chunk + lag
                term = taps_ref[m, lag : lag + 1, lanes] * cgrad_ref[head, m, at : at + chunk, :]
                total = term if total is None else total + term
            grad_ref[:, c, 0, m] = total.astype(jnp.bfloat16).reshape(tp, rows, HEAD_DIM)
        tail_ref[m, :, lanes] = total[chunk - PAD :]


def spread(cgrad, taps, shape):
    tp, members, slabs, streams, rows, wide = shape
    each = wide // HEAD_DIM
    here = pl.BlockSpec(memory_space=pltpu.VMEM)
    return pl.pallas_call(
        spread_kernel,
        grid=(slabs * each,),
        in_specs=[here, here],
        out_specs=[
            pl.BlockSpec(
                (tp, members, 1, streams, rows, HEAD_DIM),
                lambda h: (0, 0, h // each, 0, 0, h % each),
            ),
            here,
        ],
        out_shape=[
            pltpu.HBM(shape, jnp.bfloat16),
            jax.ShapeDtypeStruct((streams, PAD, slabs * wide), jnp.float32),
        ],
        compiler_params=room(SPREAD),
        cost_estimate=estimate(2_000_000_000, 6 * cgrad.size),
        name="spread",
    )(cgrad, taps)


def swap(value, axes, groups):
    shape = value.shape
    return lax.all_to_all(
        value.reshape(shape[0], -1, shape[-1]),
        axes,
        split_axis=0,
        concat_axis=0,
        axis_index_groups=groups,
        tiled=True,
    ).reshape(shape)


def across(value, step):
    count = lax.axis_size("ctx")
    return lax.ppermute(value, "ctx", [(i, i ^ step) for i in range(count)])


def beside_neighbour(piece):
    other = across(piece, 1)
    even = lax.axis_index("ctx") % 2 == 0
    return jnp.concatenate(
        [jnp.where(even, piece, other), jnp.where(even, other, piece)], axis=-1
    )


def gather_columns(held, span, members):
    position = lax.axis_index("ctx").astype(jnp.int32)
    streams, taps, wide = held.shape
    steps = range(0, members, span)
    pieces = [across(held, step) if step else held for step in steps]

    def kernel(position_ref, *refs):
        o_ref = refs[-1]
        for step in steps:
            column = lax.rem(position_ref[0] ^ step, members) // span
            o_ref[:, :, pl.ds(pl.multiple_of(column * wide, wide), wide)] = refs[step // span][
                ...
            ].astype(jnp.float32)

    columns = members // span * wide
    return pl.pallas_call(
        kernel,
        grid_spec=pltpu.PrefetchScalarGridSpec(
            num_scalar_prefetch=1,
            grid=(1,),
            in_specs=[pl.BlockSpec((streams, taps, wide), lambda i, p: (0, 0, 0))] * len(pieces),
            out_specs=pl.BlockSpec((streams, taps, columns), lambda i, p: (0, 0, 0)),
        ),
        out_shape=jax.ShapeDtypeStruct((streams, taps, columns), jnp.float32),
        compiler_params=room(4),
        name="place_columns",
    )(position.reshape(1), *pieces)


def by_heads(parts, slabs, filters, doc_ids, upstream):
    count, tp = lax.axis_size("ctx"), lax.axis_size("tp")
    members = count // parts
    blocks, streams, rows, wide = slabs.shape
    width = parts * wide
    position = lax.axis_index("ctx")
    groups = [
        [(p * members + c) * tp + t for t in range(tp) for c in range(members)]
        for p in range(parts)
    ]
    every = [[p * members + c for c in range(members)] for p in range(parts)]
    if parts > 1:
        docs = doc_ids.shape[0] // parts
        doc_ids = lax.dynamic_slice_in_dim(doc_ids, position // members * docs, docs)
    shape = (tp, members, parts, streams, rows, wide)
    x = swap(slabs.reshape(tp * members, -1, wide), AXES, groups).reshape(shape)
    local = (position % members).astype(jnp.int32).reshape(1)
    pieces = split_rows(upstream, members, local)
    pieces = [across(piece, step) if step else piece for step, piece in enumerate(pieces)]
    taps = lax.dynamic_slice_in_dim(filters, position % members * width, width, 2)
    if parts > 1:
        upward = [(i, i + members) for i in range(count - members)]
        last = jnp.transpose(x[-1, -1, :, :, rows - PAD :], (1, 2, 0, 3))
        before = lax.ppermute(last.reshape(streams, PAD, width), "ctx", upward)
    else:
        before = jnp.zeros((streams, PAD, width), x.dtype)
    mixed, prob, att = forward(doc_ids, x, taps, before, members)
    attended = join_columns(swap(att, "ctx", every)[:, None])[0]
    away = [pltpu.with_memory_space_constraint(v, pltpu.HBM) for v in (mixed, prob, att)]
    cgrad, extra = backward(local, x, before, *away, pieces)
    if parts > 1:
        other = across(extra, members)
        both = extra.astype(jnp.float32) + other.astype(jnp.float32)
        span, held = 1, both[:, PAD : PAD + KW].astype(jnp.bfloat16)
    else:
        span, held = 2, beside_neighbour(extra[:, PAD : PAD + KW])
    grad, tail = spread(cgrad, taps, shape)
    if parts > 1:
        after = jnp.where(position < members, other[:, 0:PAD].astype(jnp.float32), 0.0)
        after = jnp.concatenate([jnp.zeros_like(after), after], axis=1)
        for lag in range(KW):
            tail = tail + taps[:, lag : lag + 1] * after[:, lag : lag + PAD]
        tail = tail.astype(grad.dtype).reshape(streams, PAD, parts, wide)
        grad = grad.at[-1, -1, :, :, rows - PAD :].set(jnp.transpose(tail, (2, 0, 1, 3)))
    grad, held = lax.optimization_barrier((grad, held))
    held, attended = lax.optimization_barrier((held, attended))
    filter_grad = gather_columns(held, span, members)
    grad = swap(grad.reshape(tp * members, -1, wide), AXES, groups)
    qkv_grad = join_columns(grad.reshape(slabs.shape))
    return attended, jnp.transpose(qkv_grad, (1, 0, 2)), filter_grad


def from_behind(value, axis, steps):
    count = lax.axis_size(axis)
    first, last = (max(0, -steps), min(count, count - steps))
    return lax.ppermute(value, axis, [(source, source + steps) for source in range(first, last)])


def block_docs(doc_ids, first_block, count):
    start = jnp.maximum(first_block, 0)
    picked = lax.dynamic_slice_in_dim(doc_ids, start, count)
    return jnp.repeat(picked, BLOCK)


def by_ring(qkv, filters, doc_ids, upstream):
    local = lax.all_to_all(qkv, "tp", split_axis=2, concat_axis=0, tiled=True)
    tokens = local.shape[0]
    width = local.shape[2]
    heads = width // HEAD_DIM
    blocks_here = tokens // BLOCK
    logit_scale = HEAD_DIM ** (-0.5)
    position = lax.axis_index("ctx")
    reach = STEPS + 1
    rim = from_behind(local[tokens - (KW - 1) :], "ctx", 1)
    inputs = jnp.concatenate([rim, local], axis=0).astype(jnp.float32)
    mixed = sum(
        (filters[:, lag, :] * inputs[KW - 1 - lag : KW - 1 - lag + tokens] for lag in range(KW))
    )
    mixed = mixed.astype(jnp.bfloat16)
    queries = mixed[:, 0].reshape(tokens, heads, HEAD_DIM)
    key_value = mixed[:, 1:3]
    tiles = [key_value]
    current = key_value
    for distance in range(1, STEPS + 1):
        current = from_behind(current, "ctx", 1)
        tiles.append(current)
    joined = jnp.concatenate(tiles, axis=0)
    keys = joined[:, 0].reshape(reach * tokens, heads, HEAD_DIM)
    values = joined[:, 1].reshape(reach * tokens, heads, HEAD_DIM)
    rows = jnp.arange(tokens)
    query_token = position * tokens + rows
    query_doc = block_docs(doc_ids, position * blocks_here, blocks_here)
    key_tokens = jnp.concatenate(
        [(position - distance) * tokens + rows for distance in range(reach)]
    )
    key_docs = jnp.concatenate(
        [
            block_docs(doc_ids, (position - distance) * blocks_here, blocks_here)
            for distance in range(reach)
        ]
    )
    allowed = (
        (key_tokens[None, :] >= 0)
        & (key_tokens[None, :] <= query_token[:, None])
        & (key_docs[None, :] == query_doc[:, None])
    )
    raw = (
        jnp.einsum("qhd,khd->hqk", queries, keys, preferred_element_type=jnp.float32) * logit_scale
    )
    masked = jnp.where(allowed[None], raw, -1e30)
    row_max = masked.max(axis=2)
    expo = jnp.where(allowed[None], jnp.exp(masked - row_max[:, :, None]), 0.0)
    row_sum = expo.sum(axis=2)
    weighted_values = jnp.einsum(
        "hqk,khd->qhd", expo.astype(jnp.bfloat16), values, preferred_element_type=jnp.float32
    )
    attended = (weighted_values / row_sum.T[:, :, None]).astype(jnp.bfloat16)
    grad_out = upstream.reshape(tokens, heads, HEAD_DIM)
    delta = jnp.sum(grad_out.astype(jnp.float32) * attended.astype(jnp.float32), axis=-1).T
    prob = expo / row_sum[:, :, None]
    value_part = jnp.einsum(
        "hqk,qhd->khd", prob.astype(jnp.bfloat16), grad_out, preferred_element_type=jnp.float32
    )
    probability_gradient = jnp.einsum(
        "qhd,khd->hqk", grad_out, values, preferred_element_type=jnp.float32
    )
    score_gradient = (prob * (probability_gradient - delta[:, :, None]) * logit_scale).astype(
        jnp.bfloat16
    )
    query_gradient_rows = jnp.einsum(
        "hqk,khd->qhd", score_gradient, keys, preferred_element_type=jnp.float32
    )
    key_part = jnp.einsum(
        "hqk,qhd->khd", score_gradient, queries, preferred_element_type=jnp.float32
    )
    stacked = jnp.stack(
        [key_part.reshape(reach, tokens, width), value_part.reshape(reach, tokens, width)], axis=2
    )
    partials = [stacked[distance] for distance in range(reach)]
    carried = partials[STEPS]
    for distance in range(STEPS - 1, -1, -1):
        carried = from_behind(carried, "ctx", -1)
        carried = carried + partials[distance]
    conv_grad = jnp.concatenate([query_gradient_rows.reshape(tokens, 1, width), carried], axis=1)
    grad_edge = from_behind(conv_grad[: KW - 1], "ctx", -1)
    extended = jnp.concatenate([conv_grad, grad_edge], axis=0)
    input_grad = sum((filters[:, lag, :] * extended[lag : lag + tokens] for lag in range(KW)))
    tap_terms = jnp.stack(
        [
            jnp.sum(inputs[KW - 1 - lag : KW - 1 - lag + tokens] * conv_grad, axis=0)
            for lag in range(KW)
        ],
        axis=1,
    )
    filter_grad = lax.psum(tap_terms, "ctx")
    qkv_grad = lax.all_to_all(
        input_grad.astype(jnp.bfloat16), "tp", split_axis=0, concat_axis=2, tiled=True
    )
    return (attended.reshape(tokens, width), qkv_grad, filter_grad)


def solution(mesh):
    count = mesh.shape["ctx"]

    def shards(qkv, filters, doc_ids, upstream):
        tokens, width = upstream.shape
        heads = width // HEAD_DIM
        even = tokens % BLOCK == 0 and qkv.shape[0] % PAD == 0 and count & (count - 1) == 0
        if heads % count or not even or count < 4:
            return by_ring(qkv, filters, doc_ids, upstream)
        slabs, apart = split_columns(doc_ids, jnp.transpose(qkv, (1, 0, 2)), width // count)
        forms = [functools.partial(by_heads, parts) for parts in (1, 2)]
        return lax.switch(apart[0], forms, slabs, filters, doc_ids, upstream)

    return jax.shard_map(
        shards,
        mesh=mesh,
        in_specs=(P(("ctx", "tp"), None, None), P(None, None, "tp"), P(), P("ctx", "tp")),
        out_specs=(P("ctx", "tp"), P(("ctx", "tp"), None, None), P(None, None, "tp")),
        check_vma=False,
    )
```
